32 devices in a mesh: dp: 4 (over y, x), row: 4 (over z), col: 2 (over core).
Axes of the slice: x: 2, y: 2, z: 4, core: 2. Of those that a mesh axis runs over, the one named last changes fastest.
Arguments:
- hidden: bfloat16 [4096, 2048], P(('dp', 'row'), 'col'), may hold values from -6 to 6
- norm_before: float32 [2048], P('col'), may hold values from 0.1 to 1.9
- query_weight: bfloat16 [2048, 2048], P('col', 'row'), may hold values from -0.125 to 0.125
- key_matrix: bfloat16 [2048, 1024], P('col', 'row'), may hold values from -0.125 to 0.125
- value_matrix: bfloat16 [2048, 1024], P('col', 'row'), may hold values from -0.125 to 0.125
- query_gain: float32 [128], replicated, may hold values from 0.5 to 2
- key_gain: float32 [128], replicated, may hold values from 0.5 to 2
- output_weight: bfloat16 [2048, 2048], P('row', 'col'), may hold values from -1 to 1
- norm_after: float32 [2048], P('col'), may hold values from 0.1 to 1.9
- gate_weight: bfloat16 [2048, 6144], P('col', 'row'), may hold values from -0.125 to 0.125
- up_weight: bfloat16 [2048, 6144], P('col', 'row'), may hold values from -0.125 to 0.125
- down_weight: bfloat16 [6144, 2048], P('row', 'col'), may hold values from -0.078125 to 0.078125
- cotangent: bfloat16 [4096, 2048], P(('dp', 'row'), 'col'), may hold values from -6 to 6
Outputs:
- layer_out: bfloat16 [4096, 2048], P(('dp', 'row'), 'col')
- hidden_grad: float32 [4096, 2048], P(('dp', 'row'), 'col')
- before_grad: float32 [2048], P('col')
- query_grad: float32 [2048, 2048], P('col', 'row')
- key_grad: float32 [2048, 1024], P('col', 'row')
- value_grad: float32 [2048, 1024], P('col', 'row')
- gain_query: float32 [128], replicated
- gain_key: float32 [128], replicated
- output_grad: float32 [2048, 2048], P('row', 'col')
- after_grad: float32 [2048], P('col')
- gate_grad: float32 [2048, 6144], P('col', 'row')
- up_grad: float32 [2048, 6144], P('col', 'row')
- down_grad: float32 [6144, 2048], P('row', 'col')
The draws below stay inside these ranges and needn't reach their ends.
All inputs are finite; a program needn't handle non-finite values.
Results may differ from the reference program's by a relative error of at most 0.017.
Values may be sent and summed in bfloat16 or wider, within the bound.
No kernel may reach another device: no remote copies, remote signals or barrier semaphores. Data moves between devices by JAX's collectives and lax.ppermute only.
A program may use at most 192 MiB of HBM per device.

```python
import math
import jax
import jax.numpy as jnp
from jax import lax

MODEL_WIDTH = 2048
QUERY_HEADS = 16
KEY_VALUE_HEADS = 8
HEAD_SIZE = 128
FF = 6144
SEQUENCE_LENGTH = 1024
SEQUENCE_COUNT = 4
TOKENS = 4096


def gain_values(key):
    return jax.random.uniform(key, (HEAD_SIZE,), jnp.float32, 0.5, 2.0)


def draw_query_gain(key, part):
    return gain_values(jax.random.fold_in(key, 11))


def draw_key_gain(key, part):
    return gain_values(jax.random.fold_in(key, 23))


def level_of(key, dims, shards, smallest, largest):
    level, own = 1.0, jax.random.fold_in(key, 6)
    for dim, blocks in shards:
        heights = jnp.exp(jax.random.uniform(jax.random.fold_in(own, dim), (blocks,), jnp.float32, smallest / len(shards), largest / len(shards)))
        level = level * jnp.repeat(heights, dims[dim] // blocks).reshape([-1 if axis == dim else 1 for axis in range(len(dims))])
    return level


def scatter_about(own_key, shape, scale, limit, shards=(), kind=jnp.bfloat16):
    entries = jax.random.normal(own_key, shape, jnp.float32) * scale
    if len(shards) > 0:
        entries = level_of(own_key, shape, shards, -0.22, 0.18) * entries
    return jnp.clip(entries, min=-limit, max=limit).astype(kind)


def setup_inputs(seed: int = 0) -> dict:
    streams_of = jax.random.split(jax.random.key(seed), 14)
    hidden = scatter_about(streams_of[0], (TOKENS, MODEL_WIDTH), 1.0, 6.0, ((0, 16), (1, 2)))
    norm_before = jnp.clip(1.0 + 0.18 * jax.random.normal(streams_of[1], (MODEL_WIDTH,), jnp.float32), 0.1, 1.9)
    query_weight = scatter_about(streams_of[2], (MODEL_WIDTH, QUERY_HEADS * HEAD_SIZE), MODEL_WIDTH ** -0.5, 0.125, ((0, 2), (1, 4)))
    key_matrix = scatter_about(streams_of[3], (MODEL_WIDTH, KEY_VALUE_HEADS * HEAD_SIZE), MODEL_WIDTH ** -0.5, 0.125, ((0, 2), (1, 4)))
    value_matrix = scatter_about(streams_of[4], (MODEL_WIDTH, KEY_VALUE_HEADS * HEAD_SIZE), MODEL_WIDTH ** -0.5, 0.125, ((0, 2), (1, 4)))
    query_gain = draw_query_gain(jax.random.fold_in(streams_of[13], 71), 0)
    key_gain = draw_key_gain(jax.random.fold_in(streams_of[13], 71), 0)
    output_weight = scatter_about(streams_of[7], (QUERY_HEADS * HEAD_SIZE, MODEL_WIDTH), (QUERY_HEADS * HEAD_SIZE // 64) ** -0.5, 1.0, ((0, 4), (1, 2)))
    norm_after = jnp.clip(1.0 + 0.18 * jax.random.normal(streams_of[8], (MODEL_WIDTH,), jnp.float32), 0.1, 1.9)
    gate_weight = scatter_about(streams_of[9], (MODEL_WIDTH, FF), MODEL_WIDTH ** -0.5, 0.125, ((0, 2), (1, 4)))
    up_weight = scatter_about(streams_of[10], (MODEL_WIDTH, FF), MODEL_WIDTH ** -0.5, 0.125, ((0, 2), (1, 4)))
    down_weight = scatter_about(streams_of[11], (FF, MODEL_WIDTH), FF ** -0.5, 0.078125, ((0, 4), (1, 2)))
    cotangent = scatter_about(streams_of[12], (TOKENS, MODEL_WIDTH), 1.0, 6.0, ((0, 16), (1, 2)))
    return dict(hidden=hidden, norm_before=norm_before, query_weight=query_weight, key_matrix=key_matrix, value_matrix=value_matrix, query_gain=query_gain, key_gain=key_gain, output_weight=output_weight, norm_after=norm_after, gate_weight=gate_weight, up_weight=up_weight, down_weight=down_weight, cotangent=cotangent)


EPS = 1e-06
THETA = 1000000.0
HIGH = lax.Precision.HIGHEST

@jax.custom_vjp
def low(v):
    return lax.optimization_barrier(v.astype(jnp.bfloat16)).astype(jnp.float32)

@jax.custom_vjp
def low_back(v):
    return v

def low_keep(v):
    return (low(v), None)

def low_pass(kept, grad):
    return (grad,)

def back_keep(v):
    return (v, None)

def back_low(kept, grad):
    return (low(grad),)
low.defvjp(low_keep, low_pass)
low_back.defvjp(back_keep, back_low)

def matrix_product(left, right):
    return jnp.dot(left, right, precision=HIGH, preferred_element_type=jnp.float32)

def normed(value_rows, gain):
    factor = lax.rsqrt(lax.optimization_barrier(jnp.mean(value_rows * value_rows, axis=-1, keepdims=True)) + EPS)
    return value_rows * factor * gain

def rope_tables():
    half = HEAD_SIZE // 2
    freq = THETA ** (-(jnp.arange(half, dtype=jnp.float32) * 2.0) / HEAD_SIZE)
    angle = jnp.arange(SEQUENCE_LENGTH, dtype=jnp.float32)[:, None] * freq[None, :]
    cosine = jnp.cos(angle)
    sine = jnp.sin(angle)
    return (jnp.concatenate([cosine, cosine], 1), jnp.concatenate([-sine, sine], 1))

def rotate(value_rows, cosine, sine):
    return value_rows * cosine[None, :, None, :] + jnp.roll(value_rows, HEAD_SIZE // 2, axis=3) * sine[None, :, None, :]

def attend(blocks):
    query, key, value_tensor = blocks
    key_rows = jnp.repeat(key, QUERY_HEADS // KEY_VALUE_HEADS, axis=1)
    value_rows = jnp.repeat(value_tensor, QUERY_HEADS // KEY_VALUE_HEADS, axis=1)
    raw = low_back(jnp.einsum('qhd,khd->hqk', query, key_rows, precision=HIGH))
    places = jnp.arange(SEQUENCE_LENGTH)
    causal = (places[:, None] >= places[None, :])[None]
    scores = jnp.where(causal, raw * (1.0 / math.sqrt(HEAD_SIZE)), -1e+30)
    top = lax.optimization_barrier(jnp.max(scores, axis=2, keepdims=True))
    expo = jnp.exp(scores - top)
    prob = expo / lax.optimization_barrier(jnp.sum(expo, axis=2, keepdims=True))
    return jnp.einsum('hqk,khd->qhd', low(prob), value_rows, precision=HIGH)

def layer(hidden, norm_before, query_weight, key_matrix, value_matrix, query_gain, key_gain, output_weight, norm_after, gate_weight, up_weight, down_weight):
    cosine, sine = rope_tables()
    leading_part = low(normed(hidden, norm_before))
    query_raw = low_back(matrix_product(leading_part, query_weight)).reshape(SEQUENCE_COUNT, SEQUENCE_LENGTH, QUERY_HEADS, HEAD_SIZE)
    key_unnormed = low_back(matrix_product(leading_part, key_matrix)).reshape(SEQUENCE_COUNT, SEQUENCE_LENGTH, KEY_VALUE_HEADS, HEAD_SIZE)
    value_tensor = low(low_back(matrix_product(leading_part, value_matrix))).reshape(SEQUENCE_COUNT, SEQUENCE_LENGTH, KEY_VALUE_HEADS, HEAD_SIZE)
    query = low(rotate(normed(query_raw, query_gain), cosine, sine))
    key = low(rotate(normed(key_unnormed, key_gain), cosine, sine))
    attended = lax.map(jax.checkpoint(attend), (query, key, value_tensor))
    attended = low(low_back(attended.reshape(TOKENS, QUERY_HEADS * HEAD_SIZE)))
    middle = hidden + low_back(matrix_product(attended, output_weight))
    second = low(normed(middle, norm_after))
    gate = low_back(matrix_product(second, gate_weight))
    upper = low_back(matrix_product(second, up_weight))
    mixed = low(jax.nn.silu(gate) * upper)
    return middle + low_back(matrix_product(mixed, down_weight))

def reference(hidden, norm_before, query_weight, key_matrix, value_matrix, query_gain, key_gain, output_weight, norm_after, gate_weight, up_weight, down_weight, cotangent):
    inputs = (hidden, norm_before, query_weight, key_matrix, value_matrix, query_gain, key_gain, output_weight, norm_after, gate_weight, up_weight, down_weight)
    inputs = tuple((item.astype(jnp.float32) for item in inputs))
    result, pullback = jax.vjp(layer, *inputs)
    grads = pullback(cotangent.astype(jnp.float32))
    return (result.astype(jnp.bfloat16), grads[0], grads[1], grads[2], grads[3], grads[4], grads[5], grads[6], grads[7], grads[8], grads[9], grads[10], grads[11])
```

```python
import functools
import math

import jax
import jax.numpy as jnp
from jax import lax
from jax.experimental import pallas as pl
from jax.experimental.pallas import tpu as pltpu
from jax.sharding import PartitionSpec as P

MODEL_WIDTH = 2048
HEAD_SIZE = 128
SEQUENCE_LENGTH = 1024
EPS = 1e-06
THETA = 1000000.0
ROWS = 4
BLOCK = SEQUENCE_LENGTH // ROWS
SCALE = 1.0 / math.sqrt(HEAD_SIZE)
LOG2 = SCALE * math.log2(math.e)

F32 = jnp.float32
BF16 = jnp.bfloat16


def swap(x):
    return lax.ppermute(x, "col", [(0, 1), (1, 0)])


def row_swap(x, mask):
    return lax.ppermute(x, "row", [(i, i ^ mask) for i in range(ROWS)])


def gather_slots(x):
    two = row_swap(x, 2)
    one = row_swap(x, 1)
    three = row_swap(two, 1)
    return [x, one, two, three]


def scatter_slots(own, one, two, three):
    got_three = row_swap(three.astype(BF16), 1)
    got_one = row_swap(one.astype(BF16), 1)
    got_two = row_swap((two + got_three.astype(F32)).astype(BF16), 2)
    return own + got_one.astype(F32) + got_two.astype(F32)


def dp_swap(x, mask, dp):
    return lax.ppermute(x, "dp", [(i, i ^ mask) for i in range(dp)])


def halving(part, bits, me, dp):
    first, second = bits
    v1, v2 = (me // first) % 2, (me // second) % 2
    half = part.shape[0] // 2
    kept = lax.dynamic_slice_in_dim(part, v1 * half, half, 0)
    sent = lax.dynamic_slice_in_dim(part, (1 - v1) * half, half, 0)
    total = (kept.astype(F32) + dp_swap(sent, first, dp).astype(F32)).astype(BF16)
    quarter = half // 2
    kept = lax.dynamic_slice_in_dim(total, v2 * quarter, quarter, 0)
    sent = lax.dynamic_slice_in_dim(total, (1 - v2) * quarter, quarter, 0)
    mine = (kept.astype(F32) + dp_swap(sent, second, dp).astype(F32)).astype(BF16)
    near = dp_swap(mine, second, dp)
    far = dp_swap(mine, first, dp)
    cross = dp_swap(near, first, dp)
    return [mine, near, far, cross]


def piece_rows(bits, me):
    first, second = bits
    rows = []
    for mask in (0, second, first, first + second):
        who = me ^ mask
        rows.append(((who // first) % 2) * 2 + (who // second) % 2)
    return rows


def assemble_kernel(spans, table_ref, *refs):
    pieces, outs = refs[:8], refs[8:]
    half, slot = pl.program_id(0), pl.program_id(1)
    for h in range(2):
        for s in range(4):

            @pl.when((half == h) & (slot == s))
            def _(piece=pieces[h * 4 + s]):
                for (lo, hi), out in zip(spans, outs):
                    out[...] = piece[:, lo:hi].astype(F32)


def assemble(pieces_a, pieces_b, me, core, widths, split):
    rows, columns = pieces_a[0].shape
    spans, at = [], 0
    for width in widths:
        spans.append((at, at + width))
        at += width
    block_rows, block_cols = [], []
    for half, bits in ((core, (1, 2)), (1 - core, (2, 1))):
        ids = piece_rows(bits, me)
        block_rows += [half * 4 + r if split == 0 else r for r in ids]
        block_cols.append(half if split == 1 else 0 * half)
    table = jnp.stack(block_rows + block_cols).astype(jnp.int32)
    full = [
        (rows * (8 if split == 0 else 4), width * (2 if split == 1 else 1)) for width in widths
    ]
    return pl.pallas_call(
        functools.partial(assemble_kernel, spans),
        out_shape=[jax.ShapeDtypeStruct(shape, F32) for shape in full],
        grid_spec=pltpu.PrefetchScalarGridSpec(
            num_scalar_prefetch=1,
            grid=(2, 4),
            in_specs=[pl.BlockSpec((rows, columns), lambda h, s, t: (0, 0))] * 8,
            out_specs=[
                pl.BlockSpec((rows, width), lambda h, s, t: (t[h * 4 + s], t[8 + h]))
                for width in widths
            ],
        ),
        cost_estimate=pl.CostEstimate(
            flops=0, transcendentals=0, bytes_accessed=8 * rows * columns * 6
        ),
    )(table, *pieces_a, *pieces_b)


def reduce_grads(part_a, part_b, me, core, dp, widths, split):
    if dp == 4:
        pieces_a = halving(part_a, (1, 2), me, dp)
        pieces_b = halving(part_b, (2, 1), me, dp)
        return assemble(pieces_a, pieces_b, me, core, widths, split)
    total_a, total_b = lax.psum(part_a, "dp"), lax.psum(part_b, "dp")
    outs, at = [], 0
    for width in widths:
        a, b = total_a[:, at : at + width], total_b[:, at : at + width]
        axis = split
        nat = jnp.where(core == 0, jnp.concatenate([a, b], axis), jnp.concatenate([b, a], axis))
        outs.append(nat.astype(F32))
        at += width
    return outs


def rope_tables():
    half = HEAD_SIZE // 2
    freq = THETA ** (-(jnp.arange(half, dtype=F32) * 2.0) / HEAD_SIZE)
    angle = jnp.arange(SEQUENCE_LENGTH, dtype=F32)[:, None] * freq[None, :]
    cosine = jnp.cos(angle)
    sine = jnp.sin(angle)
    return (jnp.concatenate([cosine, cosine], 1), jnp.concatenate([-sine, sine], 1))


def dot(a, b, dims):
    return lax.dot_general(a, b, (dims, ((), ())), preferred_element_type=F32)


NN = ((1,), (0,))
NT = ((1,), (1,))
TN = ((0,), (0,))


def unit_rows(x):
    factor = lax.rsqrt(jnp.mean(x * x, axis=1, keepdims=True) + EPS)
    return x * factor, factor


def raw_scores(query, key, block):
    scores = dot(query, key, NT)
    row = lax.broadcasted_iota(jnp.int32, scores.shape, 0) + block * BLOCK
    column = lax.broadcasted_iota(jnp.int32, scores.shape, 1)
    return jnp.where(row >= column, scores, -1e30)


def attend_kernel(groups, table, *refs):
    raws = refs[:ROWS]
    cosine, sine, q_gain, k_gain = refs[ROWS : ROWS + 4]
    att, lse, query, key, value = refs[ROWS + 4 :]
    width = HEAD_SIZE
    for s in range(ROWS):
        rows = pl.ds(pl.multiple_of(table[s] * BLOCK, BLOCK), BLOCK)
        cos, sin = cosine[rows, :], sine[rows, :]
        for h in range(groups + 1):
            unit, _ = unit_rows(raws[s][:, h * width : (h + 1) * width])
            gained = unit * (q_gain[...] if h < groups else k_gain[...])
            turned = gained * cos + pltpu.roll(gained, width // 2, 1) * sin
            if h < groups:
                query[rows, h * width : (h + 1) * width] = turned.astype(BF16)
            else:
                key[rows, :] = turned.astype(BF16)
        value[rows, :] = raws[s][:, (groups + 1) * width :].astype(BF16)
    for i in range(ROWS):
        span = (i + 1) * BLOCK
        slot = table[ROWS + i]
        rows = pl.ds(pl.multiple_of(slot * BLOCK, BLOCK), BLOCK)
        for h in range(groups):
            cols = slice(h * width, (h + 1) * width)
            scores = raw_scores(query[i * BLOCK : span, cols], key[:span, :], i)
            top = jnp.max(scores, axis=1, keepdims=True)
            expo = jnp.exp2((scores - top) * LOG2)
            total = jnp.sum(expo, axis=1, keepdims=True)
            prob = (expo * (1.0 / total)).astype(BF16)
            att[rows, cols] = dot(prob, value[:span, :], NN).astype(BF16)
            log = top * LOG2 + jnp.log2(total)
            lse[i * BLOCK : span, cols] = jnp.broadcast_to(log, (BLOCK, width))


def attend_back_kernel(groups, table, *refs):
    raws = refs[:ROWS]
    grads = refs[ROWS : 2 * ROWS]
    cosine, sine, q_gain, k_gain, query, key, value, lse = refs[2 * ROWS : 2 * ROWS + 8]
    out, gains, d_query, d_key, d_value, grad = refs[2 * ROWS + 8 :]
    width = HEAD_SIZE
    for s in range(ROWS):
        rows = pl.ds(pl.multiple_of(table[s] * BLOCK, BLOCK), BLOCK)
        grad[rows, :] = grads[s][...]
    d_key[...] = jnp.zeros_like(d_key)
    d_value[...] = jnp.zeros_like(d_value)
    for i in range(ROWS):
        span = (i + 1) * BLOCK
        for h in range(groups):
            cols = slice(h * width, (h + 1) * width)
            q = query[i * BLOCK : span, cols]
            g = grad[i * BLOCK : span, cols]
            scores = raw_scores(q, key[:span, :], i)
            log = lse[i * BLOCK : span, h * width : h * width + 1]
            prob = jnp.exp2(scores * LOG2 - log)
            dprob = dot(g, value[:span, :], NT)
            delta = jnp.sum(prob * dprob, axis=1, keepdims=True)
            dscore = (SCALE * prob * (dprob - delta)).astype(BF16)
            d_query[i * BLOCK : span, cols] = dot(dscore, key[:span, :], NN)
            d_key[:span, :] += dot(dscore, q, TN)
            d_value[:span, :] += dot(prob.astype(BF16), g, TN)
    gain_sums = [jnp.zeros((1, width), F32), jnp.zeros((1, width), F32)]
    for s in range(ROWS):
        rows = pl.ds(pl.multiple_of(table[s] * BLOCK, BLOCK), BLOCK)
        cos, sin = cosine[rows, :], sine[rows, :]
        for h in range(groups + 1):
            cols = slice(h * width, (h + 1) * width)
            unit, factor = unit_rows(raws[s][:, cols])
            turned = d_query[rows, cols] if h < groups else d_key[rows, :]
            back = turned * cos + pltpu.roll(turned * sin, width // 2, 1)
            scaled = back * (q_gain[...] if h < groups else k_gain[...])
            inner = jnp.mean(scaled * unit, axis=1, keepdims=True)
            which = 0 if h < groups else 1
            gain_sums[which] += jnp.sum(back * unit, axis=0, keepdims=True)
            out[s * BLOCK : (s + 1) * BLOCK, cols] = (factor * (scaled - unit * inner)).astype(BF16)
        out[s * BLOCK : (s + 1) * BLOCK, (groups + 1) * width :] = d_value[rows, :].astype(BF16)
    gains[0:1, :] = gain_sums[0]
    gains[1:2, :] = gain_sums[1]


SMEM = pl.BlockSpec(memory_space=pltpu.SMEM)
VMEM = pl.BlockSpec(memory_space=pltpu.VMEM)


def attention_cost(groups, products):
    area = groups * SEQUENCE_LENGTH * SEQUENCE_LENGTH * 5 // 8
    return pl.CostEstimate(
        flops=2 * products * area * HEAD_SIZE + 30 * area,
        transcendentals=area,
        bytes_accessed=SEQUENCE_LENGTH * HEAD_SIZE * 4 * (groups + 2) * 3,
    )


def attend(table, raws, cosine, sine, q_gain, k_gain, groups):
    wide = (SEQUENCE_LENGTH, groups * HEAD_SIZE)
    one = (SEQUENCE_LENGTH, HEAD_SIZE)
    return pl.pallas_call(
        functools.partial(attend_kernel, groups),
        out_shape=[
            jax.ShapeDtypeStruct(wide, BF16),
            jax.ShapeDtypeStruct(wide, F32),
            jax.ShapeDtypeStruct(wide, BF16),
            jax.ShapeDtypeStruct(one, BF16),
            jax.ShapeDtypeStruct(one, BF16),
        ],
        in_specs=[SMEM] + [VMEM] * (ROWS + 4),
        out_specs=[VMEM] * 5,
        cost_estimate=attention_cost(groups, 2),
    )(table, *raws, cosine, sine, q_gain[None], k_gain[None])


def attend_back(table, raws, grads, cosine, sine, q_gain, k_gain, saved, groups):
    query, key, value, lse = saved
    return pl.pallas_call(
        functools.partial(attend_back_kernel, groups),
        out_shape=[
            jax.ShapeDtypeStruct((SEQUENCE_LENGTH, (groups + 2) * HEAD_SIZE), BF16),
            jax.ShapeDtypeStruct((2, HEAD_SIZE), F32),
        ],
        in_specs=[SMEM] + [VMEM] * (2 * ROWS + 8),
        out_specs=[VMEM] * 2,
        scratch_shapes=[
            pltpu.VMEM((SEQUENCE_LENGTH, groups * HEAD_SIZE), F32),
            pltpu.VMEM((SEQUENCE_LENGTH, HEAD_SIZE), F32),
            pltpu.VMEM((SEQUENCE_LENGTH, HEAD_SIZE), F32),
            pltpu.VMEM((SEQUENCE_LENGTH, groups * HEAD_SIZE), BF16),
        ],
        cost_estimate=attention_cost(groups, 5),
    )(table, *raws, *grads, cosine, sine, q_gain[None], k_gain[None], query, key, value, lse)


def own_other(weight, core, axis):
    half = weight.shape[axis] // 2
    return (
        lax.dynamic_slice_in_dim(weight, core * half, half, axis),
        lax.dynamic_slice_in_dim(weight, (1 - core) * half, half, axis),
    )


def norm_stats(x):
    part = jnp.sum(x * x, axis=1)
    factor = lax.rsqrt((part + swap(part)) / MODEL_WIDTH + EPS)
    return x * factor[:, None], factor


def norm_backward(grad, unit, factor, gain):
    scaled = grad * gain
    part = jnp.sum(scaled * unit, axis=1)
    inner = (part + swap(part)) / MODEL_WIDTH
    return (factor[:, None] * (scaled - unit * inner[:, None]), jnp.sum(grad * unit, axis=0))


def cat(items, axis):
    return jnp.concatenate(items, axis)


def after(x, *others):
    return lax.optimization_barrier((x, *others))[0]


def on_device(
    hidden,
    norm_before,
    query_weight,
    key_matrix,
    value_matrix,
    query_gain,
    key_gain,
    output_weight,
    norm_after,
    gate_weight,
    up_weight,
    down_weight,
    cotangent,
):
    dp = lax.axis_size("dp")
    k, core, me = lax.axis_index("row"), lax.axis_index("col"), lax.axis_index("dp")
    table = jnp.stack([k ^ i for i in range(ROWS)] * 2).astype(jnp.int32)
    groups = query_weight.shape[1] // (2 * HEAD_SIZE)
    cosine, sine = rope_tables()

    q_own, q_oth = own_other(query_weight, core, 1)
    k_own, k_oth = own_other(key_matrix, core, 1)
    v_own, v_oth = own_other(value_matrix, core, 1)
    g_own, g_oth = own_other(gate_weight, core, 1)
    u_own, u_oth = own_other(up_weight, core, 1)
    down_own, down_oth = own_other(down_weight, core, 0)
    out_own, out_oth = own_other(output_weight, core, 0)
    qkv_own, qkv_oth = cat([q_own, k_own, v_own], 1), cat([q_oth, k_oth, v_oth], 1)
    gu_own, gu_oth = cat([g_own, u_own], 1), cat([g_oth, u_oth], 1)

    resid = hidden.astype(F32)
    unit_one, factor_one = norm_stats(resid)
    n1 = gather_slots((unit_one * norm_before).astype(BF16))
    qkv_full = cat([qkv_own, swap(qkv_oth)], 0)
    raws = [dot(cat([x, swap(x)], 1), qkv_full, NN) for x in n1]
    att, lse, query, key, value = attend(table, raws, cosine, sine, query_gain, key_gain, groups)

    cot = gather_slots(after(cotangent, n1[3]))
    gu_full = cat([gu_own, swap(gu_oth)], 0)
    down_full = cat([down_own, swap(down_oth)], 1)

    att_oth = swap(att)
    att_both = cat([att, att_oth], 1)
    out_both = cat([out_own, out_oth], 0)
    parts = [dot(att_both[s * BLOCK : (s + 1) * BLOCK], out_both, NN) for s in range(ROWS)]
    middle = resid + scatter_slots(*parts)

    unit_two, factor_two = norm_stats(middle)
    n2 = gather_slots((unit_two * norm_after).astype(BF16))
    ff = g_own.shape[1]
    g_mixed = [dot(cat([x, swap(x)], 1), down_full, NT) for x in cot]
    mixed, dgu, mixed_oth, dgu_oth = [], [], [], []
    for s in range(ROWS):
        both = dot(cat([n2[s], swap(n2[s])], 1), gu_full, NN)
        gate, upper = both[:, :ff], both[:, ff:]
        sigma = jax.nn.sigmoid(gate)
        activ = gate * sigma
        gm = g_mixed[s]
        packed = cat(
            [
                (activ * upper).astype(BF16),
                (gm * upper * sigma * (1.0 + gate * (1.0 - sigma))).astype(BF16),
                (gm * activ).astype(BF16),
            ],
            1,
        )
        other = swap(packed)
        mixed.append(packed[:, :ff])
        dgu.append(packed[:, ff:])
        mixed_oth.append(other[:, :ff])
        dgu_oth.append(other[:, ff:])
    gu_both = cat([gu_own, gu_oth], 1)
    parts = [dot(cat([dgu[s], dgu_oth[s]], 1), gu_both, NT) for s in range(ROWS)]
    dsecond = scatter_slots(*parts)

    cot_all = cat(cot, 0)
    mixed_all, mixed_oth_all = cat(mixed, 0), cat(mixed_oth, 0)
    (down_grad,) = reduce_grads(
        dot(mixed_all, cot_all, TN).astype(BF16),
        dot(mixed_oth_all, cot_all, TN).astype(BF16),
        me, core, dp, (down_weight.shape[1],), 0,
    )
    n2_all = cat(n2, 0)
    gate_grad, up_grad = reduce_grads(
        dot(n2_all, cat(dgu, 0), TN).astype(BF16),
        dot(n2_all, cat(dgu_oth, 0), TN).astype(BF16),
        me, core, dp, (ff, ff), 1,
    )

    dmid_norm, after_part = norm_backward(dsecond, unit_two, factor_two, norm_after)
    dmiddle = cotangent.astype(F32) + dmid_norm
    dmid = gather_slots(dmiddle.astype(BF16))

    down_both = cat([down_own, down_oth], 0)
    parts = [dot(cat([mixed[s], mixed_oth[s]], 1), down_both, NN) for s in range(ROWS)]
    parts[1], parts[3] = after(parts[1], dmid[3]), after(parts[3], dmid[3])
    layer_out = (middle + scatter_slots(*parts)).astype(BF16)

    datt = [
        (dot(x, out_own, NT) + swap(dot(x, out_oth, NT).astype(BF16)).astype(F32)).astype(BF16)
        for x in dmid
    ]
    dmid_all = cat(dmid, 0)
    (output_grad,) = reduce_grads(
        dot(att, dmid_all, TN).astype(BF16),
        dot(att_oth, dmid_all, TN).astype(BF16),
        me, core, dp, (output_weight.shape[1],), 0,
    )
    dqkv, gain_parts = attend_back(
        table, raws, datt, cosine, sine, query_gain, key_gain, (query, key, value, lse), groups
    )
    dqkv_oth = swap(dqkv)
    dqkv_both = cat([dqkv, dqkv_oth], 1)
    qkv_both = cat([qkv_own, qkv_oth], 1)
    parts = [dot(dqkv_both[s * BLOCK : (s + 1) * BLOCK], qkv_both, NT) for s in range(ROWS)]
    dfirst = scatter_slots(*parts)
    n1_all = cat(n1, 0)
    query_grad, key_grad, value_grad = reduce_grads(
        dot(n1_all, dqkv, TN).astype(BF16),
        dot(n1_all, dqkv_oth, TN).astype(BF16),
        me, core, dp, (q_own.shape[1], k_own.shape[1], v_own.shape[1]), 1,
    )
    dres_norm, before_part = norm_backward(dfirst, unit_one, factor_one, norm_before)
    hidden_grad = dmiddle + dres_norm

    before_grad, after_grad = lax.psum((before_part, after_part), ("dp", "row"))
    gain_query, gain_key = lax.psum((gain_parts[0], gain_parts[1]), ("dp", "row", "col"))
    return (
        layer_out,
        hidden_grad,
        before_grad,
        query_grad,
        key_grad,
        value_grad,
        gain_query,
        gain_key,
        output_grad,
        after_grad,
        gate_grad,
        up_grad,
        down_grad,
    )


def solution(mesh):
    placed = (
        P(("dp", "row"), "col"),
        P("col"),
        P("col", "row"),
        P("col", "row"),
        P("col", "row"),
        P(),
        P(),
        P("row", "col"),
        P("col"),
        P("col", "row"),
        P("col", "row"),
        P("row", "col"),
        P(("dp", "row"), "col"),
    )
    return jax.shard_map(
        on_device,
        mesh=mesh,
        in_specs=placed,
        out_specs=(
            P(("dp", "row"), "col"),
            P(("dp", "row"), "col"),
            P("col"),
            P("col", "row"),
            P("col", "row"),
            P("col", "row"),
            P(),
            P(),
            P("row", "col"),
            P("col"),
            P("col", "row"),
            P("col", "row"),
            P("row", "col"),
        ),
        check_vma=False,
    )
```

```python
import functools
import math

import jax
import jax.numpy as jnp
from jax import lax
from jax.experimental import pallas as pl
from jax.experimental.pallas import tpu as pltpu
from jax.sharding import PartitionSpec as P

MODEL_WIDTH = 2048
HEAD_SIZE = 128
SEQUENCE_LENGTH = 1024
EPS = 1e-06
THETA = 1000000.0
ROWS = 4
BLOCK = SEQUENCE_LENGTH // ROWS
SCALE = 1.0 / math.sqrt(HEAD_SIZE)
LOG2 = SCALE * math.log2(math.e)

F32 = jnp.float32
BF16 = jnp.bfloat16
SMEM = pl.BlockSpec(memory_space=pltpu.SMEM)
VMEM = pl.BlockSpec(memory_space=pltpu.VMEM)
NO_COST = pl.CostEstimate(flops=1, transcendentals=0, bytes_accessed=1)


def swap(x):
    return lax.ppermute(x, "col", [(0, 1), (1, 0)])


def row_swap(x, mask):
    return lax.ppermute(x, "row", [(i, i ^ mask) for i in range(ROWS)])


def after(x, *others):
    return lax.optimization_barrier((x, *others))[0]


def dp_swap(x, mask, dp):
    return lax.ppermute(x, "dp", [(i, i ^ mask) for i in range(dp)])


def small_sum(x, axis, size):
    swapped = lambda mask: lax.ppermute(x, axis, [(i, i ^ mask) for i in range(size)])
    if size == 4:
        return (x + swapped(1)) + (swapped(2) + swapped(3))
    return lax.psum(x, axis)


def halving(part, bits, me, dp):
    first, second = bits
    v1, v2 = (me // first) % 2, (me // second) % 2
    half = part.shape[0] // 2
    kept = lax.dynamic_slice_in_dim(part, v1 * half, half, 0)
    sent = lax.dynamic_slice_in_dim(part, (1 - v1) * half, half, 0)
    total = (kept.astype(F32) + dp_swap(sent, first, dp).astype(F32)).astype(BF16)
    quarter = half // 2
    kept = lax.dynamic_slice_in_dim(total, v2 * quarter, quarter, 0)
    sent = lax.dynamic_slice_in_dim(total, (1 - v2) * quarter, quarter, 0)
    mine = (kept.astype(F32) + dp_swap(sent, second, dp).astype(F32)).astype(BF16)
    near = dp_swap(mine, second, dp)
    far = dp_swap(mine, first, dp)
    cross = dp_swap(near, first, dp)
    return [mine, near, far, cross]


def piece_rows(bits, me):
    first, second = bits
    rows = []
    for mask in (0, second, first, first + second):
        who = me ^ mask
        rows.append(((who // first) % 2) * 2 + (who // second) % 2)
    return rows


def assemble_kernel(spans, table_ref, *refs):
    pieces, outs = refs[:8], refs[8:]
    half, slot = pl.program_id(0), pl.program_id(1)
    for h in range(2):
        for s in range(4):

            @pl.when((half == h) & (slot == s))
            def _(piece=pieces[h * 4 + s]):
                for (lo, hi), out in zip(spans, outs):
                    out[...] = piece[:, lo:hi].astype(F32)


def assemble(pieces_a, pieces_b, me, core, widths, split):
    rows, columns = pieces_a[0].shape
    spans, at = [], 0
    for width in widths:
        spans.append((at, at + width))
        at += width
    block_rows, block_cols = [], []
    for half, bits in ((core, (1, 2)), (1 - core, (2, 1))):
        ids = piece_rows(bits, me)
        block_rows += [half * 4 + r if split == 0 else r for r in ids]
        block_cols.append(half if split == 1 else 0 * half)
    table = jnp.stack(block_rows + block_cols).astype(jnp.int32)
    full = [
        (rows * (8 if split == 0 else 4), width * (2 if split == 1 else 1)) for width in widths
    ]
    return pl.pallas_call(
        functools.partial(assemble_kernel, spans),
        out_shape=[jax.ShapeDtypeStruct(shape, F32) for shape in full],
        grid_spec=pltpu.PrefetchScalarGridSpec(
            num_scalar_prefetch=1,
            grid=(2, 4),
            in_specs=[pl.BlockSpec((rows, columns), lambda h, s, t: (0, 0))] * 8,
            out_specs=[
                pl.BlockSpec((rows, width), lambda h, s, t: (t[h * 4 + s], t[8 + h]))
                for width in widths
            ],
        ),
        compiler_params=pltpu.CompilerParams(vmem_limit_bytes=16 << 20),
        cost_estimate=NO_COST,
    )(table, *pieces_a, *pieces_b)


def place_kernel(widths, table_ref, a_ref, b_ref, *outs):
    for half, ref in enumerate((a_ref, b_ref)):

        @pl.when(pl.program_id(0) == half)
        def _(ref=ref):
            at = 0
            for width, out in zip(widths, outs):
                out[...] = ref[:, at : at + width].astype(F32)
                at += width


def place(total_a, total_b, core, widths):
    rows, columns = total_a.shape
    block = min(256, rows)
    last = rows // block - 1
    table = jnp.stack([core, 1 - core]).astype(jnp.int32)
    return pl.pallas_call(
        functools.partial(place_kernel, widths),
        out_shape=[jax.ShapeDtypeStruct((rows, 2 * width), F32) for width in widths],
        grid_spec=pltpu.PrefetchScalarGridSpec(
            num_scalar_prefetch=1,
            grid=(2, rows // block),
            in_specs=[
                pl.BlockSpec((block, columns), lambda h, r, t: (jnp.where(h == 0, r, last), 0)),
                pl.BlockSpec((block, columns), lambda h, r, t: (jnp.where(h == 1, r, 0), 0)),
            ],
            out_specs=[pl.BlockSpec((block, width), lambda h, r, t: (r, t[h])) for width in widths],
        ),
        compiler_params=pltpu.CompilerParams(vmem_limit_bytes=16 << 20),
        cost_estimate=NO_COST,
    )(table, total_a, total_b)


def reduce_grads(part_a, part_b, me, core, dp, widths, split):
    if dp == 4:
        pieces_a = halving(part_a, (1, 2), me, dp)
        pieces_b = halving(part_b, (2, 1), me, dp)
        return assemble(pieces_a, pieces_b, me, core, widths, split)
    total_a, total_b = lax.psum(part_a, "dp"), lax.psum(part_b, "dp")
    outs, at = [], 0
    for width in widths:
        a, b = total_a[:, at : at + width], total_b[:, at : at + width]
        axis = split
        nat = jnp.where(core == 0, jnp.concatenate([a, b], axis), jnp.concatenate([b, a], axis))
        outs.append(nat.astype(F32))
        at += width
    return outs


def rope_tables():
    half = HEAD_SIZE // 2
    freq = THETA ** (-(jnp.arange(half, dtype=F32) * 2.0) / HEAD_SIZE)
    angle = jnp.arange(SEQUENCE_LENGTH, dtype=F32)[:, None] * freq[None, :]
    cosine = jnp.cos(angle)
    sine = jnp.sin(angle)
    return (jnp.concatenate([cosine, cosine], 1), jnp.concatenate([-sine, sine], 1))


def dot(a, b, dims):
    return lax.dot_general(a, b, (dims, ((), ())), preferred_element_type=F32)


NN = ((1,), (0,))
NT = ((1,), (1,))
TN = ((0,), (0,))


def unit_rows(x):
    factor = lax.rsqrt(jnp.mean(x * x, axis=1, keepdims=True) + EPS)
    return x * factor, factor


def raw_scores(query, key, block):
    scores = dot(query, key, NT)
    row = lax.broadcasted_iota(jnp.int32, scores.shape, 0) + block * BLOCK
    column = lax.broadcasted_iota(jnp.int32, scores.shape, 1)
    return jnp.where(row >= column, scores, -1e30)


def attend_kernel(groups, table, *refs):
    raws = refs[:ROWS]
    cosine, sine, q_gain, k_gain = refs[ROWS : ROWS + 4]
    att, lse, query, key, value = refs[ROWS + 4 :]
    width = HEAD_SIZE
    for s in range(ROWS):
        rows = pl.ds(pl.multiple_of(table[s] * BLOCK, BLOCK), BLOCK)
        cos, sin = cosine[rows, :], sine[rows, :]
        for h in range(groups + 1):
            unit, _ = unit_rows(raws[s][:, h * width : (h + 1) * width])
            gained = unit * (q_gain[...] if h < groups else k_gain[...])
            turned = gained * cos + pltpu.roll(gained, width // 2, 1) * sin
            if h < groups:
                query[rows, h * width : (h + 1) * width] = turned.astype(BF16)
            else:
                key[rows, :] = turned.astype(BF16)
        value[rows, :] = raws[s][:, (groups + 1) * width :].astype(BF16)
    for i in range(ROWS):
        span = (i + 1) * BLOCK
        slot = table[ROWS + i]
        rows = pl.ds(pl.multiple_of(slot * BLOCK, BLOCK), BLOCK)
        for h in range(groups):
            cols = slice(h * width, (h + 1) * width)
            scores = raw_scores(query[i * BLOCK : span, cols], key[:span, :], i)
            top = jnp.max(scores, axis=1, keepdims=True)
            expo = jnp.exp2((scores - top) * LOG2)
            total = jnp.sum(expo, axis=1, keepdims=True)
            prob = (expo * (1.0 / total)).astype(BF16)
            att[rows, cols] = dot(prob, value[:span, :], NN).astype(BF16)
            log = top * LOG2 + jnp.log2(total)
            lse[i * BLOCK : span, cols] = jnp.broadcast_to(log, (BLOCK, width))


def attend_back_kernel(groups, table, *refs):
    raws = refs[:ROWS]
    grads, others = refs[ROWS : 2 * ROWS], refs[2 * ROWS : 3 * ROWS]
    cosine, sine, q_gain, k_gain, query, key, value, lse = refs[3 * ROWS : 3 * ROWS + 8]
    out, gains, d_query, d_key, d_value, grad = refs[3 * ROWS + 8 :]
    width = HEAD_SIZE
    for s in range(ROWS):
        rows = pl.ds(pl.multiple_of(table[s] * BLOCK, BLOCK), BLOCK)
        grad[rows, :] = (grads[s][...] + others[s][...].astype(F32)).astype(BF16)
    d_key[...] = jnp.zeros_like(d_key)
    d_value[...] = jnp.zeros_like(d_value)
    for i in range(ROWS):
        span = (i + 1) * BLOCK
        for h in range(groups):
            cols = slice(h * width, (h + 1) * width)
            q = query[i * BLOCK : span, cols]
            g = grad[i * BLOCK : span, cols]
            scores = raw_scores(q, key[:span, :], i)
            log = lse[i * BLOCK : span, h * width : h * width + 1]
            prob = jnp.exp2(scores * LOG2 - log)
            dprob = dot(g, value[:span, :], NT)
            delta = jnp.sum(prob * dprob, axis=1, keepdims=True)
            dscore = (SCALE * prob * (dprob - delta)).astype(BF16)
            d_query[i * BLOCK : span, cols] = dot(dscore, key[:span, :], NN)
            d_key[:span, :] += dot(dscore, q, TN)
            d_value[:span, :] += dot(prob.astype(BF16), g, TN)
    gain_sums = [jnp.zeros((1, width), F32), jnp.zeros((1, width), F32)]
    for s in range(ROWS):
        rows = pl.ds(pl.multiple_of(table[s] * BLOCK, BLOCK), BLOCK)
        cos, sin = cosine[rows, :], sine[rows, :]
        for h in range(groups + 1):
            cols = slice(h * width, (h + 1) * width)
            unit, factor = unit_rows(raws[s][:, cols])
            turned = d_query[rows, cols] if h < groups else d_key[rows, :]
            back = turned * cos + pltpu.roll(turned * sin, width // 2, 1)
            scaled = back * (q_gain[...] if h < groups else k_gain[...])
            inner = jnp.mean(scaled * unit, axis=1, keepdims=True)
            which = 0 if h < groups else 1
            gain_sums[which] += jnp.sum(back * unit, axis=0, keepdims=True)
            out[s * BLOCK : (s + 1) * BLOCK, cols] = (factor * (scaled - unit * inner)).astype(BF16)
        out[s * BLOCK : (s + 1) * BLOCK, (groups + 1) * width :] = d_value[rows, :].astype(BF16)
    gains[0:1, :] = gain_sums[0]
    gains[1:2, :] = gain_sums[1]


def attend(table, raws, cosine, sine, q_gain, k_gain, groups):
    wide = (SEQUENCE_LENGTH, groups * HEAD_SIZE)
    one = (SEQUENCE_LENGTH, HEAD_SIZE)
    return pl.pallas_call(
        functools.partial(attend_kernel, groups),
        out_shape=[
            jax.ShapeDtypeStruct(wide, BF16),
            jax.ShapeDtypeStruct(wide, F32),
            jax.ShapeDtypeStruct(wide, BF16),
            jax.ShapeDtypeStruct(one, BF16),
            jax.ShapeDtypeStruct(one, BF16),
        ],
        in_specs=[SMEM] + [VMEM] * (ROWS + 4),
        out_specs=[VMEM] * 5,
        compiler_params=pltpu.CompilerParams(vmem_limit_bytes=16 << 20),
        cost_estimate=NO_COST,
    )(table, *raws, cosine, sine, q_gain[None], k_gain[None])


def attend_back(table, raws, grads, others, cosine, sine, q_gain, k_gain, saved, groups):
    query, key, value, lse = saved
    return pl.pallas_call(
        functools.partial(attend_back_kernel, groups),
        out_shape=[
            jax.ShapeDtypeStruct((SEQUENCE_LENGTH, (groups + 2) * HEAD_SIZE), BF16),
            jax.ShapeDtypeStruct((2, HEAD_SIZE), F32),
        ],
        in_specs=[SMEM] + [VMEM] * (3 * ROWS + 8),
        out_specs=[VMEM] * 2,
        scratch_shapes=[
            pltpu.VMEM((SEQUENCE_LENGTH, groups * HEAD_SIZE), F32),
            pltpu.VMEM((SEQUENCE_LENGTH, HEAD_SIZE), F32),
            pltpu.VMEM((SEQUENCE_LENGTH, HEAD_SIZE), F32),
            pltpu.VMEM((SEQUENCE_LENGTH, groups * HEAD_SIZE), BF16),
        ],
        compiler_params=pltpu.CompilerParams(vmem_limit_bytes=20 << 20),
        cost_estimate=NO_COST,
    )(table, *raws, *grads, *others, cosine, sine, q_gain[None], k_gain[None], query, key, value, lse)


def product(kernel, t, ins, outs):
    return pl.pallas_call(
        kernel,
        out_shape=[jax.ShapeDtypeStruct(shape, kind) for shape, kind in outs],
        in_specs=[SMEM] + [VMEM] * len(ins),
        out_specs=[VMEM] * len(outs),
        compiler_params=pltpu.CompilerParams(vmem_limit_bytes=16 << 20),
        cost_estimate=NO_COST,
    )(t, *ins)


def part(t, other, size, start=0, width=None):
    return pl.ds(pl.multiple_of(t[2 * ROWS + other] * size + start, 128), width or size)


def block_rows(t, s):
    return pl.ds(pl.multiple_of(t[s] * BLOCK, BLOCK), BLOCK)


def head_rows_kernel(t, own, other, q, k, v, x, out):
    at = 0
    for weight in (q, k, v):
        width = weight.shape[1] // 2
        cols = slice(at, at + width)
        out[:, cols] = dot(own[...], weight[:, part(t, 0, width)], NN) + dot(
            other[...], x[:, cols], NN
        )
        at += width


def head_rows(own, other, weights, x, t):
    return product(
        head_rows_kernel, t, (own, other, *weights, x), [((own.shape[0], x.shape[1]), F32)]
    )[0]


def out_rows_kernel(s, t, own, other, weight, out):
    rows = slice(s * BLOCK, (s + 1) * BLOCK)
    half = weight.shape[0] // 2
    total = dot(own[rows, :], weight[part(t, 0, half), :], NN)
    total += dot(other[rows, :], weight[part(t, 1, half), :], NN)
    out[...] = total.astype(out.dtype)


def out_rows(own, other, weight, s, kind, t):
    return product(
        functools.partial(out_rows_kernel, s), t, (own, other, weight),
        [((BLOCK, weight.shape[1]), kind)],
    )[0]


def g_mixed_kernel(t, own, other, weight, x, out):
    half = x.shape[0]
    for s in range(ROWS):
        rows = block_rows(t, s)
        total = dot(own[rows, :], weight[part(t, 0, half), :], NT)
        out[s] = total + dot(other[rows, :], x[...], NT)


def g_mixed_rows(own, other, weight, x, t):
    return product(
        g_mixed_kernel, t, (own, other, weight, x), [((ROWS, BLOCK, x.shape[0]), F32)]
    )[0]


FF_BLOCK = 256


def mlp_kernel(s, t, own, other, gate_weight, up_weight, gate_x, up_x, g_mixed, out):
    ff = gate_x.shape[1]
    for start in range(0, ff, FF_BLOCK):
        cols = slice(start, start + FF_BLOCK)
        mine = part(t, 0, ff, start, FF_BLOCK)
        gate = dot(own[...], gate_weight[:, mine], NN) + dot(other[...], gate_x[:, cols], NN)
        upper = dot(own[...], up_weight[:, mine], NN) + dot(other[...], up_x[:, cols], NN)
        sigma = 1.0 / (1.0 + jnp.exp(-gate))
        activ = gate * sigma
        grad = g_mixed[s, :, cols]
        out[0, :, cols] = (activ * upper).astype(BF16)
        out[1, :, cols] = (grad * upper * sigma * (1.0 + gate * (1.0 - sigma))).astype(BF16)
        out[2, :, cols] = (grad * activ).astype(BF16)


def mlp(own, other, gate_weight, up_weight, gate_x, up_x, g_mixed, s, t):
    return product(
        functools.partial(mlp_kernel, s), t,
        (own, other, gate_weight, up_weight, gate_x, up_x, g_mixed),
        [((3, own.shape[0], gate_x.shape[1]), BF16)],
    )[0]


def mlp_back_kernel(t, own, other, gate_weight, up_weight, out):
    ff = own.shape[2]
    mine, theirs = part(t, 0, ff), part(t, 1, ff)
    for start in range(0, out.shape[1], 256):
        rows = slice(start, start + 256)
        total = dot(own[1], gate_weight[rows, mine], NT) + dot(own[2], up_weight[rows, mine], NT)
        total += dot(other[1], gate_weight[rows, theirs], NT)
        total += dot(other[2], up_weight[rows, theirs], NT)
        out[:, rows] = total.astype(out.dtype)


def mlp_back(own, other, gate_weight, up_weight, kind, t):
    return product(
        mlp_back_kernel, t, (own, other, gate_weight, up_weight),
        [((own.shape[1], gate_weight.shape[0]), kind)],
    )[0]


def down_rows_kernel(t, weight, *refs):
    out = refs[-1]
    half = weight.shape[0] // 2
    for s in range(ROWS):
        total = dot(refs[2 * s][0], weight[part(t, 0, half), :], NN)
        total += dot(refs[2 * s + 1][0], weight[part(t, 1, half), :], NN)
        out[block_rows(t, s), :] = total.astype(BF16)


def down_rows(packs, weight, t):
    return product(
        down_rows_kernel, t, (weight, *[p for pair in packs for p in pair]),
        [((ROWS * BLOCK, weight.shape[1]), BF16)],
    )[0]


def g_heads_kernel(t, x, weight, own, sent):
    half = weight.shape[0] // 2
    own[...] = dot(x[...], weight[part(t, 0, half), :], NT)
    sent[...] = dot(x[...], weight[part(t, 1, half), :], NT).astype(BF16)


def g_heads(x, weight, t):
    shape = (x.shape[0], weight.shape[0] // 2)
    return product(g_heads_kernel, t, (x, weight), [(shape, F32), (shape, BF16)])


def head_back_kernel(s, t, own, other, q, k, v, out):
    rows = slice(s * BLOCK, (s + 1) * BLOCK)
    total = 0.0
    for which, grad in enumerate((own, other)):
        at = 0
        for weight in (q, k, v):
            width = weight.shape[1] // 2
            total += dot(grad[rows, at : at + width], weight[:, part(t, which, width)], NT)
            at += width
    out[...] = total.astype(out.dtype)


def head_back(own, other, weights, s, kind, t):
    return product(
        functools.partial(head_back_kernel, s), t, (own, other, *weights),
        [((BLOCK, weights[0].shape[0]), kind)],
    )[0]


def down_grads_kernel(t, *refs):
    packs, cot, outs = refs[: 2 * ROWS], refs[2 * ROWS], refs[2 * ROWS + 1 :]
    for which, out in enumerate(outs):
        for start in range(0, out.shape[0], FF_BLOCK):
            cols = slice(start, start + FF_BLOCK)
            total = 0.0
            for s in range(ROWS):
                total += dot(packs[2 * s + which][0, :, cols], cot[block_rows(t, s), :], TN)
            out[cols, :] = total.astype(BF16)


def down_grads(packs, cot, t):
    shape = (packs[0][0].shape[2], cot.shape[1])
    return product(
        down_grads_kernel, t, (*[p for pair in packs for p in pair], cot), [(shape, BF16)] * 2
    )


def gu_grads_kernel(t, *refs):
    packs, rows, outs = refs[: 2 * ROWS], refs[2 * ROWS : 3 * ROWS], refs[3 * ROWS :]
    ff = packs[0].shape[2]
    for start in range(0, rows[0].shape[1], 256):
        cols = slice(start, start + 256)
        for which, out in enumerate(outs):
            for part_of in range(2):
                total = 0.0
                for s in range(ROWS):
                    total += dot(rows[s][:, cols], packs[2 * s + which][part_of + 1], TN)
                out[cols, part_of * ff : (part_of + 1) * ff] = total.astype(BF16)


def gu_grads(packs, n2, t):
    shape = (n2[0].shape[1], 2 * packs[0][0].shape[2])
    return product(
        gu_grads_kernel, t, (*[p for pair in packs for p in pair], *n2), [(shape, BF16)] * 2
    )


def out_grads_kernel(t, own, other, *refs):
    for att, out in ((own, refs[-2]), (other, refs[-1])):
        total = 0.0
        for s in range(ROWS):
            total += dot(att[s * BLOCK : (s + 1) * BLOCK, :], refs[s][...], TN)
        out[...] = total.astype(BF16)


def out_grads(own, other, dmid, t):
    shape = (own.shape[1], dmid[0].shape[1])
    return product(out_grads_kernel, t, (own, other, *dmid), [(shape, BF16)] * 2)


def head_grads_kernel(t, own, other, *refs):
    for grad, out in ((own, refs[-2]), (other, refs[-1])):
        for start in range(0, out.shape[0], 256):
            cols = slice(start, start + 256)
            total = 0.0
            for s in range(ROWS):
                total += dot(refs[s][:, cols], grad[s * BLOCK : (s + 1) * BLOCK, :], TN)
            out[cols, :] = total.astype(BF16)


def head_grads(own, other, n1, t):
    shape = (n1[0].shape[1], own.shape[1])
    return product(head_grads_kernel, t, (own, other, *n1), [(shape, BF16)] * 2)


def norm_stats(x):
    part = jnp.sum(x * x, axis=1)
    factor = lax.rsqrt((part + swap(part)) / MODEL_WIDTH + EPS)
    return x * factor[:, None], factor


def norm_backward(grad, unit, factor, gain):
    scaled = grad * gain
    part = jnp.sum(scaled * unit, axis=1)
    inner = (part + swap(part)) / MODEL_WIDTH
    return (factor[:, None] * (scaled - unit * inner[:, None]), jnp.sum(grad * unit, axis=0))


def cat(items, axis):
    return jnp.concatenate(items, axis)


def on_device(
    hidden,
    norm_before,
    query_weight,
    key_matrix,
    value_matrix,
    query_gain,
    key_gain,
    output_weight,
    norm_after,
    gate_weight,
    up_weight,
    down_weight,
    cotangent,
):
    dp = lax.axis_size("dp")
    k, core, me = lax.axis_index("row"), lax.axis_index("col"), lax.axis_index("dp")
    t = jnp.stack([k ^ i for i in range(ROWS)] * 2 + [core, 1 - core]).astype(jnp.int32)
    groups = query_weight.shape[1] // (2 * HEAD_SIZE)
    token = [hidden]

    def step(function, *args):
        flat, tree = jax.tree.flatten(args)
        flat = lax.optimization_barrier((*flat, token[0]))[:-1]
        out = function(*jax.tree.unflatten(tree, flat))
        token[0] = jax.tree.leaves(out)[0]
        return out

    def now(x):
        return after(x, token[0])

    def gather(x, work, between=lambda: None):
        two, one = row_swap(x, 2), row_swap(x, 1)
        first = swap(x)
        token[0] = x
        done = [work(0, x, first)]
        between()
        two = now(two)
        three = row_swap(two, 1)
        second = swap(two)
        token[0] = two
        one = now(one)
        done.append(work(1, one, swap(one)))
        done.append(work(2, two, second))
        three = now(three)
        done.append(work(3, three, swap(three)))
        return [x, one, two, three], done

    def scatter(term, between=lambda: None):
        part_three = term(3, BF16)
        got_three = row_swap(part_three, 1)
        part_one = term(1, BF16)
        part_two = term(2, F32)
        got_three = now(got_three)
        sent = (part_two + got_three.astype(F32)).astype(BF16)
        token[0] = sent
        got_two = row_swap(sent, 2)
        got_one = row_swap(after(part_one, got_three), 1)
        own = term(0, F32)
        between()
        got_one, got_two = now(got_one), now(got_two)
        return own + got_one.astype(F32) + got_two.astype(F32)

    resid = hidden.astype(F32)
    unit_one, factor_one = norm_stats(resid)
    sent_one = (unit_one * norm_before).astype(BF16)

    def for_other(weight, axis):
        half = weight.shape[axis] // 2
        return lax.dynamic_slice_in_dim(after(weight, sent_one), (1 - core) * half, half, axis)

    heads = (query_weight, key_matrix, value_matrix)
    qkv_x = swap(cat([for_other(w, 1) for w in heads], 1))
    gate_x, up_x = swap(for_other(gate_weight, 1)), swap(for_other(up_weight, 1))
    down_x = swap(for_other(down_weight, 0))
    cosine, sine = rope_tables()

    n1, raws = gather(
        sent_one, lambda s, own, other: step(head_rows, own, other, heads, qkv_x, t)
    )
    cot = lax.all_gather(now(cotangent), "row", axis=0, tiled=True)
    att, lse, query, key, value = step(
        lambda *a: attend(*a, groups), t, raws, cosine, sine, query_gain, key_gain
    )
    att_oth = swap(att)
    middle = resid + scatter(
        lambda s, kind: step(
            lambda *a: out_rows(*a[:3], s, kind, a[3]), att, att_oth, output_weight, t
        )
    )

    cot = after(cot, middle)
    cot_x = swap(cot)
    unit_two, factor_two = norm_stats(middle)
    sent_two = (unit_two * norm_after).astype(BF16)
    g_mixed = []

    def hidden_units(s, own, other):
        if s == 0:
            g_mixed.append(step(g_mixed_rows, cot, cot_x, down_weight, down_x, t))
        packed = step(
            lambda *a: mlp(*a[:7], s, a[7]),
            own, other, gate_weight, up_weight, gate_x, up_x, g_mixed[0], t,
        )
        return packed, swap(packed)

    n2, packs = gather(sent_two, hidden_units)
    grads = {}

    def ff_grads():
        grads["down"] = step(down_grads, packs, cot, t)
        grads["gu"] = step(gu_grads, packs, n2, t)

    dsecond = scatter(
        lambda s, kind: step(
            lambda *a: mlp_back(*a[:4], kind, a[4]), *packs[s], gate_weight, up_weight, t
        ),
        ff_grads,
    )
    (down_grad,) = reduce_grads(*grads["down"], me, core, dp, (down_weight.shape[1],), 0)
    ff = gate_x.shape[1]
    gate_grad, up_grad = place(*lax.psum(tuple(grads["gu"]), "dp"), core, (ff, ff))

    dmid_norm, after_part = norm_backward(dsecond, unit_two, factor_two, norm_after)
    dmiddle = cotangent.astype(F32) + dmid_norm

    def g_attended(s, own, other):
        mine, sent = step(g_heads, own, output_weight, t)
        return mine, swap(sent)

    width = down_weight.shape[1]
    last = []
    dmid, datt = gather(
        dmiddle.astype(BF16), g_attended,
        lambda: last.append(step(down_rows, packs, down_weight, t)),
    )
    last_sum = lax.psum_scatter(now(last[0]), "row", scatter_dimension=0, tiled=True)

    dqkv, gain_parts = step(
        lambda *a: attend_back(*a, groups),
        t, raws, [d for d, _ in datt], [d for _, d in datt],
        cosine, sine, query_gain, key_gain, (query, key, value, lse),
    )
    dqkv_oth = swap(dqkv)

    def head_grad():
        grads["qkv"] = step(head_grads, dqkv, dqkv_oth, n1, t)
        grads["out"] = step(out_grads, att, att_oth, dmid, t)

    dfirst = scatter(
        lambda s, kind: step(
            lambda *a: head_back(*a[:2], a[2:5], s, kind, a[5]), dqkv, dqkv_oth, *heads, t
        ),
        head_grad,
    )
    layer_out = (middle + last_sum.astype(F32)).astype(BF16)
    query_grad, key_grad, value_grad = reduce_grads(
        *grads["qkv"], me, core, dp, tuple(w.shape[1] // 2 for w in heads), 1
    )
    (output_grad,) = reduce_grads(*grads["out"], me, core, dp, (width,), 0)
    dres_norm, before_part = norm_backward(dfirst, unit_one, factor_one, norm_before)
    hidden_grad = dmiddle + dres_norm

    def everywhere(x):
        return small_sum(small_sum(x, "row", ROWS), "dp", dp)

    early = everywhere(cat([after_part, gain_parts.reshape(-1)], 0))
    before_grad = everywhere(before_part)
    after_grad = early[:width]
    gains = early[width:] + swap(early[width:])
    return (
        layer_out,
        hidden_grad,
        before_grad,
        query_grad,
        key_grad,
        value_grad,
        gains[:HEAD_SIZE],
        gains[HEAD_SIZE:],
        output_grad,
        after_grad,
        gate_grad,
        up_grad,
        down_grad,
    )


def solution(mesh):
    placed = (
        P(("dp", "row"), "col"),
        P("col"),
        P("col", "row"),
        P("col", "row"),
        P("col", "row"),
        P(),
        P(),
        P("row", "col"),
        P("col"),
        P("col", "row"),
        P("col", "row"),
        P("row", "col"),
        P(("dp", "row"), "col"),
    )
    return jax.shard_map(
        on_device,
        mesh=mesh,
        in_specs=placed,
        out_specs=(
            P(("dp", "row"), "col"),
            P(("dp", "row"), "col"),
            P("col"),
            P("col", "row"),
            P("col", "row"),
            P("col", "row"),
            P(),
            P(),
            P("row", "col"),
            P("col"),
            P("col", "row"),
            P("col", "row"),
            P("row", "col"),
        ),
        check_vma=False,
    )
```

```python
import functools
import math

import jax
import jax.numpy as jnp
from jax import lax
from jax.experimental import pallas as pl
from jax.experimental.pallas import tpu as pltpu
from jax.sharding import PartitionSpec as P

MODEL_WIDTH = 2048
HEAD_SIZE = 128
SEQUENCE_LENGTH = 1024
EPS = 1e-06
THETA = 1000000.0
ROWS = 4
BLOCK = SEQUENCE_LENGTH // ROWS
SCALE = 1.0 / math.sqrt(HEAD_SIZE)
LOG2 = SCALE * math.log2(math.e)

F32 = jnp.float32
BF16 = jnp.bfloat16
SMEM = pl.BlockSpec(memory_space=pltpu.SMEM)
VMEM = pl.BlockSpec(memory_space=pltpu.VMEM)
NO_COST = pl.CostEstimate(flops=1, transcendentals=0, bytes_accessed=1)


def swap(x):
    return lax.ppermute(x, "col", [(0, 1), (1, 0)])


def row_swap(x, mask):
    return lax.ppermute(x, "row", [(i, i ^ mask) for i in range(ROWS)])


def after(x, *others):
    return lax.optimization_barrier((x, *others))[0]


def dp_swap(x, mask, dp):
    return lax.ppermute(x, "dp", [(i, i ^ mask) for i in range(dp)])


def small_sum(x, axis, size):
    swapped = lambda mask: lax.ppermute(x, axis, [(i, i ^ mask) for i in range(size)])
    if size == 4:
        return (x + swapped(1)) + (swapped(2) + swapped(3))
    return lax.psum(x, axis)


def piece_rows(bits, me):
    first, second = bits
    rows = []
    for mask in (0, second, first, first + second):
        who = me ^ mask
        rows.append(((who // first) % 2) * 2 + (who // second) % 2)
    return rows


def assemble_kernel(spans, table_ref, *refs):
    pieces, outs = refs[:8], refs[8:]
    half, slot = pl.program_id(0), pl.program_id(1)
    for h in range(2):
        for s in range(4):

            @pl.when((half == h) & (slot == s))
            def _(piece=pieces[h * 4 + s]):
                for (lo, hi), out in zip(spans, outs):
                    out[...] = piece[:, lo:hi].astype(F32)


def assemble(pieces_a, pieces_b, me, core, widths, split):
    rows, columns = pieces_a[0].shape
    spans, at = [], 0
    for width in widths:
        spans.append((at, at + width))
        at += width
    block_rows, block_cols = [], []
    for half, bits in ((core, (1, 2)), (1 - core, (2, 1))):
        ids = piece_rows(bits, me)
        block_rows += [half * 4 + r if split == 0 else r for r in ids]
        block_cols.append(half if split == 1 else 0 * half)
    table = jnp.stack(block_rows + block_cols).astype(jnp.int32)
    full = [
        (rows * (8 if split == 0 else 4), width * (2 if split == 1 else 1)) for width in widths
    ]
    return pl.pallas_call(
        functools.partial(assemble_kernel, spans),
        out_shape=[jax.ShapeDtypeStruct(shape, F32) for shape in full],
        grid_spec=pltpu.PrefetchScalarGridSpec(
            num_scalar_prefetch=1,
            grid=(2, 4),
            in_specs=[pl.BlockSpec((rows, columns), lambda h, s, t: (0, 0))] * 8,
            out_specs=[
                pl.BlockSpec((rows, width), lambda h, s, t: (t[h * 4 + s], t[8 + h]))
                for width in widths
            ],
        ),
        compiler_params=pltpu.CompilerParams(vmem_limit_bytes=16 << 20),
        cost_estimate=NO_COST,
    )(table, *pieces_a, *pieces_b)


def place_kernel(widths, table_ref, a_ref, b_ref, *outs):
    for half, ref in enumerate((a_ref, b_ref)):

        @pl.when(pl.program_id(0) == half)
        def _(ref=ref):
            at = 0
            for width, out in zip(widths, outs):
                out[...] = ref[:, at : at + width].astype(F32)
                at += width


def place(total_a, total_b, core, widths):
    rows, columns = total_a.shape
    block = min(256, rows)
    last = rows // block - 1
    table = jnp.stack([core, 1 - core]).astype(jnp.int32)
    return pl.pallas_call(
        functools.partial(place_kernel, widths),
        out_shape=[jax.ShapeDtypeStruct((rows, 2 * width), F32) for width in widths],
        grid_spec=pltpu.PrefetchScalarGridSpec(
            num_scalar_prefetch=1,
            grid=(2, rows // block),
            in_specs=[
                pl.BlockSpec((block, columns), lambda h, r, t: (jnp.where(h == 0, r, last), 0)),
                pl.BlockSpec((block, columns), lambda h, r, t: (jnp.where(h == 1, r, 0), 0)),
            ],
            out_specs=[pl.BlockSpec((block, width), lambda h, r, t: (r, t[h])) for width in widths],
        ),
        compiler_params=pltpu.CompilerParams(vmem_limit_bytes=16 << 20),
        cost_estimate=NO_COST,
    )(table, total_a, total_b)


def whole_sums(parts, core, widths, split):
    total_a, total_b = lax.psum(tuple(cat(list(p), 0) for p in parts), "dp")
    outs, at = [], 0
    for width in widths:
        a, b = total_a[:, at : at + width], total_b[:, at : at + width]
        nat = jnp.where(core == 0, cat([a, b], split), cat([b, a], split))
        outs.append(nat.astype(F32))
        at += width
    return outs


def cat(items, axis):
    return jnp.concatenate(items, axis)


def rope_tables():
    half = HEAD_SIZE // 2
    freq = THETA ** (-(jnp.arange(half, dtype=F32) * 2.0) / HEAD_SIZE)
    angle = jnp.arange(SEQUENCE_LENGTH, dtype=F32)[:, None] * freq[None, :]
    cosine = jnp.cos(angle)
    sine = jnp.sin(angle)
    return (jnp.concatenate([cosine, cosine], 1), jnp.concatenate([-sine, sine], 1))


def dot(a, b, dims):
    return lax.dot_general(a, b, (dims, ((), ())), preferred_element_type=F32)


NN = ((1,), (0,))
NT = ((1,), (1,))
TN = ((0,), (0,))


def unit_rows(x):
    factor = lax.rsqrt(jnp.mean(x * x, axis=1, keepdims=True) + EPS)
    return x * factor, factor


def raw_scores(query, key, block):
    scores = dot(query, key, NT)
    row = lax.broadcasted_iota(jnp.int32, scores.shape, 0) + block * BLOCK
    column = lax.broadcasted_iota(jnp.int32, scores.shape, 1)
    return jnp.where(row >= column, scores, -1e30)


def attend_kernel(groups, table, *refs):
    raws = refs[:ROWS]
    cosine, sine, q_gain, k_gain = refs[ROWS : ROWS + 4]
    att, lse, query, key, value = refs[ROWS + 4 :]
    width = HEAD_SIZE
    for s in range(ROWS):
        rows = pl.ds(pl.multiple_of(table[s] * BLOCK, BLOCK), BLOCK)
        cos, sin = cosine[rows, :], sine[rows, :]
        for h in range(groups + 1):
            unit, _ = unit_rows(raws[s][:, h * width : (h + 1) * width])
            gained = unit * (q_gain[...] if h < groups else k_gain[...])
            turned = gained * cos + pltpu.roll(gained, width // 2, 1) * sin
            if h < groups:
                query[rows, h * width : (h + 1) * width] = turned.astype(BF16)
            else:
                key[rows, :] = turned.astype(BF16)
        value[rows, :] = raws[s][:, (groups + 1) * width :].astype(BF16)
    for i in range(ROWS):
        span = (i + 1) * BLOCK
        slot = table[ROWS + i]
        rows = pl.ds(pl.multiple_of(slot * BLOCK, BLOCK), BLOCK)
        for h in range(groups):
            cols = slice(h * width, (h + 1) * width)
            scores = raw_scores(query[i * BLOCK : span, cols], key[:span, :], i)
            top = jnp.max(scores, axis=1, keepdims=True)
            expo = jnp.exp2((scores - top) * LOG2)
            total = jnp.sum(expo, axis=1, keepdims=True)
            prob = (expo * (1.0 / total)).astype(BF16)
            att[rows, cols] = dot(prob, value[:span, :], NN).astype(BF16)
            log = top * LOG2 + jnp.log2(total)
            lse[i * BLOCK : span, cols] = jnp.broadcast_to(log, (BLOCK, width))


def attend_back_kernel(groups, table, *refs):
    raws = refs[:ROWS]
    grads, others = refs[ROWS : 2 * ROWS], refs[2 * ROWS : 3 * ROWS]
    cosine, sine, q_gain, k_gain, query, key, value, lse = refs[3 * ROWS : 3 * ROWS + 8]
    out, gains, d_query, d_key, d_value, grad = refs[3 * ROWS + 8 :]
    width = HEAD_SIZE
    for s in range(ROWS):
        rows = pl.ds(pl.multiple_of(table[s] * BLOCK, BLOCK), BLOCK)
        grad[rows, :] = (grads[s][...] + others[s][...].astype(F32)).astype(BF16)
    d_key[...] = jnp.zeros_like(d_key)
    d_value[...] = jnp.zeros_like(d_value)
    for i in range(ROWS):
        span = (i + 1) * BLOCK
        for h in range(groups):
            cols = slice(h * width, (h + 1) * width)
            q = query[i * BLOCK : span, cols]
            g = grad[i * BLOCK : span, cols]
            scores = raw_scores(q, key[:span, :], i)
            log = lse[i * BLOCK : span, h * width : h * width + 1]
            prob = jnp.exp2(scores * LOG2 - log)
            dprob = dot(g, value[:span, :], NT)
            delta = jnp.sum(prob * dprob, axis=1, keepdims=True)
            dscore = (SCALE * prob * (dprob - delta)).astype(BF16)
            d_query[i * BLOCK : span, cols] = dot(dscore, key[:span, :], NN)
            d_key[:span, :] += dot(dscore, q, TN)
            d_value[:span, :] += dot(prob.astype(BF16), g, TN)
    gain_sums = [jnp.zeros((1, width), F32), jnp.zeros((1, width), F32)]
    for s in range(ROWS):
        rows = pl.ds(pl.multiple_of(table[s] * BLOCK, BLOCK), BLOCK)
        cos, sin = cosine[rows, :], sine[rows, :]
        for h in range(groups + 1):
            cols = slice(h * width, (h + 1) * width)
            unit, factor = unit_rows(raws[s][:, cols])
            turned = d_query[rows, cols] if h < groups else d_key[rows, :]
            back = turned * cos + pltpu.roll(turned * sin, width // 2, 1)
            scaled = back * (q_gain[...] if h < groups else k_gain[...])
            inner = jnp.mean(scaled * unit, axis=1, keepdims=True)
            which = 0 if h < groups else 1
            gain_sums[which] += jnp.sum(back * unit, axis=0, keepdims=True)
            out[s * BLOCK : (s + 1) * BLOCK, cols] = (factor * (scaled - unit * inner)).astype(BF16)
        out[s * BLOCK : (s + 1) * BLOCK, (groups + 1) * width :] = d_value[rows, :].astype(BF16)
    gains[0:1, :] = gain_sums[0]
    gains[1:2, :] = gain_sums[1]


def attend(table, raws, cosine, sine, q_gain, k_gain, groups):
    wide = (SEQUENCE_LENGTH, groups * HEAD_SIZE)
    one = (SEQUENCE_LENGTH, HEAD_SIZE)
    return pl.pallas_call(
        functools.partial(attend_kernel, groups),
        out_shape=[
            jax.ShapeDtypeStruct(wide, BF16),
            jax.ShapeDtypeStruct(wide, F32),
            jax.ShapeDtypeStruct(wide, BF16),
            jax.ShapeDtypeStruct(one, BF16),
            jax.ShapeDtypeStruct(one, BF16),
        ],
        in_specs=[SMEM] + [VMEM] * (ROWS + 4),
        out_specs=[VMEM] * 5,
        compiler_params=pltpu.CompilerParams(vmem_limit_bytes=16 << 20),
        cost_estimate=NO_COST,
    )(table, *raws, cosine, sine, q_gain[None], k_gain[None])


def attend_back(table, raws, grads, others, cosine, sine, q_gain, k_gain, saved, groups):
    query, key, value, lse = saved
    return pl.pallas_call(
        functools.partial(attend_back_kernel, groups),
        out_shape=[
            jax.ShapeDtypeStruct((SEQUENCE_LENGTH, (groups + 2) * HEAD_SIZE), BF16),
            jax.ShapeDtypeStruct((2, HEAD_SIZE), F32),
        ],
        in_specs=[SMEM] + [VMEM] * (3 * ROWS + 8),
        out_specs=[VMEM] * 2,
        scratch_shapes=[
            pltpu.VMEM((SEQUENCE_LENGTH, groups * HEAD_SIZE), F32),
            pltpu.VMEM((SEQUENCE_LENGTH, HEAD_SIZE), F32),
            pltpu.VMEM((SEQUENCE_LENGTH, HEAD_SIZE), F32),
            pltpu.VMEM((SEQUENCE_LENGTH, groups * HEAD_SIZE), BF16),
        ],
        compiler_params=pltpu.CompilerParams(vmem_limit_bytes=20 << 20),
        cost_estimate=NO_COST,
    )(table, *raws, *grads, *others, cosine, sine, q_gain[None], k_gain[None], query, key, value, lse)


def product(kernel, t, ins, outs):
    return pl.pallas_call(
        kernel,
        out_shape=[jax.ShapeDtypeStruct(shape, kind) for shape, kind in outs],
        in_specs=[SMEM] + [VMEM] * len(ins),
        out_specs=[VMEM] * len(outs),
        compiler_params=pltpu.CompilerParams(vmem_limit_bytes=16 << 20),
        cost_estimate=NO_COST,
    )(t, *ins)


def part(t, other, size, start=0, width=None):
    return pl.ds(pl.multiple_of(t[2 * ROWS + other] * size + start, 128), width or size)


def block_rows(t, s):
    return pl.ds(pl.multiple_of(t[s] * BLOCK, BLOCK), BLOCK)


def head_rows_kernel(t, own, other, q, k, v, x, out):
    at = 0
    for weight in (q, k, v):
        width = weight.shape[1] // 2
        cols = slice(at, at + width)
        out[:, cols] = dot(own[...], weight[:, part(t, 0, width)], NN) + dot(
            other[...], x[:, cols], NN
        )
        at += width


def head_rows(own, other, weights, x, t):
    return product(
        head_rows_kernel, t, (own, other, *weights, x), [((own.shape[0], x.shape[1]), F32)]
    )[0]


def out_rows_kernel(s, t, own, other, weight, out):
    rows = slice(s * BLOCK, (s + 1) * BLOCK)
    half = weight.shape[0] // 2
    total = dot(own[rows, :], weight[part(t, 0, half), :], NN)
    total += dot(other[rows, :], weight[part(t, 1, half), :], NN)
    out[...] = total.astype(out.dtype)


def out_rows(own, other, weight, s, kind, t):
    return product(
        functools.partial(out_rows_kernel, s), t, (own, other, weight),
        [((BLOCK, weight.shape[1]), kind)],
    )[0]


def g_mixed_kernel(t, own, other, weight, x, out):
    half = x.shape[0]
    for s in range(ROWS):
        rows = block_rows(t, s)
        total = dot(own[rows, :], weight[part(t, 0, half), :], NT)
        out[s] = total + dot(other[rows, :], x[...], NT)


def g_mixed_rows(own, other, weight, x, t):
    return product(
        g_mixed_kernel, t, (own, other, weight, x), [((ROWS, BLOCK, x.shape[0]), F32)]
    )[0]


FF_BLOCK = 256


def mlp_kernel(s, t, own, other, gate_weight, up_weight, gate_x, up_x, g_mixed, out):
    ff = gate_x.shape[1]
    for start in range(0, ff, FF_BLOCK):
        cols = slice(start, start + FF_BLOCK)
        mine = part(t, 0, ff, start, FF_BLOCK)
        gate = dot(own[...], gate_weight[:, mine], NN) + dot(other[...], gate_x[:, cols], NN)
        upper = dot(own[...], up_weight[:, mine], NN) + dot(other[...], up_x[:, cols], NN)
        sigma = 1.0 / (1.0 + jnp.exp(-gate))
        activ = gate * sigma
        grad = g_mixed[s, :, cols]
        out[0, :, cols] = (activ * upper).astype(BF16)
        out[1, :, cols] = (grad * upper * sigma * (1.0 + gate * (1.0 - sigma))).astype(BF16)
        out[2, :, cols] = (grad * activ).astype(BF16)


def mlp(own, other, gate_weight, up_weight, gate_x, up_x, g_mixed, s, t):
    return product(
        functools.partial(mlp_kernel, s), t,
        (own, other, gate_weight, up_weight, gate_x, up_x, g_mixed),
        [((3, own.shape[0], gate_x.shape[1]), BF16)],
    )[0]


def mlp_back_kernel(t, own, other, gate_weight, up_weight, out):
    ff = own.shape[2]
    mine, theirs = part(t, 0, ff), part(t, 1, ff)
    for start in range(0, out.shape[1], 256):
        rows = slice(start, start + 256)
        total = dot(own[1], gate_weight[rows, mine], NT) + dot(own[2], up_weight[rows, mine], NT)
        total += dot(other[1], gate_weight[rows, theirs], NT)
        total += dot(other[2], up_weight[rows, theirs], NT)
        out[:, rows] = total.astype(out.dtype)


def mlp_back(own, other, gate_weight, up_weight, kind, t):
    return product(
        mlp_back_kernel, t, (own, other, gate_weight, up_weight),
        [((own.shape[1], gate_weight.shape[0]), kind)],
    )[0]


def down_rows_kernel(t, weight, *refs):
    half = weight.shape[0] // 2
    for s in range(ROWS):
        out = refs[2 * ROWS + s]
        total = dot(refs[2 * s][0], weight[part(t, 0, half), :], NN)
        total += dot(refs[2 * s + 1][0], weight[part(t, 1, half), :], NN)
        out[...] = total.astype(out.dtype)


def down_rows(packs, weight, t):
    shape = (BLOCK, weight.shape[1])
    return product(
        down_rows_kernel, t, (weight, *[p for pair in packs for p in pair]),
        [(shape, kind) for kind in (F32, BF16, F32, BF16)],
    )


def g_heads_kernel(t, x, weight, own, sent):
    half = weight.shape[0] // 2
    own[...] = dot(x[...], weight[part(t, 0, half), :], NT)
    sent[...] = dot(x[...], weight[part(t, 1, half), :], NT).astype(BF16)


def g_heads(x, weight, t):
    shape = (x.shape[0], weight.shape[0] // 2)
    return product(g_heads_kernel, t, (x, weight), [(shape, F32), (shape, BF16)])


def head_back_kernel(s, t, own, other, q, k, v, out):
    rows = slice(s * BLOCK, (s + 1) * BLOCK)
    total = 0.0
    for which, grad in enumerate((own, other)):
        at = 0
        for weight in (q, k, v):
            width = weight.shape[1] // 2
            total += dot(grad[rows, at : at + width], weight[:, part(t, which, width)], NT)
            at += width
    out[...] = total.astype(out.dtype)


def head_back(own, other, weights, s, kind, t):
    return product(
        functools.partial(head_back_kernel, s), t, (own, other, *weights),
        [((BLOCK, weights[0].shape[0]), kind)],
    )[0]


def halves(t, which, size):
    kept = t[2 * ROWS + 2 + which]
    return kept * size, (1 - kept) * size


def down_grads_kernel(t, *refs):
    packs, cot, outs = refs[: 2 * ROWS], refs[2 * ROWS], refs[2 * ROWS + 1 :]
    half = outs[0].shape[0]
    for which in range(2):
        for out, begin in zip(outs[2 * which : 2 * which + 2], halves(t, which, half)):
            cols = pl.ds(pl.multiple_of(begin, 128), half)
            total = 0.0
            for s in range(ROWS):
                total += dot(packs[2 * s + which][0, :, cols], cot[block_rows(t, s), :], TN)
            out[...] = total.astype(BF16)


def down_grads(packs, cot, t):
    shape = (packs[0][0].shape[2] // 2, cot.shape[1])
    return product(
        down_grads_kernel, t, (*[p for pair in packs for p in pair], cot), [(shape, BF16)] * 4
    )


def gu_grads_kernel(t, *refs):
    packs, rows, outs = refs[: 2 * ROWS], refs[2 * ROWS : 3 * ROWS], refs[3 * ROWS :]
    ff = packs[0].shape[2]
    for start in range(0, rows[0].shape[1], 256):
        cols = slice(start, start + 256)
        for which, out in enumerate(outs):
            for part_of in range(2):
                total = 0.0
                for s in range(ROWS):
                    total += dot(rows[s][:, cols], packs[2 * s + which][part_of + 1], TN)
                out[cols, part_of * ff : (part_of + 1) * ff] = total.astype(BF16)


def gu_grads(packs, n2, t):
    shape = (n2[0].shape[1], 2 * packs[0][0].shape[2])
    return product(
        gu_grads_kernel, t, (*[p for pair in packs for p in pair], *n2), [(shape, BF16)] * 2
    )


def out_grads_kernel(t, own, other, *refs):
    outs = refs[ROWS:]
    half = outs[0].shape[0]
    for which, att in enumerate((own, other)):
        for out, begin in zip(outs[2 * which : 2 * which + 2], halves(t, which, half)):
            cols = pl.ds(pl.multiple_of(begin, 128), half)
            total = 0.0
            for s in range(ROWS):
                total += dot(att[s * BLOCK : (s + 1) * BLOCK, cols], refs[s][...], TN)
            out[...] = total.astype(BF16)


def out_grads(own, other, dmid, t):
    shape = (own.shape[1] // 2, dmid[0].shape[1])
    return product(out_grads_kernel, t, (own, other, *dmid), [(shape, BF16)] * 4)


def head_grads_kernel(t, own, other, *refs):
    outs = refs[ROWS:]
    half = outs[0].shape[0]
    for which, grad in enumerate((own, other)):
        for out, begin in zip(outs[2 * which : 2 * which + 2], halves(t, which, half)):
            for start in range(0, half, 256):
                cols = pl.ds(pl.multiple_of(begin + start, 128), 256)
                total = 0.0
                for s in range(ROWS):
                    total += dot(refs[s][:, cols], grad[s * BLOCK : (s + 1) * BLOCK, :], TN)
                out[start : start + 256, :] = total.astype(BF16)


def head_grads(own, other, n1, t):
    shape = (n1[0].shape[1] // 2, own.shape[1])
    return product(head_grads_kernel, t, (own, other, *n1), [(shape, BF16)] * 4)


def norm_stats(x):
    part = jnp.sum(x * x, axis=1)
    factor = lax.rsqrt((part + swap(part)) / MODEL_WIDTH + EPS)
    return x * factor[:, None], factor


def norm_backward(grad, unit, factor, gain):
    scaled = grad * gain
    part = jnp.sum(scaled * unit, axis=1)
    inner = (part + swap(part)) / MODEL_WIDTH
    return (factor[:, None] * (scaled - unit * inner[:, None]), jnp.sum(grad * unit, axis=0))


def on_device(
    hidden,
    norm_before,
    query_weight,
    key_matrix,
    value_matrix,
    query_gain,
    key_gain,
    output_weight,
    norm_after,
    gate_weight,
    up_weight,
    down_weight,
    cotangent,
):
    dp = lax.axis_size("dp")
    k, core, me = lax.axis_index("row"), lax.axis_index("col"), lax.axis_index("dp")
    keeps = [me % 2, (me // 2) % 2] if dp == 4 else [0 * me, 0 * me]
    t = jnp.stack([k ^ i for i in range(ROWS)] * 2 + [core, 1 - core] + keeps).astype(jnp.int32)
    groups = query_weight.shape[1] // (2 * HEAD_SIZE)
    token = [hidden]

    def step(function, *args):
        flat, tree = jax.tree.flatten(args)
        flat = lax.optimization_barrier((*flat, token[0]))[:-1]
        out = function(*jax.tree.unflatten(tree, flat))
        token[0] = jax.tree.leaves(out)[0]
        return out

    def now(x):
        return after(x, token[0])

    def gather(x, work, between=lambda: None):
        two, one = row_swap(x, 2), row_swap(x, 1)
        first = swap(x)
        token[0] = x
        done = [work(0, x, first)]
        between()
        two = now(two)
        three = row_swap(two, 1)
        second = swap(two)
        token[0] = two
        one = now(one)
        done.append(work(1, one, swap(one)))
        done.append(work(2, two, second))
        three = now(three)
        done.append(work(3, three, swap(three)))
        return [x, one, two, three], done

    def halving(kept, sent, bits):
        first, second = bits
        keep = (me // second) % 2
        got = dp_swap(sent, first, dp)
        yield
        kept, got = now(kept), now(got)
        size = kept.shape[0] // 2

        def add(v):
            a = lax.dynamic_slice_in_dim(kept, v * size, size, 0)
            b = lax.dynamic_slice_in_dim(got, v * size, size, 0)
            return (a.astype(F32) + b.astype(F32)).astype(BF16)

        sent, mine = add(1 - keep), add(keep)
        token[0] = sent
        got = dp_swap(sent, second, dp)
        yield
        mine = (mine.astype(F32) + now(got).astype(F32)).astype(BF16)
        token[0] = mine
        near = dp_swap(mine, second, dp)
        far = dp_swap(mine, first, dp)
        yield
        near = now(near)
        token[0] = near
        return [mine, near, far, dp_swap(near, first, dp)]

    class Sum:
        def __init__(self, parts, widths, split):
            self.args = (core, widths, split)
            self.halves = (parts[:2], parts[2:])
            if dp == 4:
                self.runs = [halving(*parts[:2], (1, 2)), halving(*parts[2:], (2, 1))]
                self.done = [None, None]
                self.step()
            else:
                self.outs = whole_sums(self.halves, *self.args)

        def step(self):
            if dp != 4:
                return
            for i, run in enumerate(self.runs):
                try:
                    next(run)
                except StopIteration as stop:
                    self.done[i] = stop.value

        def result(self):
            if dp != 4:
                return self.outs
            return assemble(*self.done, me, *self.args)

    def spread(parts):
        got_three = row_swap(parts[3], 1)
        yield
        got_three = now(got_three)
        sent = (parts[2] + got_three.astype(F32)).astype(BF16)
        token[0] = sent
        got_two = row_swap(sent, 2)
        got_one = row_swap(after(parts[1], got_three), 1)
        yield
        return parts[0] + now(got_one).astype(F32) + now(got_two).astype(F32)

    def scatter(term, between=lambda: None):
        part_three = term(3, BF16)
        got_three = row_swap(part_three, 1)
        part_one = term(1, BF16)
        part_two = term(2, F32)
        got_three = now(got_three)
        sent = (part_two + got_three.astype(F32)).astype(BF16)
        token[0] = sent
        got_two = row_swap(sent, 2)
        got_one = row_swap(after(part_one, got_three), 1)
        own = term(0, F32)
        between()
        got_one, got_two = now(got_one), now(got_two)
        return own + got_one.astype(F32) + got_two.astype(F32)

    resid = hidden.astype(F32)
    unit_one, factor_one = norm_stats(resid)
    sent_one = (unit_one * norm_before).astype(BF16)

    def for_other(weight, axis):
        half = weight.shape[axis] // 2
        return lax.dynamic_slice_in_dim(after(weight, sent_one), (1 - core) * half, half, axis)

    heads = (query_weight, key_matrix, value_matrix)
    qkv_x = swap(cat([for_other(w, 1) for w in heads], 1))
    gate_x, up_x = swap(for_other(gate_weight, 1)), swap(for_other(up_weight, 1))
    down_x = swap(for_other(down_weight, 0))
    cosine, sine = rope_tables()

    n1, raws = gather(
        sent_one, lambda s, own, other: step(head_rows, own, other, heads, qkv_x, t)
    )
    cot = lax.all_gather(cotangent, "row", axis=0, tiled=True)
    att, lse, query, key, value = step(
        lambda *a: attend(*a, groups), t, raws, cosine, sine, query_gain, key_gain
    )
    att_oth = swap(att)
    middle = resid + scatter(
        lambda s, kind: step(
            lambda *a: out_rows(*a[:3], s, kind, a[3]), att, att_oth, output_weight, t
        )
    )

    cot = after(cot, middle)
    cot_x = swap(cot)
    unit_two, factor_two = norm_stats(middle)
    sent_two = (unit_two * norm_after).astype(BF16)
    g_mixed = []

    def hidden_units(s, own, other):
        if s == 0:
            g_mixed.append(step(g_mixed_rows, cot, cot_x, down_weight, down_x, t))
        packed = step(
            lambda *a: mlp(*a[:7], s, a[7]),
            own, other, gate_weight, up_weight, gate_x, up_x, g_mixed[0], t,
        )
        return packed, swap(packed)

    n2, packs = gather(sent_two, hidden_units)
    width = down_weight.shape[1]
    down_sum = Sum(step(down_grads, packs, cot, t), (width,), 0)
    gu_sums = lax.psum(tuple(step(gu_grads, packs, n2, t)), "dp")
    dsecond = scatter(
        lambda s, kind: step(
            lambda *a: mlp_back(*a[:4], kind, a[4]), *packs[s], gate_weight, up_weight, t
        ),
        down_sum.step,
    )
    dmid_norm, after_part = norm_backward(dsecond, unit_two, factor_two, norm_after)
    dmiddle = cotangent.astype(F32) + dmid_norm

    def g_attended(s, own, other):
        mine, sent = step(g_heads, own, output_weight, t)
        return mine, swap(sent)

    last = []

    def feed_forward_rows():
        last.extend(step(down_rows, packs, down_weight, t))
        down_sum.step()

    dmid, datt = gather(dmiddle.astype(BF16), g_attended, feed_forward_rows)
    last_run = spread(last)
    next(last_run)
    down_sum.step()

    out_sum = Sum(step(out_grads, att, att_oth, dmid, t), (width,), 0)
    dqkv, gain_parts = step(
        lambda *a: attend_back(*a, groups),
        t, raws, [d for d, _ in datt], [d for _, d in datt],
        cosine, sine, query_gain, key_gain, (query, key, value, lse),
    )
    next(last_run)
    dqkv_oth = swap(dqkv)
    out_sum.step()
    sums = []

    def head_grad():
        sums.append(
            Sum(
                step(head_grads, dqkv, dqkv_oth, n1, t),
                tuple(w.shape[1] // 2 for w in heads), 1,
            )
        )
        out_sum.step()

    dfirst = scatter(
        lambda s, kind: step(
            lambda *a: head_back(*a[:2], a[2:5], s, kind, a[5]), dqkv, dqkv_oth, *heads, t
        ),
        head_grad,
    )
    (qkv_sum,) = sums
    qkv_sum.step()
    out_sum.step()
    try:
        next(last_run)
    except StopIteration as stop:
        layer_out = (middle + stop.value).astype(BF16)
    qkv_sum.step()
    (down_grad,) = down_sum.result()
    qkv_sum.step()
    (output_grad,) = out_sum.result()
    ff = gate_x.shape[1]
    gate_grad, up_grad = place(*gu_sums, core, (ff, ff))
    query_grad, key_grad, value_grad = qkv_sum.result()
    dres_norm, before_part = norm_backward(dfirst, unit_one, factor_one, norm_before)
    hidden_grad = dmiddle + dres_norm

    def everywhere(x):
        return small_sum(small_sum(x, "row", ROWS), "dp", dp)

    early = everywhere(cat([after_part, gain_parts.reshape(-1)], 0))
    before_grad = everywhere(before_part)
    after_grad = early[:width]
    gains = early[width:] + swap(early[width:])
    return (
        layer_out,
        hidden_grad,
        before_grad,
        query_grad,
        key_grad,
        value_grad,
        gains[:HEAD_SIZE],
        gains[HEAD_SIZE:],
        output_grad,
        after_grad,
        gate_grad,
        up_grad,
        down_grad,
    )


def solution(mesh):
    placed = (
        P(("dp", "row"), "col"),
        P("col"),
        P("col", "row"),
        P("col", "row"),
        P("col", "row"),
        P(),
        P(),
        P("row", "col"),
        P("col"),
        P("col", "row"),
        P("col", "row"),
        P("row", "col"),
        P(("dp", "row"), "col"),
    )
    return jax.shard_map(
        on_device,
        mesh=mesh,
        in_specs=placed,
        out_specs=(
            P(("dp", "row"), "col"),
            P(("dp", "row"), "col"),
            P("col"),
            P("col", "row"),
            P("col", "row"),
            P("col", "row"),
            P(),
            P(),
            P("row", "col"),
            P("col"),
            P("col", "row"),
            P("col", "row"),
            P("row", "col"),
        ),
        check_vma=False,
    )
```

```python
import functools
import math

import jax
import jax.numpy as jnp
from jax import lax
from jax.experimental import pallas as pl
from jax.experimental.pallas import tpu as pltpu
from jax.sharding import PartitionSpec as P

MODEL_WIDTH = 2048
HEAD_SIZE = 128
SEQUENCE_LENGTH = 1024
EPS = 1e-06
THETA = 1000000.0
ROWS = 4
BLOCK = SEQUENCE_LENGTH // ROWS
SCALE = 1.0 / math.sqrt(HEAD_SIZE)
LOG2 = SCALE * math.log2(math.e)

F32 = jnp.float32
BF16 = jnp.bfloat16
SMEM = pl.BlockSpec(memory_space=pltpu.SMEM)
VMEM = pl.BlockSpec(memory_space=pltpu.VMEM)
NO_COST = pl.CostEstimate(flops=1, transcendentals=0, bytes_accessed=1)


def swap(x):
    return lax.ppermute(x, "col", [(0, 1), (1, 0)])


def row_swap(x, mask):
    return lax.ppermute(x, "row", [(i, i ^ mask) for i in range(ROWS)])


def after(x, *others):
    return lax.optimization_barrier((x, *others))[0]


def dp_swap(x, mask, dp):
    return lax.ppermute(x, "dp", [(i, i ^ mask) for i in range(dp)])


def small_sum(x, axis, size):
    if size != 4:
        return lax.psum(x, axis)
    for mask in (1, 2):
        x = x + lax.ppermute(x, axis, [(i, i ^ mask) for i in range(size)])
    return x


def piece_rows(bits, me):
    first, second = bits
    rows = []
    for mask in (0, second, first, first + second):
        who = me ^ mask
        rows.append(((who // first) % 2) * 2 + (who // second) % 2)
    return rows


def assemble_kernel(tall, spans, table_ref, *refs):
    pieces, outs = refs[:6], refs[6:]
    rows, columns = pieces[0].shape
    half, slot = pl.program_id(0), pl.program_id(1)
    for h in range(2):
        for s in range(4):

            @pl.when((half == h) & (slot == s))
            def _(piece=pieces[h * 3 + min(s, 2)], base=rows if s == 3 else 0):
                for (lo, hi), out in zip(spans, outs):
                    out[...] = piece[base : base + tall, lo:hi].astype(F32)
                short = outs[-1].shape[0]
                for c in range(outs[-1].shape[1] // columns):
                    start = base + tall + c * short
                    outs[-1][:, c * columns : (c + 1) * columns] = piece[
                        start : start + short, :
                    ].astype(F32)


def assemble(pieces_a, pieces_b, ids_a, ids_b, core, widths, tall, wide):
    rows, columns = pieces_a[0].shape
    spans, at = [], 0
    for width in widths:
        spans.append((at, at + width))
        at += width
    short = (rows - tall) * columns // wide
    table = jnp.stack([*ids_a, *ids_b, core, 1 - core]).astype(jnp.int32)
    return pl.pallas_call(
        functools.partial(assemble_kernel, tall, spans),
        out_shape=[jax.ShapeDtypeStruct((tall * 4, width * 2), F32) for width in widths]
        + [jax.ShapeDtypeStruct((short * 8, wide), F32)],
        grid_spec=pltpu.PrefetchScalarGridSpec(
            num_scalar_prefetch=1,
            grid=(2, 4),
            in_specs=[pl.BlockSpec(p.shape, lambda h, s, t: (0, 0)) for p in (*pieces_a, *pieces_b)],
            out_specs=[
                pl.BlockSpec((tall, width), lambda h, s, t: (t[h * 4 + s], t[8 + h]))
                for width in widths
            ]
            + [pl.BlockSpec((short, wide), lambda h, s, t: (t[8 + h] * 4 + t[h * 4 + s], 0))],
        ),
        compiler_params=pltpu.CompilerParams(vmem_limit_bytes=16 << 20),
        cost_estimate=NO_COST,
    )(table, *pieces_a, *pieces_b)


def assemble_ff_kernel(table_ref, *refs):
    pieces, (gate, up, down) = refs[:6], refs[6:]
    rows, columns = pieces[0].shape
    tall, ff = gate.shape
    half, slot = pl.program_id(0), pl.program_id(1)
    for h in range(2):
        for s in range(4):

            @pl.when((half == h) & (slot == s))
            def _(piece=pieces[h * 3 + min(s, 2)], base=rows if s == 3 else 0):
                for chunk in range(2 * ff // 256):
                    out, at = (gate, chunk * 256) if chunk * 256 < ff else (up, chunk * 256 - ff)
                    block, col = divmod(chunk * 256, columns)
                    start = base + block * tall
                    out[:, at : at + 256] = piece[start : start + tall, col : col + 256].astype(F32)
                start, short = base + 2 * ff // columns * tall, ff * down.shape[1] // columns
                for c in range(2):
                    down[c * short : (c + 1) * short, :] = piece[
                        start : start + short, c * down.shape[1] : (c + 1) * down.shape[1]
                    ].astype(F32)


def assemble_ff(pieces_a, pieces_b, ids_a, ids_b, core, width, ff):
    table = jnp.stack([*ids_a, *ids_b, core, 1 - core]).astype(jnp.int32)
    quarter = width // 4
    return pl.pallas_call(
        assemble_ff_kernel,
        out_shape=[jax.ShapeDtypeStruct((width, 2 * ff), F32)] * 2
        + [jax.ShapeDtypeStruct((2 * ff, width), F32)],
        grid_spec=pltpu.PrefetchScalarGridSpec(
            num_scalar_prefetch=1,
            grid=(2, 4),
            in_specs=[pl.BlockSpec(p.shape, lambda h, s, t: (0, 0)) for p in (*pieces_a, *pieces_b)],
            out_specs=[pl.BlockSpec((quarter, ff), lambda h, s, t: (t[h * 4 + s], t[8 + h]))] * 2
            + [pl.BlockSpec((ff, quarter), lambda h, s, t: (t[8 + h], t[h * 4 + s]))],
        ),
        compiler_params=pltpu.CompilerParams(vmem_limit_bytes=32 << 20),
        cost_estimate=NO_COST,
    )(table, *pieces_a, *pieces_b)


def cat(items, axis):
    return jnp.concatenate(items, axis)


def rope_tables():
    half = HEAD_SIZE // 2
    freq = THETA ** (-(jnp.arange(half, dtype=F32) * 2.0) / HEAD_SIZE)
    angle = jnp.arange(SEQUENCE_LENGTH, dtype=F32)[:, None] * freq[None, :]
    cosine = jnp.cos(angle)
    sine = jnp.sin(angle)
    return (jnp.concatenate([cosine, cosine], 1), jnp.concatenate([-sine, sine], 1))


def dot(a, b, dims):
    return lax.dot_general(a, b, (dims, ((), ())), preferred_element_type=F32)


NN = ((1,), (0,))
NT = ((1,), (1,))
TN = ((0,), (0,))


def unit_rows(x):
    factor = lax.rsqrt(jnp.mean(x * x, axis=1, keepdims=True) + EPS)
    return x * factor, factor


def raw_scores(query, key, block):
    scores = dot(query, key, NT)
    row = lax.broadcasted_iota(jnp.int32, scores.shape, 0) + block * BLOCK
    column = lax.broadcasted_iota(jnp.int32, scores.shape, 1)
    return jnp.where(row >= column, scores, -1e30)


def attend_kernel(groups, table, *refs):
    raws = refs[:ROWS]
    cosine, sine, q_gain, k_gain = refs[ROWS : ROWS + 4]
    att, lse, query, key, value = refs[ROWS + 4 :]
    width = HEAD_SIZE
    for s in range(ROWS):
        rows = pl.ds(pl.multiple_of(table[s] * BLOCK, BLOCK), BLOCK)
        cos, sin = cosine[rows, :], sine[rows, :]
        for h in range(groups + 1):
            unit, _ = unit_rows(raws[s][:, h * width : (h + 1) * width])
            gained = unit * (q_gain[...] if h < groups else k_gain[...])
            turned = gained * cos + pltpu.roll(gained, width // 2, 1) * sin
            if h < groups:
                query[rows, h * width : (h + 1) * width] = turned.astype(BF16)
            else:
                key[rows, :] = turned.astype(BF16)
        value[rows, :] = raws[s][:, (groups + 1) * width :].astype(BF16)
    for i in range(ROWS):
        span = (i + 1) * BLOCK
        slot = table[ROWS + i]
        rows = pl.ds(pl.multiple_of(slot * BLOCK, BLOCK), BLOCK)
        for h in range(groups):
            cols = slice(h * width, (h + 1) * width)
            scores = raw_scores(query[i * BLOCK : span, cols], key[:span, :], i)
            top = jnp.max(scores, axis=1, keepdims=True)
            expo = jnp.exp2((scores - top) * LOG2)
            total = jnp.sum(expo, axis=1, keepdims=True)
            prob = (expo * (1.0 / total)).astype(BF16)
            att[rows, cols] = dot(prob, value[:span, :], NN).astype(BF16)
            log = top * LOG2 + jnp.log2(total)
            lse[i * BLOCK : span, cols] = jnp.broadcast_to(log, (BLOCK, width))


def attend_back_kernel(groups, table, *refs):
    raws = refs[:ROWS]
    grads, others = refs[ROWS : 2 * ROWS], refs[2 * ROWS : 3 * ROWS]
    cosine, sine, q_gain, k_gain, query, key, value, lse = refs[3 * ROWS : 3 * ROWS + 8]
    out, gains, d_query, d_key, d_value, grad = refs[3 * ROWS + 8 :]
    width = HEAD_SIZE
    for s in range(ROWS):
        rows = pl.ds(pl.multiple_of(table[s] * BLOCK, BLOCK), BLOCK)
        grad[rows, :] = (grads[s][...] + others[s][...].astype(F32)).astype(BF16)
    d_key[...] = jnp.zeros_like(d_key)
    d_value[...] = jnp.zeros_like(d_value)
    for i in range(ROWS):
        span = (i + 1) * BLOCK
        for h in range(groups):
            cols = slice(h * width, (h + 1) * width)
            q = query[i * BLOCK : span, cols]
            g = grad[i * BLOCK : span, cols]
            scores = raw_scores(q, key[:span, :], i)
            log = lse[i * BLOCK : span, h * width : h * width + 1]
            prob = jnp.exp2(scores * LOG2 - log)
            dprob = dot(g, value[:span, :], NT)
            delta = jnp.sum(prob * dprob, axis=1, keepdims=True)
            dscore = (SCALE * prob * (dprob - delta)).astype(BF16)
            d_query[i * BLOCK : span, cols] = dot(dscore, key[:span, :], NN)
            d_key[:span, :] += dot(dscore, q, TN)
            d_value[:span, :] += dot(prob.astype(BF16), g, TN)
    gain_sums = [jnp.zeros((1, width), F32), jnp.zeros((1, width), F32)]
    for s in range(ROWS):
        rows = pl.ds(pl.multiple_of(table[s] * BLOCK, BLOCK), BLOCK)
        cos, sin = cosine[rows, :], sine[rows, :]
        for h in range(groups + 1):
            cols = slice(h * width, (h + 1) * width)
            unit, factor = unit_rows(raws[s][:, cols])
            turned = d_query[rows, cols] if h < groups else d_key[rows, :]
            back = turned * cos + pltpu.roll(turned * sin, width // 2, 1)
            scaled = back * (q_gain[...] if h < groups else k_gain[...])
            inner = jnp.mean(scaled * unit, axis=1, keepdims=True)
            which = 0 if h < groups else 1
            gain_sums[which] += jnp.sum(back * unit, axis=0, keepdims=True)
            out[s * BLOCK : (s + 1) * BLOCK, cols] = (factor * (scaled - unit * inner)).astype(BF16)
        out[s * BLOCK : (s + 1) * BLOCK, (groups + 1) * width :] = d_value[rows, :].astype(BF16)
    gains[0:1, :] = gain_sums[0]
    gains[1:2, :] = gain_sums[1]


def attend(table, raws, cosine, sine, q_gain, k_gain, groups):
    wide = (SEQUENCE_LENGTH, groups * HEAD_SIZE)
    one = (SEQUENCE_LENGTH, HEAD_SIZE)
    return pl.pallas_call(
        functools.partial(attend_kernel, groups),
        out_shape=[
            jax.ShapeDtypeStruct(wide, BF16),
            jax.ShapeDtypeStruct(wide, F32),
            jax.ShapeDtypeStruct(wide, BF16),
            jax.ShapeDtypeStruct(one, BF16),
            jax.ShapeDtypeStruct(one, BF16),
        ],
        in_specs=[SMEM] + [VMEM] * (ROWS + 4),
        out_specs=[VMEM] * 5,
        compiler_params=pltpu.CompilerParams(vmem_limit_bytes=16 << 20),
        cost_estimate=NO_COST,
    )(table, *raws, cosine, sine, q_gain[None], k_gain[None])


def attend_back(table, raws, grads, others, cosine, sine, q_gain, k_gain, saved, groups):
    query, key, value, lse = saved
    return pl.pallas_call(
        functools.partial(attend_back_kernel, groups),
        out_shape=[
            jax.ShapeDtypeStruct((SEQUENCE_LENGTH, (groups + 2) * HEAD_SIZE), BF16),
            jax.ShapeDtypeStruct((2, HEAD_SIZE), F32),
        ],
        in_specs=[SMEM] + [VMEM] * (3 * ROWS + 8),
        out_specs=[VMEM] * 2,
        scratch_shapes=[
            pltpu.VMEM((SEQUENCE_LENGTH, groups * HEAD_SIZE), F32),
            pltpu.VMEM((SEQUENCE_LENGTH, HEAD_SIZE), F32),
            pltpu.VMEM((SEQUENCE_LENGTH, HEAD_SIZE), F32),
            pltpu.VMEM((SEQUENCE_LENGTH, groups * HEAD_SIZE), BF16),
        ],
        compiler_params=pltpu.CompilerParams(vmem_limit_bytes=20 << 20),
        cost_estimate=NO_COST,
    )(table, *raws, *grads, *others, cosine, sine, q_gain[None], k_gain[None], query, key, value, lse)


def product(kernel, t, ins, outs):
    return pl.pallas_call(
        kernel,
        out_shape=[jax.ShapeDtypeStruct(shape, kind) for shape, kind in outs],
        in_specs=[SMEM] + [VMEM] * len(ins),
        out_specs=[VMEM] * len(outs),
        compiler_params=pltpu.CompilerParams(vmem_limit_bytes=16 << 20),
        cost_estimate=NO_COST,
    )(t, *ins)


def part(t, other, size, start=0, width=None):
    return pl.ds(pl.multiple_of(t[2 * ROWS + other] * size + start, 128), width or size)


def block_rows(t, s):
    return pl.ds(pl.multiple_of(t[s] * BLOCK, BLOCK), BLOCK)


def head_rows_kernel(t, own, other, q, k, v, x, out):
    at = 0
    for weight in (q, k, v):
        width = weight.shape[1] // 2
        cols = slice(at, at + width)
        out[:, cols] = dot(own[...], weight[:, part(t, 0, width)], NN) + dot(
            other[...], x[:, cols], NN
        )
        at += width


def head_rows(own, other, weights, x, t):
    return product(
        head_rows_kernel, t, (own, other, *weights, x), [((own.shape[0], x.shape[1]), F32)]
    )[0]


def out_rows_kernel(s, t, own, other, weight, out):
    rows = slice(s * BLOCK, (s + 1) * BLOCK)
    half = weight.shape[0] // 2
    total = dot(own[rows, :], weight[part(t, 0, half), :], NN)
    total += dot(other[rows, :], weight[part(t, 1, half), :], NN)
    out[...] = total.astype(out.dtype)


def out_rows(own, other, weight, s, kind, t):
    return product(
        functools.partial(out_rows_kernel, s), t, (own, other, weight),
        [((BLOCK, weight.shape[1]), kind)],
    )[0]


def g_mixed_kernel(t, own, other, weight, x, out):
    half = x.shape[0]
    for s in range(ROWS):
        rows = block_rows(t, s)
        total = dot(own[rows, :], weight[part(t, 0, half), :], NT)
        out[s] = total + dot(other[rows, :], x[...], NT)


def g_mixed_rows(own, other, weight, x, t):
    return product(
        g_mixed_kernel, t, (own, other, weight, x), [((ROWS, BLOCK, x.shape[0]), F32)]
    )[0]


FF_BLOCK = 256


def mlp_kernel(s, t, own, other, gate_weight, up_weight, gate_x, up_x, g_mixed, out):
    ff = gate_x.shape[1]
    for start in range(0, ff, FF_BLOCK):
        cols = slice(start, start + FF_BLOCK)
        mine = part(t, 0, ff, start, FF_BLOCK)
        gate = dot(own[...], gate_weight[:, mine], NN) + dot(other[...], gate_x[:, cols], NN)
        upper = dot(own[...], up_weight[:, mine], NN) + dot(other[...], up_x[:, cols], NN)
        sigma = 1.0 / (1.0 + jnp.exp(-gate))
        activ = gate * sigma
        grad = g_mixed[s, :, cols]
        out[0, :, cols] = (activ * upper).astype(BF16)
        out[1, :, cols] = (grad * upper * sigma * (1.0 + gate * (1.0 - sigma))).astype(BF16)
        out[2, :, cols] = (grad * activ).astype(BF16)


def mlp(own, other, gate_weight, up_weight, gate_x, up_x, g_mixed, s, t):
    return product(
        functools.partial(mlp_kernel, s), t,
        (own, other, gate_weight, up_weight, gate_x, up_x, g_mixed),
        [((3, own.shape[0], gate_x.shape[1]), BF16)],
    )[0]


def mlp_back_kernel(t, own, other, gate_weight, up_weight, out):
    ff = own.shape[2]
    mine, theirs = part(t, 0, ff), part(t, 1, ff)
    for start in range(0, out.shape[1], 256):
        rows = slice(start, start + 256)
        total = dot(own[1], gate_weight[rows, mine], NT) + dot(own[2], up_weight[rows, mine], NT)
        total += dot(other[1], gate_weight[rows, theirs], NT)
        total += dot(other[2], up_weight[rows, theirs], NT)
        out[:, rows] = total.astype(out.dtype)


def mlp_back(own, other, gate_weight, up_weight, kind, t):
    return product(
        mlp_back_kernel, t, (own, other, gate_weight, up_weight),
        [((own.shape[1], gate_weight.shape[0]), kind)],
    )[0]


def down_rows_kernel(t, weight, *refs):
    half = weight.shape[0] // 2
    for s in range(ROWS):
        out = refs[2 * ROWS + s]
        total = dot(refs[2 * s][0], weight[part(t, 0, half), :], NN)
        total += dot(refs[2 * s + 1][0], weight[part(t, 1, half), :], NN)
        out[...] = total.astype(out.dtype)


def down_rows(packs, weight, t):
    shape = (BLOCK, weight.shape[1])
    return product(
        down_rows_kernel, t, (weight, *[p for pair in packs for p in pair]),
        [(shape, kind) for kind in (F32, BF16, F32, BF16)],
    )


def g_heads_kernel(t, x, weight, own, sent):
    half = weight.shape[0] // 2
    own[...] = dot(x[...], weight[part(t, 0, half), :], NT)
    sent[...] = dot(x[...], weight[part(t, 1, half), :], NT).astype(BF16)


def g_heads(x, weight, t):
    shape = (x.shape[0], weight.shape[0] // 2)
    return product(g_heads_kernel, t, (x, weight), [(shape, F32), (shape, BF16)])


def head_back_kernel(s, t, own, other, q, k, v, out):
    rows = slice(s * BLOCK, (s + 1) * BLOCK)
    total = 0.0
    for which, grad in enumerate((own, other)):
        at = 0
        for weight in (q, k, v):
            width = weight.shape[1] // 2
            total += dot(grad[rows, at : at + width], weight[:, part(t, which, width)], NT)
            at += width
    out[...] = total.astype(out.dtype)


def head_back(own, other, weights, s, kind, t):
    return product(
        functools.partial(head_back_kernel, s), t, (own, other, *weights),
        [((BLOCK, weights[0].shape[0]), kind)],
    )[0]


GRAD_COLUMNS = 512


def ff_grads_kernel(which, t, *refs):
    packs, n2, cot, outs = refs[:ROWS], refs[ROWS : 2 * ROWS], refs[2 * ROWS], refs[2 * ROWS + 1 :]
    ff = packs[0].shape[2]
    tall = cot.shape[1] // 4
    short = ff * tall // GRAD_COLUMNS
    kept = t[2 * ROWS + 2 + which]
    for out, half in zip(outs, (kept, 1 - kept)):
        for j in range(2):
            base = j * out.shape[0] // 2
            cols = pl.ds(pl.multiple_of((half * 2 + j) * tall, 128), tall)
            for part_of in range(2):
                total = 0.0
                for s in range(ROWS):
                    total += dot(n2[s][:, cols], packs[s][part_of + 1], TN)
                total = total.astype(BF16)
                for at in range(0, ff, 256):
                    block, col = divmod(part_of * ff + at, GRAD_COLUMNS)
                    start = base + block * tall
                    out[start : start + tall, col : col + 256] = total[:, at : at + 256]
            total = 0.0
            for s in range(ROWS):
                total += dot(packs[s][0], cot[block_rows(t, s), cols], TN)
            total = total.astype(BF16)
            start = base + 2 * ff // GRAD_COLUMNS * tall
            for c in range(2):
                out[start : start + short, c * tall : (c + 1) * tall] = total[
                    c * short : (c + 1) * short, :
                ]


def ff_grads(which, packs, n2, cot, t):
    rows = 3 * packs[0].shape[2] * cot.shape[1] // GRAD_COLUMNS // 2
    return product(
        functools.partial(ff_grads_kernel, which), t, (*packs, *n2, cot),
        [((rows, GRAD_COLUMNS), BF16)] * 2,
    )


def last_grads_kernel(t, att, att_other, grad, grad_other, *refs):
    dmid, n1, outs = refs[:ROWS], refs[ROWS : 2 * ROWS], refs[2 * ROWS :]
    columns = grad.shape[1]
    tall, short = n1[0].shape[1] // 4, att.shape[1] // 4
    for which, (x, y) in enumerate(((grad, att), (grad_other, att_other))):
        kept = t[2 * ROWS + 2 + which]
        for out, half in zip(outs[2 * which : 2 * which + 2], (kept, 1 - kept)):
            heads = pl.ds(pl.multiple_of(half * 2 * short, 128), 2 * short)
            total = 0.0
            for s in range(ROWS):
                total += dot(y[s * BLOCK : (s + 1) * BLOCK, heads], dmid[s][...], TN)
            total = total.astype(BF16)
            at = 0
            for j in range(2):
                cols = pl.ds(pl.multiple_of(half * 2 * tall + j * tall, 128), tall)
                upper = 0.0
                for s in range(ROWS):
                    upper += dot(n1[s][:, cols], x[s * BLOCK : (s + 1) * BLOCK, :], TN)
                out[at : at + tall, :] = upper.astype(BF16)
                at += tall
                for c in range(total.shape[1] // columns):
                    out[at : at + short, :] = total[
                        j * short : (j + 1) * short, c * columns : (c + 1) * columns
                    ]
                    at += short


def last_grads(att, att_other, grad, grad_other, dmid, n1, t):
    columns = grad.shape[1]
    rows = n1[0].shape[1] // 2 + att.shape[1] // 2 * dmid[0].shape[1] // columns
    return product(
        last_grads_kernel, t, (att, att_other, grad, grad_other, *dmid, *n1),
        [((rows, columns), BF16)] * 4,
    )


def add_halves_kernel(which, t, kept, got, away, mine):
    size = away.shape[0]
    half = t[2 * ROWS + 3 - which]
    for out, v in ((away, 1 - half), (mine, half)):
        rows = pl.ds(pl.multiple_of(v * size, 128), size)
        out[...] = (kept[rows, :].astype(F32) + got[rows, :].astype(F32)).astype(BF16)


def add_halves(kept, got, which, t):
    shape = (kept.shape[0] // 2, kept.shape[1])
    return product(
        functools.partial(add_halves_kernel, which), t, (kept, got), [(shape, BF16)] * 2
    )


def add_kernel(t, x, y, out):
    out[...] = (x[...].astype(F32) + y[...].astype(F32)).astype(BF16)


def add(x, y, t):
    return product(add_kernel, t, (x, y), [(x.shape, BF16)])[0]


def join_kernel(t, x, y, out):
    rows = x.shape[0]
    out[:rows, :] = x[...]
    out[rows:, :] = y[...]


def join(x, y, t):
    return product(join_kernel, t, (x, y), [((2 * x.shape[0], x.shape[1]), BF16)])[0]


def norm_stats(x):
    part = jnp.sum(x * x, axis=1)
    factor = lax.rsqrt((part + swap(part)) / MODEL_WIDTH + EPS)
    return x * factor[:, None], factor


def norm_backward(grad, unit, factor, gain):
    scaled = grad * gain
    part = jnp.sum(scaled * unit, axis=1)
    inner = (part + swap(part)) / MODEL_WIDTH
    return (factor[:, None] * (scaled - unit * inner[:, None]), jnp.sum(grad * unit, axis=0))


def on_device(
    hidden,
    norm_before,
    query_weight,
    key_matrix,
    value_matrix,
    query_gain,
    key_gain,
    output_weight,
    norm_after,
    gate_weight,
    up_weight,
    down_weight,
    cotangent,
):
    dp = lax.axis_size("dp")
    k, core, me = lax.axis_index("row"), lax.axis_index("col"), lax.axis_index("dp")
    keeps = [me % 2, (me // 2) % 2] if dp == 4 else [0 * me, 0 * me]
    t = jnp.stack([k ^ i for i in range(ROWS)] * 2 + [core, 1 - core] + keeps).astype(jnp.int32)
    groups = query_weight.shape[1] // (2 * HEAD_SIZE)
    token = [hidden]

    def step(function, *args):
        flat, tree = jax.tree.flatten(args)
        flat = lax.optimization_barrier((*flat, token[0]))[:-1]
        out = function(*jax.tree.unflatten(tree, flat))
        token[0] = jax.tree.leaves(out)[0]
        return out

    def now(x):
        return after(x, token[0])

    def gather(x, work, between=lambda: None, later=lambda: None, late=False, then=lambda: None):
        two = row_swap(x, 2)
        first = swap(x)
        token[0] = x
        done = [work(0, x, first)]
        between()
        one = row_swap(now(x) if late else x, 1)
        then()
        two = now(two)
        three = row_swap(two, 1)
        second = swap(two)
        token[0] = two
        one = now(one)
        done.append(work(1, one, swap(one)))
        done.append(work(2, two, second))
        later()
        three = now(three)
        done.append(work(3, three, swap(three)))
        return [x, one, two, three], done

    turns = ((1, 2), (2, 1))

    def halving(kept, sent, which):
        first, second = turns[which]
        got = dp_swap(sent, first, dp)
        yield
        sent, mine = step(lambda *a: add_halves(*a[:2], which, a[2]), kept, got, t)
        got = dp_swap(sent, second, dp)
        yield
        mine = step(add, mine, got, t)
        near = dp_swap(mine, second, dp)
        yield
        return [mine, near, dp_swap(step(join, mine, near, t), first, dp)]

    if dp == 4:
        ids = [piece_rows(bits, me) for bits in turns]
    else:
        ids = [[0 * core + i for i in range(4)]] * 2

    class Sum:
        def __init__(self):
            self.runs, self.parts, self.pieces = [], [], []

        def add(self, kept, sent):
            self.parts.append((kept, sent))
            if dp == 4:
                self.runs.append(halving(kept, sent, len(self.runs)))
                next(self.runs[-1])

        def step(self, chosen=slice(None)):
            for run in self.runs[chosen]:
                try:
                    next(run)
                except StopIteration as stop:
                    self.pieces.append(stop.value)

        def finish(self):
            if self.pieces:
                token[0] = after(*(piece[2] for piece in self.pieces))

        def result(self):
            if dp != 4:
                for kept, sent in lax.psum(tuple(self.parts), "dp"):
                    size = kept.shape[0] // 2
                    self.pieces.append((kept[:size], kept[size:], sent))
            return (*self.pieces, *ids, core)

    def spread(parts):
        got_three = row_swap(parts[3], 1)
        yield
        got_three = now(got_three)
        sent = (parts[2] + got_three.astype(F32)).astype(BF16)
        token[0] = sent
        got_two = row_swap(sent, 2)
        got_one = row_swap(after(parts[1], got_three), 1)
        yield
        return parts[0] + now(got_one).astype(F32) + now(got_two).astype(F32)

    def scatter(term, between=lambda: None):
        part_three = term(3, BF16)
        got_three = row_swap(part_three, 1)
        part_one = term(1, BF16)
        part_two = term(2, F32)
        got_three = now(got_three)
        sent = (part_two + got_three.astype(F32)).astype(BF16)
        token[0] = sent
        got_two = row_swap(sent, 2)
        got_one = row_swap(after(part_one, got_three), 1)
        own = term(0, F32)
        between()
        got_one, got_two = now(got_one), now(got_two)
        return own + got_one.astype(F32) + got_two.astype(F32)

    resid = hidden.astype(F32)
    unit_one, factor_one = norm_stats(resid)
    sent_one = (unit_one * norm_before).astype(BF16)

    def for_other(weight, axis):
        half = weight.shape[axis] // 2
        return lax.dynamic_slice_in_dim(after(weight, sent_one), (1 - core) * half, half, axis)

    heads = (query_weight, key_matrix, value_matrix)
    qkv_x = swap(cat([for_other(w, 1) for w in heads], 1))
    gate_x, up_x = swap(for_other(gate_weight, 1)), swap(for_other(up_weight, 1))
    down_x = swap(for_other(down_weight, 0))
    cosine, sine = rope_tables()

    n1, raws = gather(
        sent_one, lambda s, own, other: step(head_rows, own, other, heads, qkv_x, t)
    )
    cot = lax.all_gather(cotangent, "row", axis=0, tiled=True)
    att, lse, query, key, value = step(
        lambda *a: attend(*a, groups), t, raws, cosine, sine, query_gain, key_gain
    )
    att_oth = swap(att)
    middle = resid + scatter(
        lambda s, kind: step(
            lambda *a: out_rows(*a[:3], s, kind, a[3]), att, att_oth, output_weight, t
        )
    )

    cot = after(cot, middle)
    cot_x = swap(cot)
    unit_two, factor_two = norm_stats(middle)
    sent_two = (unit_two * norm_after).astype(BF16)
    g_mixed = []

    def hidden_units(s, own, other):
        if s == 0:
            g_mixed.append(step(g_mixed_rows, cot, cot_x, down_weight, down_x, t))
        packed = step(
            lambda *a: mlp(*a[:7], s, a[7]),
            own, other, gate_weight, up_weight, gate_x, up_x, g_mixed[0], t,
        )
        return packed, swap(packed)

    n2, packs = gather(sent_two, hidden_units)
    width = down_weight.shape[1]
    ff_sum, last_sum = Sum(), Sum()
    for which in range(2):
        ff_sum.add(
            *step(
                lambda *a: ff_grads(which, *a), [p[which] for p in packs], n2, cot, t
            )
        )
    dsecond = scatter(
        lambda s, kind: step(
            lambda *a: mlp_back(*a[:4], kind, a[4]), *packs[s], gate_weight, up_weight, t
        )
    )
    token[0] = dsecond
    ff_sum.step(slice(0, 1))
    dmid_norm, after_part = norm_backward(dsecond, unit_two, factor_two, norm_after)
    dmiddle = cotangent.astype(F32) + dmid_norm

    swapped = []

    def g_attended(s, own, other):
        if swapped:
            token[0] = after(swapped[-1], token[0])
        mine, sent = step(g_heads, own, output_weight, t)
        swapped.append(swap(sent))
        return mine, swapped[-1]

    last = []

    def second_half():
        ff_sum.step(slice(1, 2))

    def feed_forward_rows():
        last.extend(step(down_rows, packs, down_weight, t))

    dmid, datt = gather(dmiddle.astype(BF16), g_attended, second_half, ff_sum.step, True, feed_forward_rows)

    dqkv, gain_parts = step(
        lambda *a: attend_back(*a, groups),
        t, raws, [d for d, _ in datt], [d for _, d in datt],
        cosine, sine, query_gain, key_gain, (query, key, value, lse),
    )
    dqkv_oth = swap(dqkv)
    ff_sum.step()
    parts = step(last_grads, att, att_oth, dqkv, dqkv_oth, dmid, n1, t)
    last_sum.add(*parts[:2])
    last_sum.add(*parts[2:])
    dfirst = scatter(
        lambda s, kind: step(
            lambda *a: head_back(*a[:2], a[2:5], s, kind, a[5]), dqkv, dqkv_oth, *heads, t
        )
    )
    token[0] = dfirst
    ff_sum.finish()
    last_run = spread(last)
    next(last_run)
    gate_grad, up_grad, down_grad = step(
        lambda *a: assemble_ff(*a, width, gate_x.shape[1]), *ff_sum.result()
    )
    last_sum.step()
    dres_norm, before_part = norm_backward(now(dfirst), unit_one, factor_one, norm_before)
    hidden_grad = dmiddle + dres_norm
    next(last_run)
    last_sum.step()
    last_sum.step()
    try:
        next(last_run)
    except StopIteration as stop:
        layer_out = (middle + stop.value).astype(BF16)
    query_grad, key_grad, value_grad, output_grad = assemble(
        *last_sum.result(), tuple(w.shape[1] // 2 for w in heads), width // 4, width
    )
    small = cat([after_part, before_part, gain_parts.reshape(-1)], 0)
    small = small_sum(small_sum(small, "row", ROWS), "dp", dp)
    after_grad, before_grad = small[:width], small[width : 2 * width]
    gains = small[2 * width :] + swap(small[2 * width :])
    return (
        layer_out,
        hidden_grad,
        before_grad,
        query_grad,
        key_grad,
        value_grad,
        gains[:HEAD_SIZE],
        gains[HEAD_SIZE:],
        output_grad,
        after_grad,
        gate_grad,
        up_grad,
        down_grad,
    )


def solution(mesh):
    placed = (
        P(("dp", "row"), "col"),
        P("col"),
        P("col", "row"),
        P("col", "row"),
        P("col", "row"),
        P(),
        P(),
        P("row", "col"),
        P("col"),
        P("col", "row"),
        P("col", "row"),
        P("row", "col"),
        P(("dp", "row"), "col"),
    )
    return jax.shard_map(
        on_device,
        mesh=mesh,
        in_specs=placed,
        out_specs=(
            P(("dp", "row"), "col"),
            P(("dp", "row"), "col"),
            P("col"),
            P("col", "row"),
            P("col", "row"),
            P("col", "row"),
            P(),
            P(),
            P("row", "col"),
            P("col"),
            P("col", "row"),
            P("col", "row"),
            P("row", "col"),
        ),
        check_vma=False,
    )
```

```python
import functools
import math

import jax
import jax.numpy as jnp
from jax import lax
from jax.experimental import pallas as pl
from jax.experimental.pallas import tpu as pltpu
from jax.sharding import PartitionSpec as P

MODEL_WIDTH = 2048
HEAD_SIZE = 128
SEQUENCE_LENGTH = 1024
EPS = 1e-06
THETA = 1000000.0
ROWS = 4
BLOCK = SEQUENCE_LENGTH // ROWS
SCALE = 1.0 / math.sqrt(HEAD_SIZE)
LOG2 = SCALE * math.log2(math.e)

F32 = jnp.float32
BF16 = jnp.bfloat16
SMEM = pl.BlockSpec(memory_space=pltpu.SMEM)
VMEM = pl.BlockSpec(memory_space=pltpu.VMEM)
NO_COST = pl.CostEstimate(flops=1, transcendentals=0, bytes_accessed=1)


def swap(x):
    return lax.ppermute(x, "col", [(0, 1), (1, 0)])


def row_swap(x, mask):
    return lax.ppermute(x, "row", [(i, i ^ mask) for i in range(ROWS)])


def after(x, *others):
    return lax.optimization_barrier((x, *others))[0]


def dp_swap(x, mask, dp):
    return lax.ppermute(x, "dp", [(i, i ^ mask) for i in range(dp)])


def finish(run):
    try:
        while True:
            next(run)
    except StopIteration as stop:
        return stop.value


def piece_rows(bits, me):
    first, second = bits
    rows = []
    for mask in (0, second, first, first + second):
        who = me ^ mask
        rows.append(((who // first) % 2) * 2 + (who // second) % 2)
    return rows


def assemble_kernel(tall, spans, table_ref, *refs):
    pieces, outs = refs[:6], refs[6:]
    rows, columns = pieces[0].shape
    half, slot = pl.program_id(0), pl.program_id(1)
    for h in range(2):
        for s in range(4):

            @pl.when((half == h) & (slot == s))
            def _(piece=pieces[h * 3 + min(s, 2)], base=rows if s == 3 else 0):
                for (lo, hi), out in zip(spans, outs):
                    out[...] = piece[base : base + tall, lo:hi].astype(F32)
                short = outs[-1].shape[0]
                for c in range(outs[-1].shape[1] // columns):
                    start = base + tall + c * short
                    outs[-1][:, c * columns : (c + 1) * columns] = piece[
                        start : start + short, :
                    ].astype(F32)


def assemble(pieces_a, pieces_b, ids_a, ids_b, core, widths, tall, wide):
    rows, columns = pieces_a[0].shape
    spans, at = [], 0
    for width in widths:
        spans.append((at, at + width))
        at += width
    short = (rows - tall) * columns // wide
    table = jnp.stack([*ids_a, *ids_b, core, 1 - core]).astype(jnp.int32)
    return pl.pallas_call(
        functools.partial(assemble_kernel, tall, spans),
        out_shape=[jax.ShapeDtypeStruct((tall * 4, width * 2), F32) for width in widths]
        + [jax.ShapeDtypeStruct((short * 8, wide), F32)],
        grid_spec=pltpu.PrefetchScalarGridSpec(
            num_scalar_prefetch=1,
            grid=(2, 4),
            in_specs=[pl.BlockSpec(p.shape, lambda h, s, t: (0, 0)) for p in (*pieces_a, *pieces_b)],
            out_specs=[
                pl.BlockSpec((tall, width), lambda h, s, t: (t[h * 4 + s], t[8 + h]))
                for width in widths
            ]
            + [pl.BlockSpec((short, wide), lambda h, s, t: (t[8 + h] * 4 + t[h * 4 + s], 0))],
        ),
        compiler_params=pltpu.CompilerParams(vmem_limit_bytes=16 << 20),
        cost_estimate=NO_COST,
    )(table, *pieces_a, *pieces_b)


def assemble_ff_kernel(table_ref, *refs):
    pieces, (gate, up, down) = refs[:6], refs[6:]
    rows, columns = pieces[0].shape
    tall, ff = gate.shape
    half, slot = pl.program_id(0), pl.program_id(1)
    for h in range(2):
        for s in range(4):

            @pl.when((half == h) & (slot == s))
            def _(piece=pieces[h * 3 + min(s, 2)], base=rows if s == 3 else 0):
                for chunk in range(2 * ff // 256):
                    out, at = (gate, chunk * 256) if chunk * 256 < ff else (up, chunk * 256 - ff)
                    block, col = divmod(chunk * 256, columns)
                    start = base + block * tall
                    out[:, at : at + 256] = piece[start : start + tall, col : col + 256].astype(F32)
                start, short = base + 2 * ff // columns * tall, ff * down.shape[1] // columns
                for c in range(2):
                    down[c * short : (c + 1) * short, :] = piece[
                        start : start + short, c * down.shape[1] : (c + 1) * down.shape[1]
                    ].astype(F32)


def assemble_ff(pieces_a, pieces_b, ids_a, ids_b, core, width, ff):
    table = jnp.stack([*ids_a, *ids_b, core, 1 - core]).astype(jnp.int32)
    quarter = width // 4
    return pl.pallas_call(
        assemble_ff_kernel,
        out_shape=[jax.ShapeDtypeStruct((width, 2 * ff), F32)] * 2
        + [jax.ShapeDtypeStruct((2 * ff, width), F32)],
        grid_spec=pltpu.PrefetchScalarGridSpec(
            num_scalar_prefetch=1,
            grid=(2, 4),
            in_specs=[pl.BlockSpec(p.shape, lambda h, s, t: (0, 0)) for p in (*pieces_a, *pieces_b)],
            out_specs=[pl.BlockSpec((quarter, ff), lambda h, s, t: (t[h * 4 + s], t[8 + h]))] * 2
            + [pl.BlockSpec((ff, quarter), lambda h, s, t: (t[8 + h], t[h * 4 + s]))],
        ),
        compiler_params=pltpu.CompilerParams(vmem_limit_bytes=32 << 20),
        cost_estimate=NO_COST,
    )(table, *pieces_a, *pieces_b)


def cat(items, axis):
    return jnp.concatenate(items, axis)


def rope_tables():
    half = HEAD_SIZE // 2
    freq = THETA ** (-(jnp.arange(half, dtype=F32) * 2.0) / HEAD_SIZE)
    angle = jnp.arange(SEQUENCE_LENGTH, dtype=F32)[:, None] * freq[None, :]
    cosine = jnp.cos(angle)
    sine = jnp.sin(angle)
    return (jnp.concatenate([cosine, cosine], 1), jnp.concatenate([-sine, sine], 1))


def dot(a, b, dims):
    return lax.dot_general(a, b, (dims, ((), ())), preferred_element_type=F32)


NN = ((1,), (0,))
NT = ((1,), (1,))
TN = ((0,), (0,))


def unit_rows(x):
    factor = lax.rsqrt(jnp.mean(x * x, axis=1, keepdims=True) + EPS)
    return x * factor, factor


def raw_scores(query, key, block):
    scores = dot(query, key, NT)
    row = lax.broadcasted_iota(jnp.int32, scores.shape, 0) + block * BLOCK
    column = lax.broadcasted_iota(jnp.int32, scores.shape, 1)
    return jnp.where(row >= column, scores, -1e30)


def attend_kernel(groups, table, *refs):
    raws = refs[:ROWS]
    cosine, sine, q_gain, k_gain = refs[ROWS : ROWS + 4]
    att, lse, query, key, value = refs[ROWS + 4 :]
    width = HEAD_SIZE
    for s in range(ROWS):
        rows = pl.ds(pl.multiple_of(table[s] * BLOCK, BLOCK), BLOCK)
        cos, sin = cosine[rows, :], sine[rows, :]
        for h in range(groups + 1):
            unit, _ = unit_rows(raws[s][:, h * width : (h + 1) * width])
            gained = unit * (q_gain[...] if h < groups else k_gain[...])
            turned = gained * cos + pltpu.roll(gained, width // 2, 1) * sin
            if h < groups:
                query[rows, h * width : (h + 1) * width] = turned.astype(BF16)
            else:
                key[rows, :] = turned.astype(BF16)
        value[rows, :] = raws[s][:, (groups + 1) * width :].astype(BF16)
    for i in range(ROWS):
        span = (i + 1) * BLOCK
        slot = table[ROWS + i]
        rows = pl.ds(pl.multiple_of(slot * BLOCK, BLOCK), BLOCK)
        for h in range(groups):
            cols = slice(h * width, (h + 1) * width)
            scores = raw_scores(query[i * BLOCK : span, cols], key[:span, :], i)
            top = jnp.max(scores, axis=1, keepdims=True)
            expo = jnp.exp2((scores - top) * LOG2)
            total = jnp.sum(expo, axis=1, keepdims=True)
            prob = (expo * (1.0 / total)).astype(BF16)
            att[rows, cols] = dot(prob, value[:span, :], NN).astype(BF16)
            log = top * LOG2 + jnp.log2(total)
            lse[i * BLOCK : span, cols] = jnp.broadcast_to(log, (BLOCK, width))


def attend_back_kernel(groups, table, *refs):
    raws = refs[:ROWS]
    grads, others = refs[ROWS : 2 * ROWS], refs[2 * ROWS : 3 * ROWS]
    cosine, sine, q_gain, k_gain, query, key, value, lse = refs[3 * ROWS : 3 * ROWS + 8]
    out, gains, d_query, d_key, d_value, grad = refs[3 * ROWS + 8 :]
    width = HEAD_SIZE
    for s in range(ROWS):
        rows = pl.ds(pl.multiple_of(table[s] * BLOCK, BLOCK), BLOCK)
        grad[rows, :] = (grads[s][...] + others[s][...].astype(F32)).astype(BF16)
    d_key[...] = jnp.zeros_like(d_key)
    d_value[...] = jnp.zeros_like(d_value)
    for i in range(ROWS):
        span = (i + 1) * BLOCK
        for h in range(groups):
            cols = slice(h * width, (h + 1) * width)
            q = query[i * BLOCK : span, cols]
            g = grad[i * BLOCK : span, cols]
            scores = raw_scores(q, key[:span, :], i)
            log = lse[i * BLOCK : span, h * width : h * width + 1]
            prob = jnp.exp2(scores * LOG2 - log)
            dprob = dot(g, value[:span, :], NT)
            delta = jnp.sum(prob * dprob, axis=1, keepdims=True)
            dscore = (SCALE * prob * (dprob - delta)).astype(BF16)
            d_query[i * BLOCK : span, cols] = dot(dscore, key[:span, :], NN)
            d_key[:span, :] += dot(dscore, q, TN)
            d_value[:span, :] += dot(prob.astype(BF16), g, TN)
    gain_sums = [jnp.zeros((1, width), F32), jnp.zeros((1, width), F32)]
    for s in range(ROWS):
        rows = pl.ds(pl.multiple_of(table[s] * BLOCK, BLOCK), BLOCK)
        cos, sin = cosine[rows, :], sine[rows, :]
        for h in range(groups + 1):
            cols = slice(h * width, (h + 1) * width)
            unit, factor = unit_rows(raws[s][:, cols])
            turned = d_query[rows, cols] if h < groups else d_key[rows, :]
            back = turned * cos + pltpu.roll(turned * sin, width // 2, 1)
            scaled = back * (q_gain[...] if h < groups else k_gain[...])
            inner = jnp.mean(scaled * unit, axis=1, keepdims=True)
            which = 0 if h < groups else 1
            gain_sums[which] += jnp.sum(back * unit, axis=0, keepdims=True)
            out[s * BLOCK : (s + 1) * BLOCK, cols] = (factor * (scaled - unit * inner)).astype(BF16)
        out[s * BLOCK : (s + 1) * BLOCK, (groups + 1) * width :] = d_value[rows, :].astype(BF16)
    gains[0:1, :] = gain_sums[0]
    gains[1:2, :] = gain_sums[1]


def attend(table, raws, cosine, sine, q_gain, k_gain, groups):
    wide = (SEQUENCE_LENGTH, groups * HEAD_SIZE)
    one = (SEQUENCE_LENGTH, HEAD_SIZE)
    return pl.pallas_call(
        functools.partial(attend_kernel, groups),
        out_shape=[
            jax.ShapeDtypeStruct(wide, BF16),
            jax.ShapeDtypeStruct(wide, F32),
            jax.ShapeDtypeStruct(wide, BF16),
            jax.ShapeDtypeStruct(one, BF16),
            jax.ShapeDtypeStruct(one, BF16),
        ],
        in_specs=[SMEM] + [VMEM] * (ROWS + 4),
        out_specs=[VMEM] * 5,
        compiler_params=pltpu.CompilerParams(vmem_limit_bytes=16 << 20),
        cost_estimate=NO_COST,
    )(table, *raws, cosine, sine, q_gain[None], k_gain[None])


def attend_back(table, raws, grads, others, cosine, sine, q_gain, k_gain, saved, groups):
    query, key, value, lse = saved
    return pl.pallas_call(
        functools.partial(attend_back_kernel, groups),
        out_shape=[
            jax.ShapeDtypeStruct((SEQUENCE_LENGTH, (groups + 2) * HEAD_SIZE), BF16),
            jax.ShapeDtypeStruct((2, HEAD_SIZE), F32),
        ],
        in_specs=[SMEM] + [VMEM] * (3 * ROWS + 8),
        out_specs=[VMEM] * 2,
        scratch_shapes=[
            pltpu.VMEM((SEQUENCE_LENGTH, groups * HEAD_SIZE), F32),
            pltpu.VMEM((SEQUENCE_LENGTH, HEAD_SIZE), F32),
            pltpu.VMEM((SEQUENCE_LENGTH, HEAD_SIZE), F32),
            pltpu.VMEM((SEQUENCE_LENGTH, groups * HEAD_SIZE), BF16),
        ],
        compiler_params=pltpu.CompilerParams(vmem_limit_bytes=20 << 20),
        cost_estimate=NO_COST,
    )(table, *raws, *grads, *others, cosine, sine, q_gain[None], k_gain[None], query, key, value, lse)


def product(kernel, t, ins, outs):
    return pl.pallas_call(
        kernel,
        out_shape=[jax.ShapeDtypeStruct(shape, kind) for shape, kind in outs],
        in_specs=[SMEM] + [VMEM] * len(ins),
        out_specs=[VMEM] * len(outs),
        compiler_params=pltpu.CompilerParams(vmem_limit_bytes=16 << 20),
        cost_estimate=NO_COST,
    )(t, *ins)


def part(t, other, size, start=0, width=None):
    return pl.ds(pl.multiple_of(t[2 * ROWS + other] * size + start, 128), width or size)


def block_rows(t, s):
    return pl.ds(pl.multiple_of(t[s] * BLOCK, BLOCK), BLOCK)


def head_rows_kernel(t, own, other, q, k, v, x, out):
    at = 0
    for weight in (q, k, v):
        width = weight.shape[1] // 2
        cols = slice(at, at + width)
        out[:, cols] = dot(own[...], weight[:, part(t, 0, width)], NN) + dot(
            other[...], x[:, cols], NN
        )
        at += width


def head_rows(own, other, weights, x, t):
    return product(
        head_rows_kernel, t, (own, other, *weights, x), [((own.shape[0], x.shape[1]), F32)]
    )[0]


def out_rows_kernel(s, t, own, other, weight, out):
    rows = slice(s * BLOCK, (s + 1) * BLOCK)
    half = weight.shape[0] // 2
    total = dot(own[rows, :], weight[part(t, 0, half), :], NN)
    total += dot(other[rows, :], weight[part(t, 1, half), :], NN)
    out[...] = total.astype(out.dtype)


def out_rows(own, other, weight, s, kind, t):
    return product(
        functools.partial(out_rows_kernel, s), t, (own, other, weight),
        [((BLOCK, weight.shape[1]), kind)],
    )[0]


def g_mixed_kernel(t, own, other, weight, x, out):
    half = x.shape[0]
    for s in range(ROWS):
        rows = block_rows(t, s)
        total = dot(own[rows, :], weight[part(t, 0, half), :], NT)
        out[s] = total + dot(other[rows, :], x[...], NT)


def g_mixed_rows(own, other, weight, x, t):
    return product(
        g_mixed_kernel, t, (own, other, weight, x), [((ROWS, BLOCK, x.shape[0]), F32)]
    )[0]


FF_BLOCK = 256


def mlp_kernel(s, t, own, other, gate_weight, up_weight, gate_x, up_x, g_mixed, out):
    ff = gate_x.shape[1]
    for start in range(0, ff, FF_BLOCK):
        cols = slice(start, start + FF_BLOCK)
        mine = part(t, 0, ff, start, FF_BLOCK)
        gate = dot(own[...], gate_weight[:, mine], NN) + dot(other[...], gate_x[:, cols], NN)
        upper = dot(own[...], up_weight[:, mine], NN) + dot(other[...], up_x[:, cols], NN)
        sigma = 1.0 / (1.0 + jnp.exp(-gate))
        activ = gate * sigma
        grad = g_mixed[s, :, cols]
        out[0, :, cols] = (activ * upper).astype(BF16)
        out[1, :, cols] = (grad * upper * sigma * (1.0 + gate * (1.0 - sigma))).astype(BF16)
        out[2, :, cols] = (grad * activ).astype(BF16)


def mlp(own, other, gate_weight, up_weight, gate_x, up_x, g_mixed, s, t):
    return product(
        functools.partial(mlp_kernel, s), t,
        (own, other, gate_weight, up_weight, gate_x, up_x, g_mixed),
        [((3, own.shape[0], gate_x.shape[1]), BF16)],
    )[0]


def mlp_back_kernel(t, own, other, gate_weight, up_weight, out):
    ff = own.shape[2]
    mine, theirs = part(t, 0, ff), part(t, 1, ff)
    for start in range(0, out.shape[1], 256):
        rows = slice(start, start + 256)
        total = dot(own[1], gate_weight[rows, mine], NT) + dot(own[2], up_weight[rows, mine], NT)
        total += dot(other[1], gate_weight[rows, theirs], NT)
        total += dot(other[2], up_weight[rows, theirs], NT)
        out[:, rows] = total.astype(out.dtype)


def mlp_back(own, other, gate_weight, up_weight, kind, t):
    return product(
        mlp_back_kernel, t, (own, other, gate_weight, up_weight),
        [((own.shape[1], gate_weight.shape[0]), kind)],
    )[0]


def down_rows_kernel(t, weight, *refs):
    half = weight.shape[0] // 2
    for s in range(ROWS):
        out = refs[2 * ROWS + s]
        total = dot(refs[2 * s][0], weight[part(t, 0, half), :], NN)
        total += dot(refs[2 * s + 1][0], weight[part(t, 1, half), :], NN)
        out[...] = total.astype(out.dtype)


def down_rows(packs, weight, t):
    shape = (BLOCK, weight.shape[1])
    return product(
        down_rows_kernel, t, (weight, *[p for pair in packs for p in pair]),
        [(shape, kind) for kind in (F32, BF16, F32, BF16)],
    )


def g_heads_kernel(t, x, weight, own, sent):
    half = weight.shape[0] // 2
    own[...] = dot(x[...], weight[part(t, 0, half), :], NT)
    sent[...] = dot(x[...], weight[part(t, 1, half), :], NT).astype(BF16)


def g_heads(x, weight, t):
    shape = (x.shape[0], weight.shape[0] // 2)
    return product(g_heads_kernel, t, (x, weight), [(shape, F32), (shape, BF16)])


def head_back_kernel(s, t, own, other, q, k, v, out):
    rows = slice(s * BLOCK, (s + 1) * BLOCK)
    total = 0.0
    for which, grad in enumerate((own, other)):
        at = 0
        for weight in (q, k, v):
            width = weight.shape[1] // 2
            total += dot(grad[rows, at : at + width], weight[:, part(t, which, width)], NT)
            at += width
    out[...] = total.astype(out.dtype)


def head_back(own, other, weights, s, kind, t):
    return product(
        functools.partial(head_back_kernel, s), t, (own, other, *weights),
        [((BLOCK, weights[0].shape[0]), kind)],
    )[0]


GRAD_COLUMNS = 512


def ff_grads_kernel(which, stays, t, *refs):
    packs, n2, cot, out = refs[:ROWS], refs[ROWS : 2 * ROWS], refs[2 * ROWS], refs[2 * ROWS + 1]
    ff = packs[0].shape[2]
    tall = cot.shape[1] // 4
    short = ff * tall // GRAD_COLUMNS
    kept = t[2 * ROWS + 2 + which]
    half = kept if stays else 1 - kept
    for j in range(2):
        base = j * out.shape[0] // 2
        cols = pl.ds(pl.multiple_of((half * 2 + j) * tall, 128), tall)
        for part_of in range(2):
            total = 0.0
            for s in range(ROWS):
                total += dot(n2[s][:, cols], packs[s][part_of + 1], TN)
            total = total.astype(BF16)
            for at in range(0, ff, 256):
                block, col = divmod(part_of * ff + at, GRAD_COLUMNS)
                start = base + block * tall
                out[start : start + tall, col : col + 256] = total[:, at : at + 256]
        total = 0.0
        for s in range(ROWS):
            total += dot(packs[s][0], cot[block_rows(t, s), cols], TN)
        total = total.astype(BF16)
        start = base + 2 * ff // GRAD_COLUMNS * tall
        for c in range(2):
            out[start : start + short, c * tall : (c + 1) * tall] = total[
                c * short : (c + 1) * short, :
            ]


def ff_grads(which, stays, packs, n2, cot, t):
    rows = 3 * packs[0].shape[2] * cot.shape[1] // GRAD_COLUMNS // 2
    return product(
        functools.partial(ff_grads_kernel, which, stays), t, (*packs, *n2, cot),
        [((rows, GRAD_COLUMNS), BF16)],
    )[0]


def last_grads_kernel(t, att, att_other, grad, grad_other, *refs):
    dmid, n1, outs = refs[:ROWS], refs[ROWS : 2 * ROWS], refs[2 * ROWS :]
    columns = grad.shape[1]
    tall, short = n1[0].shape[1] // 4, att.shape[1] // 4
    for which, (x, y) in enumerate(((grad, att), (grad_other, att_other))):
        kept = t[2 * ROWS + 2 + which]
        for out, half in zip(outs[2 * which : 2 * which + 2], (kept, 1 - kept)):
            heads = pl.ds(pl.multiple_of(half * 2 * short, 128), 2 * short)
            total = 0.0
            for s in range(ROWS):
                total += dot(y[s * BLOCK : (s + 1) * BLOCK, heads], dmid[s][...], TN)
            total = total.astype(BF16)
            at = 0
            for j in range(2):
                cols = pl.ds(pl.multiple_of(half * 2 * tall + j * tall, 128), tall)
                upper = 0.0
                for s in range(ROWS):
                    upper += dot(n1[s][:, cols], x[s * BLOCK : (s + 1) * BLOCK, :], TN)
                out[at : at + tall, :] = upper.astype(BF16)
                at += tall
                for c in range(total.shape[1] // columns):
                    out[at : at + short, :] = total[
                        j * short : (j + 1) * short, c * columns : (c + 1) * columns
                    ]
                    at += short


def last_grads(att, att_other, grad, grad_other, dmid, n1, t):
    columns = grad.shape[1]
    rows = n1[0].shape[1] // 2 + att.shape[1] // 2 * dmid[0].shape[1] // columns
    return product(
        last_grads_kernel, t, (att, att_other, grad, grad_other, *dmid, *n1),
        [((rows, columns), BF16)] * 4,
    )


def add_halves_kernel(which, t, kept, got, away, mine):
    size = away.shape[0]
    half = t[2 * ROWS + 3 - which]
    for out, v in ((away, 1 - half), (mine, half)):
        rows = pl.ds(pl.multiple_of(v * size, 128), size)
        out[...] = (kept[rows, :].astype(F32) + got[rows, :].astype(F32)).astype(BF16)


def add_halves(kept, got, which, t):
    shape = (kept.shape[0] // 2, kept.shape[1])
    return product(
        functools.partial(add_halves_kernel, which), t, (kept, got), [(shape, BF16)] * 2
    )


def add_kernel(t, x, y, out):
    out[...] = (x[...].astype(F32) + y[...].astype(F32)).astype(BF16)


def add(x, y, t):
    return product(add_kernel, t, (x, y), [(x.shape, BF16)])[0]


def join_kernel(t, x, y, out):
    rows = x.shape[0]
    out[:rows, :] = x[...]
    out[rows:, :] = y[...]


def join(x, y, t):
    return product(join_kernel, t, (x, y), [((2 * x.shape[0], x.shape[1]), BF16)])[0]


def norm_stats(x):
    part = jnp.sum(x * x, axis=1)
    factor = lax.rsqrt((part + swap(part)) / MODEL_WIDTH + EPS)
    return x * factor[:, None], factor


def norm_backward(grad, unit, factor, gain):
    scaled = grad * gain
    part = jnp.sum(scaled * unit, axis=1)
    inner = (part + swap(part)) / MODEL_WIDTH
    return (factor[:, None] * (scaled - unit * inner[:, None]), jnp.sum(grad * unit, axis=0))


def on_device(
    hidden,
    norm_before,
    query_weight,
    key_matrix,
    value_matrix,
    query_gain,
    key_gain,
    output_weight,
    norm_after,
    gate_weight,
    up_weight,
    down_weight,
    cotangent,
):
    dp = lax.axis_size("dp")
    k, core, me = lax.axis_index("row"), lax.axis_index("col"), lax.axis_index("dp")
    keeps = [me % 2, (me // 2) % 2] if dp == 4 else [0 * me, 0 * me]
    t = jnp.stack([k ^ i for i in range(ROWS)] * 2 + [core, 1 - core] + keeps).astype(jnp.int32)
    groups = query_weight.shape[1] // (2 * HEAD_SIZE)
    token = [hidden]

    def step(function, *args):
        flat, tree = jax.tree.flatten(args)
        flat = lax.optimization_barrier((*flat, token[0]))[:-1]
        out = function(*jax.tree.unflatten(tree, flat))
        token[0] = jax.tree.leaves(out)[0]
        return out

    def now(x):
        return after(x, token[0])

    def gather(x, work, between=lambda: None, later=lambda: None, late=False, then=lambda: None):
        two = row_swap(x, 2)
        first = swap(x)
        token[0] = x
        done = [work(0, x, first)]
        between()
        one = row_swap(now(x) if late else x, 1)
        then()
        two = now(two)
        three = row_swap(two, 1)
        second = swap(two)
        token[0] = two
        one = now(one)
        done.append(work(1, one, swap(one)))
        done.append(work(2, two, second))
        later()
        three = now(three)
        done.append(work(3, three, swap(three)))
        return [x, one, two, three], done

    turns = ((1, 2), (2, 1))

    def halving(sent, kept, which):
        first, second = turns[which]
        got = dp_swap(sent, first, dp)
        yield
        sent, mine = step(lambda *a: add_halves(*a[:2], which, a[2]), kept[which], got, t)
        got = dp_swap(sent, second, dp)
        yield
        mine = step(add, mine, got, t)
        near = dp_swap(mine, second, dp)
        yield
        return [mine, near, dp_swap(step(join, mine, near, t), first, dp)]

    if dp == 4:
        ids = [piece_rows(bits, me) for bits in turns]
    else:
        ids = [[0 * core + i for i in range(4)]] * 2

    class Sum:
        def __init__(self):
            self.runs, self.sent, self.kept, self.pieces = [], [], [], []

        def add(self, sent):
            self.sent.append(sent)
            if dp == 4:
                self.runs.append(halving(sent, self.kept, len(self.runs)))
                next(self.runs[-1])

        def step(self, chosen=slice(None)):
            for run in self.runs[chosen]:
                try:
                    next(run)
                except StopIteration as stop:
                    self.pieces.append(stop.value)

        def finish(self):
            if self.pieces:
                token[0] = after(*(piece[2] for piece in self.pieces))

        def result(self):
            if dp != 4:
                for kept, sent in lax.psum(tuple(zip(self.kept, self.sent)), "dp"):
                    size = kept.shape[0] // 2
                    self.pieces.append((kept[:size], kept[size:], sent))
            return (*self.pieces, *ids, core)

    def small_sum(x):
        for axis, size in (("row", ROWS), ("dp", dp)):
            for mask in (1, 2):
                if size == 4:
                    got = lax.ppermute(x, axis, [(i, i ^ mask) for i in range(size)])
                    yield
                    x = x + now(got)
                    token[0] = x
                else:
                    yield
            if size != 4:
                x = lax.psum(x, axis)
        return x

    def spread(parts):
        got_three = row_swap(parts[3], 1)
        yield
        got_three = now(got_three)
        sent = (parts[2] + got_three.astype(F32)).astype(BF16)
        token[0] = sent
        got_two = row_swap(sent, 2)
        got_one = row_swap(after(parts[1], got_three), 1)
        yield
        return parts[0] + now(got_one).astype(F32) + now(got_two).astype(F32)

    def scatter(term, between=lambda: None):
        part_three = term(3, BF16)
        got_three = row_swap(part_three, 1)
        part_one = term(1, BF16)
        part_two = term(2, F32)
        got_three = now(got_three)
        sent = (part_two + got_three.astype(F32)).astype(BF16)
        token[0] = sent
        got_two = row_swap(sent, 2)
        got_one = row_swap(after(part_one, got_three), 1)
        own = term(0, F32)
        between()
        got_one, got_two = now(got_one), now(got_two)
        return own + got_one.astype(F32) + got_two.astype(F32)

    resid = hidden.astype(F32)
    unit_one, factor_one = norm_stats(resid)
    sent_one = (unit_one * norm_before).astype(BF16)

    def for_other(weight, axis):
        half = weight.shape[axis] // 2
        return lax.dynamic_slice_in_dim(after(weight, sent_one), (1 - core) * half, half, axis)

    heads = (query_weight, key_matrix, value_matrix)
    qkv_x = swap(cat([for_other(w, 1) for w in heads], 1))
    gate_x, up_x = swap(for_other(gate_weight, 1)), swap(for_other(up_weight, 1))
    down_x = swap(for_other(down_weight, 0))
    cosine, sine = rope_tables()

    def settle(x):
        token[0] = after(x, token[0])

    n1, raws = gather(
        sent_one, lambda s, own, other: step(head_rows, own, other, heads, qkv_x, t),
        lambda: settle(gate_x), lambda: settle(up_x),
    )
    settle(down_x)
    cot = lax.all_gather(cotangent, "row", axis=0, tiled=True)
    att, lse, query, key, value = step(
        lambda *a: attend(*a, groups), t, raws, cosine, sine, query_gain, key_gain
    )
    att_oth = swap(att)
    middle = resid + scatter(
        lambda s, kind: step(
            lambda *a: out_rows(*a[:3], s, kind, a[3]), att, att_oth, output_weight, t
        )
    )

    cot = after(cot, middle)
    cot_x = swap(cot)
    unit_two, factor_two = norm_stats(middle)
    sent_two = (unit_two * norm_after).astype(BF16)
    g_mixed = []

    def hidden_units(s, own, other):
        if s == 0:
            g_mixed.append(step(g_mixed_rows, cot, cot_x, down_weight, down_x, t))
        packed = step(
            lambda *a: mlp(*a[:7], s, a[7]),
            own, other, gate_weight, up_weight, gate_x, up_x, g_mixed[0], t,
        )
        return packed, swap(packed)

    n2, packs = gather(sent_two, hidden_units)
    width = down_weight.shape[1]
    ff_sum, last_sum = Sum(), Sum()
    for stays in (False, True):
        for which in range(2):
            grad = step(
                lambda *a: ff_grads(which, stays, *a), [p[which] for p in packs], n2, cot, t
            )
            if stays:
                ff_sum.kept.append(grad)
            else:
                ff_sum.add(grad)
    dsecond = scatter(
        lambda s, kind: step(
            lambda *a: mlp_back(*a[:4], kind, a[4]), *packs[s], gate_weight, up_weight, t
        )
    )
    token[0] = dsecond
    ff_sum.step(slice(0, 1))
    dmid_norm, after_part = norm_backward(dsecond, unit_two, factor_two, norm_after)
    dmiddle = cotangent.astype(F32) + dmid_norm

    swapped = []

    def g_attended(s, own, other):
        if swapped:
            token[0] = after(swapped[-1], token[0])
        mine, sent = step(g_heads, own, output_weight, t)
        swapped.append(swap(sent))
        return mine, swapped[-1]

    last = []

    def second_half():
        ff_sum.step(slice(1, 2))

    def feed_forward_rows():
        last.extend(step(down_rows, packs, down_weight, t))

    dmid, datt = gather(dmiddle.astype(BF16), g_attended, second_half, ff_sum.step, True, feed_forward_rows)

    dqkv, gain_parts = step(
        lambda *a: attend_back(*a, groups),
        t, raws, [d for d, _ in datt], [d for _, d in datt],
        cosine, sine, query_gain, key_gain, (query, key, value, lse),
    )
    dqkv_oth = swap(dqkv)
    ff_sum.step()
    parts = step(last_grads, att, att_oth, dqkv, dqkv_oth, dmid, n1, t)
    last_sum.kept += parts[::2]
    last_sum.add(parts[1])
    last_sum.add(parts[3])
    dfirst = scatter(
        lambda s, kind: step(
            lambda *a: head_back(*a[:2], a[2:5], s, kind, a[5]), dqkv, dqkv_oth, *heads, t
        )
    )
    token[0] = dfirst
    last_run = spread(last)
    next(last_run)
    dres_norm, before_part = norm_backward(now(dfirst), unit_one, factor_one, norm_before)
    hidden_grad = dmiddle + dres_norm
    small_run = small_sum(cat([after_part, before_part, gain_parts.reshape(-1)], 0))
    next(small_run)
    ff_sum.finish()
    gate_grad, up_grad, down_grad = step(
        lambda *a: assemble_ff(*a, width, gate_x.shape[1]), *ff_sum.result()
    )
    next(small_run)
    last_sum.step()
    next(small_run)
    next(last_run)
    last_sum.step()
    next(small_run)
    last_sum.step()
    small = finish(small_run)
    after_grad, before_grad = small[:width], small[width : 2 * width]
    gains = small[2 * width :] + swap(small[2 * width :])
    layer_out = (middle + finish(last_run)).astype(BF16)
    query_grad, key_grad, value_grad, output_grad = assemble(
        *last_sum.result(), tuple(w.shape[1] // 2 for w in heads), width // 4, width
    )
    return (
        layer_out,
        hidden_grad,
        before_grad,
        query_grad,
        key_grad,
        value_grad,
        gains[:HEAD_SIZE],
        gains[HEAD_SIZE:],
        output_grad,
        after_grad,
        gate_grad,
        up_grad,
        down_grad,
    )


def solution(mesh):
    placed = (
        P(("dp", "row"), "col"),
        P("col"),
        P("col", "row"),
        P("col", "row"),
        P("col", "row"),
        P(),
        P(),
        P("row", "col"),
        P("col"),
        P("col", "row"),
        P("col", "row"),
        P("row", "col"),
        P(("dp", "row"), "col"),
    )
    return jax.shard_map(
        on_device,
        mesh=mesh,
        in_specs=placed,
        out_specs=(
            P(("dp", "row"), "col"),
            P(("dp", "row"), "col"),
            P("col"),
            P("col", "row"),
            P("col", "row"),
            P("col", "row"),
            P(),
            P(),
            P("row", "col"),
            P("col"),
            P("col", "row"),
            P("col", "row"),
            P("row", "col"),
        ),
        check_vma=False,
    )
```

```python
import functools
import math

import jax
import jax.numpy as jnp
from jax import lax
from jax.experimental import pallas as pl
from jax.experimental.pallas import tpu as pltpu
from jax.sharding import PartitionSpec as P

MODEL_WIDTH = 2048
HEAD_SIZE = 128
SEQUENCE_LENGTH = 1024
EPS = 1e-06
THETA = 1000000.0
ROWS = 4
BLOCK = SEQUENCE_LENGTH // ROWS
SCALE = 1.0 / math.sqrt(HEAD_SIZE)
LOG2 = SCALE * math.log2(math.e)

F32 = jnp.float32
BF16 = jnp.bfloat16
SMEM = pl.BlockSpec(memory_space=pltpu.SMEM)
VMEM = pl.BlockSpec(memory_space=pltpu.VMEM)
NO_COST = pl.CostEstimate(flops=1, transcendentals=0, bytes_accessed=1)


def swap(x):
    return lax.ppermute(x, "col", [(0, 1), (1, 0)])


def row_swap(x, mask):
    return lax.ppermute(x, "row", [(i, i ^ mask) for i in range(ROWS)])


def after(x, *others):
    return lax.optimization_barrier((x, *others))[0]


def dp_swap(x, mask, dp):
    return lax.ppermute(x, "dp", [(i, i ^ mask) for i in range(dp)])


def finish(run):
    try:
        while True:
            next(run)
    except StopIteration as stop:
        return stop.value


def piece_rows(bits, me):
    first, second = bits
    rows = []
    for mask in (0, second, first, first + second):
        who = me ^ mask
        rows.append(((who // first) % 2) * 2 + (who // second) % 2)
    return rows


def assemble_kernel(tall, spans, table_ref, *refs):
    pieces, outs = refs[:6], refs[6:]
    rows, columns = pieces[0].shape
    half, slot = pl.program_id(0), pl.program_id(1)
    for h in range(2):
        for s in range(4):

            @pl.when((half == h) & (slot == s))
            def _(piece=pieces[h * 3 + min(s, 2)], base=rows if s == 3 else 0):
                for (lo, hi), out in zip(spans, outs):
                    out[...] = piece[base : base + tall, lo:hi].astype(F32)
                short = outs[-1].shape[0]
                for c in range(outs[-1].shape[1] // columns):
                    start = base + tall + c * short
                    outs[-1][:, c * columns : (c + 1) * columns] = piece[
                        start : start + short, :
                    ].astype(F32)


def assemble(pieces_a, pieces_b, ids_a, ids_b, core, widths, tall, wide):
    rows, columns = pieces_a[0].shape
    spans, at = [], 0
    for width in widths:
        spans.append((at, at + width))
        at += width
    short = (rows - tall) * columns // wide
    table = jnp.stack([*ids_a, *ids_b, core, 1 - core]).astype(jnp.int32)
    return pl.pallas_call(
        functools.partial(assemble_kernel, tall, spans),
        out_shape=[jax.ShapeDtypeStruct((tall * 4, width * 2), F32) for width in widths]
        + [jax.ShapeDtypeStruct((short * 8, wide), F32)],
        grid_spec=pltpu.PrefetchScalarGridSpec(
            num_scalar_prefetch=1,
            grid=(2, 4),
            in_specs=[pl.BlockSpec(p.shape, lambda h, s, t: (0, 0)) for p in (*pieces_a, *pieces_b)],
            out_specs=[
                pl.BlockSpec((tall, width), lambda h, s, t: (t[h * 4 + s], t[8 + h]))
                for width in widths
            ]
            + [pl.BlockSpec((short, wide), lambda h, s, t: (t[8 + h] * 4 + t[h * 4 + s], 0))],
        ),
        compiler_params=pltpu.CompilerParams(vmem_limit_bytes=16 << 20),
        cost_estimate=NO_COST,
    )(table, *pieces_a, *pieces_b)


def assemble_ff_kernel(table_ref, *refs):
    pieces, (gate, up, down) = refs[:6], refs[6:]
    rows, columns = pieces[0].shape
    tall, ff = gate.shape
    half, slot = pl.program_id(0), pl.program_id(1)
    for h in range(2):
        for s in range(4):

            @pl.when((half == h) & (slot == s))
            def _(piece=pieces[h * 3 + min(s, 2)], base=rows if s == 3 else 0):
                for chunk in range(2 * ff // 256):
                    out, at = (gate, chunk * 256) if chunk * 256 < ff else (up, chunk * 256 - ff)
                    block, col = divmod(chunk * 256, columns)
                    start = base + block * tall
                    out[:, at : at + 256] = piece[start : start + tall, col : col + 256].astype(F32)
                start, short = base + 2 * ff // columns * tall, ff * down.shape[1] // columns
                for c in range(2):
                    down[c * short : (c + 1) * short, :] = piece[
                        start : start + short, c * down.shape[1] : (c + 1) * down.shape[1]
                    ].astype(F32)


def assemble_ff(pieces_a, pieces_b, ids_a, ids_b, core, width, ff):
    table = jnp.stack([*ids_a, *ids_b, core, 1 - core]).astype(jnp.int32)
    quarter = width // 4
    return pl.pallas_call(
        assemble_ff_kernel,
        out_shape=[jax.ShapeDtypeStruct((width, 2 * ff), F32)] * 2
        + [jax.ShapeDtypeStruct((2 * ff, width), F32)],
        grid_spec=pltpu.PrefetchScalarGridSpec(
            num_scalar_prefetch=1,
            grid=(2, 4),
            in_specs=[pl.BlockSpec(p.shape, lambda h, s, t: (0, 0)) for p in (*pieces_a, *pieces_b)],
            out_specs=[pl.BlockSpec((quarter, ff), lambda h, s, t: (t[h * 4 + s], t[8 + h]))] * 2
            + [pl.BlockSpec((ff, quarter), lambda h, s, t: (t[8 + h], t[h * 4 + s]))],
        ),
        compiler_params=pltpu.CompilerParams(vmem_limit_bytes=32 << 20),
        cost_estimate=NO_COST,
    )(table, *pieces_a, *pieces_b)


def cat(items, axis):
    return jnp.concatenate(items, axis)


def rope_tables():
    half = HEAD_SIZE // 2
    freq = THETA ** (-(jnp.arange(half, dtype=F32) * 2.0) / HEAD_SIZE)
    angle = jnp.arange(SEQUENCE_LENGTH, dtype=F32)[:, None] * freq[None, :]
    cosine = jnp.cos(angle)
    sine = jnp.sin(angle)
    return (jnp.concatenate([cosine, cosine], 1), jnp.concatenate([-sine, sine], 1))


def dot(a, b, dims):
    return lax.dot_general(a, b, (dims, ((), ())), preferred_element_type=F32)


NN = ((1,), (0,))
NT = ((1,), (1,))
TN = ((0,), (0,))


def unit_rows(x):
    factor = lax.rsqrt(jnp.mean(x * x, axis=1, keepdims=True) + EPS)
    return x * factor, factor


def raw_scores(query, key, block):
    scores = dot(query, key, NT)
    row = lax.broadcasted_iota(jnp.int32, scores.shape, 0) + block * BLOCK
    column = lax.broadcasted_iota(jnp.int32, scores.shape, 1)
    return jnp.where(row >= column, scores, -1e30)


def attend_kernel(groups, table, *refs):
    raws = refs[:ROWS]
    cosine, sine, q_gain, k_gain = refs[ROWS : ROWS + 4]
    att, lse, query, key, value = refs[ROWS + 4 :]
    width = HEAD_SIZE
    for s in range(ROWS):
        rows = pl.ds(pl.multiple_of(table[s] * BLOCK, BLOCK), BLOCK)
        cos, sin = cosine[rows, :], sine[rows, :]
        for h in range(groups + 1):
            unit, _ = unit_rows(raws[s][:, h * width : (h + 1) * width])
            gained = unit * (q_gain[...] if h < groups else k_gain[...])
            turned = gained * cos + pltpu.roll(gained, width // 2, 1) * sin
            if h < groups:
                query[rows, h * width : (h + 1) * width] = turned.astype(BF16)
            else:
                key[rows, :] = turned.astype(BF16)
        value[rows, :] = raws[s][:, (groups + 1) * width :].astype(BF16)
    for i in range(ROWS):
        span = (i + 1) * BLOCK
        slot = table[ROWS + i]
        rows = pl.ds(pl.multiple_of(slot * BLOCK, BLOCK), BLOCK)
        for h in range(groups):
            cols = slice(h * width, (h + 1) * width)
            scores = raw_scores(query[i * BLOCK : span, cols], key[:span, :], i)
            top = jnp.max(scores, axis=1, keepdims=True)
            expo = jnp.exp2((scores - top) * LOG2)
            total = jnp.sum(expo, axis=1, keepdims=True)
            prob = (expo * (1.0 / total)).astype(BF16)
            att[rows, cols] = dot(prob, value[:span, :], NN).astype(BF16)
            log = top * LOG2 + jnp.log2(total)
            lse[i * BLOCK : span, cols] = jnp.broadcast_to(log, (BLOCK, width))


def attend_back_kernel(groups, table, *refs):
    raws = refs[:ROWS]
    grads, others = refs[ROWS : 2 * ROWS], refs[2 * ROWS : 3 * ROWS]
    cosine, sine, q_gain, k_gain, query, key, value, lse = refs[3 * ROWS : 3 * ROWS + 8]
    out, gains, d_query, d_key, d_value, grad = refs[3 * ROWS + 8 :]
    width = HEAD_SIZE
    for s in range(ROWS):
        rows = pl.ds(pl.multiple_of(table[s] * BLOCK, BLOCK), BLOCK)
        grad[rows, :] = (grads[s][...] + others[s][...].astype(F32)).astype(BF16)
    d_key[...] = jnp.zeros_like(d_key)
    d_value[...] = jnp.zeros_like(d_value)
    for i in range(ROWS):
        span = (i + 1) * BLOCK
        for h in range(groups):
            cols = slice(h * width, (h + 1) * width)
            q = query[i * BLOCK : span, cols]
            g = grad[i * BLOCK : span, cols]
            scores = raw_scores(q, key[:span, :], i)
            log = lse[i * BLOCK : span, h * width : h * width + 1]
            prob = jnp.exp2(scores * LOG2 - log)
            dprob = dot(g, value[:span, :], NT)
            delta = jnp.sum(prob * dprob, axis=1, keepdims=True)
            dscore = (SCALE * prob * (dprob - delta)).astype(BF16)
            d_query[i * BLOCK : span, cols] = dot(dscore, key[:span, :], NN)
            d_key[:span, :] += dot(dscore, q, TN)
            d_value[:span, :] += dot(prob.astype(BF16), g, TN)
    gain_sums = [jnp.zeros((1, width), F32), jnp.zeros((1, width), F32)]
    for s in range(ROWS):
        rows = pl.ds(pl.multiple_of(table[s] * BLOCK, BLOCK), BLOCK)
        cos, sin = cosine[rows, :], sine[rows, :]
        for h in range(groups + 1):
            cols = slice(h * width, (h + 1) * width)
            unit, factor = unit_rows(raws[s][:, cols])
            turned = d_query[rows, cols] if h < groups else d_key[rows, :]
            back = turned * cos + pltpu.roll(turned * sin, width // 2, 1)
            scaled = back * (q_gain[...] if h < groups else k_gain[...])
            inner = jnp.mean(scaled * unit, axis=1, keepdims=True)
            which = 0 if h < groups else 1
            gain_sums[which] += jnp.sum(back * unit, axis=0, keepdims=True)
            out[s * BLOCK : (s + 1) * BLOCK, cols] = (factor * (scaled - unit * inner)).astype(BF16)
        out[s * BLOCK : (s + 1) * BLOCK, (groups + 1) * width :] = d_value[rows, :].astype(BF16)
    gains[0:1, :] = gain_sums[0]
    gains[1:2, :] = gain_sums[1]


def attend(table, raws, cosine, sine, q_gain, k_gain, groups):
    wide = (SEQUENCE_LENGTH, groups * HEAD_SIZE)
    one = (SEQUENCE_LENGTH, HEAD_SIZE)
    return pl.pallas_call(
        functools.partial(attend_kernel, groups),
        out_shape=[
            jax.ShapeDtypeStruct(wide, BF16),
            jax.ShapeDtypeStruct(wide, F32),
            jax.ShapeDtypeStruct(wide, BF16),
            jax.ShapeDtypeStruct(one, BF16),
            jax.ShapeDtypeStruct(one, BF16),
        ],
        in_specs=[SMEM] + [VMEM] * (ROWS + 4),
        out_specs=[VMEM] * 5,
        compiler_params=pltpu.CompilerParams(vmem_limit_bytes=16 << 20),
        cost_estimate=NO_COST,
    )(table, *raws, cosine, sine, q_gain[None], k_gain[None])


def attend_back(table, raws, grads, others, cosine, sine, q_gain, k_gain, saved, groups):
    query, key, value, lse = saved
    return pl.pallas_call(
        functools.partial(attend_back_kernel, groups),
        out_shape=[
            jax.ShapeDtypeStruct((SEQUENCE_LENGTH, (groups + 2) * HEAD_SIZE), BF16),
            jax.ShapeDtypeStruct((2, HEAD_SIZE), F32),
        ],
        in_specs=[SMEM] + [VMEM] * (3 * ROWS + 8),
        out_specs=[VMEM] * 2,
        scratch_shapes=[
            pltpu.VMEM((SEQUENCE_LENGTH, groups * HEAD_SIZE), F32),
            pltpu.VMEM((SEQUENCE_LENGTH, HEAD_SIZE), F32),
            pltpu.VMEM((SEQUENCE_LENGTH, HEAD_SIZE), F32),
            pltpu.VMEM((SEQUENCE_LENGTH, groups * HEAD_SIZE), BF16),
        ],
        compiler_params=pltpu.CompilerParams(vmem_limit_bytes=20 << 20),
        cost_estimate=NO_COST,
    )(table, *raws, *grads, *others, cosine, sine, q_gain[None], k_gain[None], query, key, value, lse)


def product(kernel, t, ins, outs, wait=()):
    return pl.pallas_call(
        kernel,
        out_shape=[jax.ShapeDtypeStruct(shape, kind) for shape, kind in outs],
        in_specs=[SMEM] + [VMEM] * len(ins) + [pl.BlockSpec(memory_space=pl.ANY)] * len(wait),
        out_specs=[VMEM] * len(outs),
        compiler_params=pltpu.CompilerParams(vmem_limit_bytes=16 << 20),
        cost_estimate=NO_COST,
    )(t, *ins, *wait)


def hold_kernel(t, x, *refs):
    refs[-1][...] = x[...]


def hold(x, other, t):
    return product(hold_kernel, t, (x,), [(x.shape, x.dtype)], (other,))[0]


def part(t, other, size, start=0, width=None):
    return pl.ds(pl.multiple_of(t[2 * ROWS + other] * size + start, 128), width or size)


def block_rows(t, s):
    return pl.ds(pl.multiple_of(t[s] * BLOCK, BLOCK), BLOCK)


def head_rows_kernel(t, own, other, q, k, v, x, out):
    at = 0
    for weight in (q, k, v):
        width = weight.shape[1] // 2
        cols = slice(at, at + width)
        out[:, cols] = dot(own[...], weight[:, part(t, 0, width)], NN) + dot(
            other[...], x[:, cols], NN
        )
        at += width


def head_rows(own, other, weights, x, t):
    return product(
        head_rows_kernel, t, (own, other, *weights, x), [((own.shape[0], x.shape[1]), F32)]
    )[0]


def out_rows_kernel(s, t, own, other, weight, *refs):
    out = refs[-1]
    rows = slice(s * BLOCK, (s + 1) * BLOCK)
    half = weight.shape[0] // 2
    total = dot(own[rows, :], weight[part(t, 0, half), :], NN)
    total += dot(other[rows, :], weight[part(t, 1, half), :], NN)
    out[...] = total.astype(out.dtype)


def out_rows(own, other, weight, s, kind, t, wait=()):
    return product(
        functools.partial(out_rows_kernel, s), t, (own, other, weight),
        [((BLOCK, weight.shape[1]), kind)], wait,
    )[0]


def g_mixed_kernel(t, own, other, weight, x, out):
    half = x.shape[0]
    out[...] = dot(own[...], weight[part(t, 0, half), :], NT) + dot(other[...], x[...], NT)


def g_mixed_rows(own, other, weight, x, t):
    return product(
        g_mixed_kernel, t, (own, other, weight, x), [((own.shape[0], x.shape[0]), F32)]
    )[0]


FF_BLOCK = 256


def mlp_kernel(t, own, other, gate_weight, up_weight, gate_x, up_x, g_mixed, out):
    ff = gate_x.shape[1]
    for start in range(0, ff, FF_BLOCK):
        cols = slice(start, start + FF_BLOCK)
        mine = part(t, 0, ff, start, FF_BLOCK)
        gate = dot(own[...], gate_weight[:, mine], NN) + dot(other[...], gate_x[:, cols], NN)
        upper = dot(own[...], up_weight[:, mine], NN) + dot(other[...], up_x[:, cols], NN)
        sigma = 1.0 / (1.0 + jnp.exp(-gate))
        activ = gate * sigma
        grad = g_mixed[:, cols]
        out[0, :, cols] = (activ * upper).astype(BF16)
        out[1, :, cols] = (grad * upper * sigma * (1.0 + gate * (1.0 - sigma))).astype(BF16)
        out[2, :, cols] = (grad * activ).astype(BF16)


def mlp(own, other, gate_weight, up_weight, gate_x, up_x, g_mixed, t):
    return product(
        mlp_kernel, t,
        (own, other, gate_weight, up_weight, gate_x, up_x, g_mixed),
        [((3, own.shape[0], gate_x.shape[1]), BF16)],
    )[0]


def mlp_back_kernel(t, own, other, gate_weight, up_weight, out):
    ff = own.shape[2]
    mine, theirs = part(t, 0, ff), part(t, 1, ff)
    for start in range(0, out.shape[1], 256):
        rows = slice(start, start + 256)
        total = dot(own[1], gate_weight[rows, mine], NT) + dot(own[2], up_weight[rows, mine], NT)
        total += dot(other[1], gate_weight[rows, theirs], NT)
        total += dot(other[2], up_weight[rows, theirs], NT)
        out[:, rows] = total.astype(out.dtype)


def mlp_back(own, other, gate_weight, up_weight, kind, t):
    return product(
        mlp_back_kernel, t, (own, other, gate_weight, up_weight),
        [((own.shape[1], gate_weight.shape[0]), kind)],
    )[0]


def down_rows_kernel(t, weight, *refs):
    half = weight.shape[0] // 2
    for s in range(ROWS):
        out = refs[2 * ROWS + s]
        total = dot(refs[2 * s][0], weight[part(t, 0, half), :], NN)
        total += dot(refs[2 * s + 1][0], weight[part(t, 1, half), :], NN)
        out[...] = total.astype(out.dtype)


def down_rows(packs, weight, t):
    shape = (BLOCK, weight.shape[1])
    return product(
        down_rows_kernel, t, (weight, *[p for pair in packs for p in pair]),
        [(shape, kind) for kind in (F32, BF16, F32, BF16)],
    )


def g_heads_kernel(t, x, weight, own, sent):
    half = weight.shape[0] // 2
    own[...] = dot(x[...], weight[part(t, 0, half), :], NT)
    sent[...] = dot(x[...], weight[part(t, 1, half), :], NT).astype(BF16)


def g_heads(x, weight, t):
    shape = (x.shape[0], weight.shape[0] // 2)
    return product(g_heads_kernel, t, (x, weight), [(shape, F32), (shape, BF16)])


def head_back_kernel(s, t, own, other, q, k, v, out):
    rows = slice(s * BLOCK, (s + 1) * BLOCK)
    total = 0.0
    for which, grad in enumerate((own, other)):
        at = 0
        for weight in (q, k, v):
            width = weight.shape[1] // 2
            total += dot(grad[rows, at : at + width], weight[:, part(t, which, width)], NT)
            at += width
    out[...] = total.astype(out.dtype)


def head_back(own, other, weights, s, kind, t):
    return product(
        functools.partial(head_back_kernel, s), t, (own, other, *weights),
        [((BLOCK, weights[0].shape[0]), kind)],
    )[0]


GRAD_COLUMNS = 512


def ff_grads_kernel(which, stays, t, *refs):
    packs, n2, cot, out = refs[:ROWS], refs[ROWS : 2 * ROWS], refs[2 * ROWS : -1], refs[-1]
    ff = packs[0].shape[2]
    tall = cot[0].shape[1] // 4
    short = ff * tall // GRAD_COLUMNS
    kept = t[2 * ROWS + 2 + which]
    half = kept if stays else 1 - kept
    for j in range(2):
        base = j * out.shape[0] // 2
        cols = pl.ds(pl.multiple_of((half * 2 + j) * tall, 128), tall)
        for part_of in range(2):
            total = 0.0
            for s in range(ROWS):
                total += dot(n2[s][:, cols], packs[s][part_of + 1], TN)
            total = total.astype(BF16)
            for at in range(0, ff, 256):
                block, col = divmod(part_of * ff + at, GRAD_COLUMNS)
                start = base + block * tall
                out[start : start + tall, col : col + 256] = total[:, at : at + 256]
        total = 0.0
        for s in range(ROWS):
            total += dot(packs[s][0], cot[s][:, cols], TN)
        total = total.astype(BF16)
        start = base + 2 * ff // GRAD_COLUMNS * tall
        for c in range(2):
            out[start : start + short, c * tall : (c + 1) * tall] = total[
                c * short : (c + 1) * short, :
            ]


def ff_grads(which, stays, packs, n2, cot, t):
    rows = 3 * packs[0].shape[2] * cot[0].shape[1] // GRAD_COLUMNS // 2
    return product(
        functools.partial(ff_grads_kernel, which, stays), t, (*packs, *n2, *cot),
        [((rows, GRAD_COLUMNS), BF16)],
    )[0]


def last_grads_kernel(t, att, att_other, grad, grad_other, *refs):
    dmid, n1, outs = refs[:ROWS], refs[ROWS : 2 * ROWS], refs[2 * ROWS :]
    columns = grad.shape[1]
    tall, short = n1[0].shape[1] // 4, att.shape[1] // 4
    for which, (x, y) in enumerate(((grad, att), (grad_other, att_other))):
        kept = t[2 * ROWS + 2 + which]
        for out, half in zip(outs[2 * which : 2 * which + 2], (kept, 1 - kept)):
            heads = pl.ds(pl.multiple_of(half * 2 * short, 128), 2 * short)
            total = 0.0
            for s in range(ROWS):
                total += dot(y[s * BLOCK : (s + 1) * BLOCK, heads], dmid[s][...], TN)
            total = total.astype(BF16)
            at = 0
            for j in range(2):
                cols = pl.ds(pl.multiple_of(half * 2 * tall + j * tall, 128), tall)
                upper = 0.0
                for s in range(ROWS):
                    upper += dot(n1[s][:, cols], x[s * BLOCK : (s + 1) * BLOCK, :], TN)
                out[at : at + tall, :] = upper.astype(BF16)
                at += tall
                for c in range(total.shape[1] // columns):
                    out[at : at + short, :] = total[
                        j * short : (j + 1) * short, c * columns : (c + 1) * columns
                    ]
                    at += short


def last_grads(att, att_other, grad, grad_other, dmid, n1, t):
    columns = grad.shape[1]
    rows = n1[0].shape[1] // 2 + att.shape[1] // 2 * dmid[0].shape[1] // columns
    return product(
        last_grads_kernel, t, (att, att_other, grad, grad_other, *dmid, *n1),
        [((rows, columns), BF16)] * 4,
    )


def add_halves_kernel(which, t, kept, got, away, mine):
    size = away.shape[0]
    half = t[2 * ROWS + 3 - which]
    for out, v in ((away, 1 - half), (mine, half)):
        rows = pl.ds(pl.multiple_of(v * size, 128), size)
        out[...] = (kept[rows, :].astype(F32) + got[rows, :].astype(F32)).astype(BF16)


def add_halves(kept, got, which, t):
    shape = (kept.shape[0] // 2, kept.shape[1])
    return product(
        functools.partial(add_halves_kernel, which), t, (kept, got), [(shape, BF16)] * 2
    )


def add_kernel(t, x, y, out):
    out[...] = (x[...].astype(F32) + y[...].astype(F32)).astype(BF16)


def add(x, y, t):
    return product(add_kernel, t, (x, y), [(x.shape, BF16)])[0]


def join_kernel(t, x, y, out):
    rows = x.shape[0]
    out[:rows, :] = x[...]
    out[rows:, :] = y[...]


def join(x, y, t):
    return product(join_kernel, t, (x, y), [((2 * x.shape[0], x.shape[1]), BF16)])[0]


def norm_stats(x):
    part = jnp.sum(x * x, axis=1)
    factor = lax.rsqrt((part + swap(part)) / MODEL_WIDTH + EPS)
    return x * factor[:, None], factor


def norm_backward(grad, unit, factor, gain):
    scaled = grad * gain
    part = jnp.sum(scaled * unit, axis=1)
    inner = (part + swap(part)) / MODEL_WIDTH
    return (factor[:, None] * (scaled - unit * inner[:, None]), jnp.sum(grad * unit, axis=0))


def on_device(
    hidden,
    norm_before,
    query_weight,
    key_matrix,
    value_matrix,
    query_gain,
    key_gain,
    output_weight,
    norm_after,
    gate_weight,
    up_weight,
    down_weight,
    cotangent,
):
    dp = lax.axis_size("dp")
    k, core, me = lax.axis_index("row"), lax.axis_index("col"), lax.axis_index("dp")
    keeps = [me % 2, (me // 2) % 2] if dp == 4 else [0 * me, 0 * me]
    t = jnp.stack([k ^ i for i in range(ROWS)] * 2 + [core, 1 - core] + keeps).astype(jnp.int32)
    groups = query_weight.shape[1] // (2 * HEAD_SIZE)
    token = [hidden]

    def step(function, *args):
        flat, tree = jax.tree.flatten(args)
        flat = lax.optimization_barrier((*flat, token[0]))[:-1]
        out = function(*jax.tree.unflatten(tree, flat))
        token[0] = jax.tree.leaves(out)[0]
        return out

    def now(x):
        return after(x, token[0])

    def gather(x, work, between=lambda: None, later=lambda: None, late=False, then=lambda: None):
        two = row_swap(x, 2)
        first = swap(x)
        token[0] = x
        done = [work(0, x, first)]
        between()
        one = row_swap(now(x) if late else x, 1)
        then()
        two = now(two)
        three = row_swap(two, 1)
        second = swap(two)
        token[0] = two
        one = now(one)
        done.append(work(1, one, swap(one)))
        done.append(work(2, two, second))
        later()
        three = now(three)
        done.append(work(3, three, swap(three)))
        return [x, one, two, three], done

    turns = ((1, 2), (2, 1))

    def halving(sent, kept, which):
        first, second = turns[which]
        got = dp_swap(sent, first, dp)
        yield
        sent, mine = step(lambda *a: add_halves(*a[:2], which, a[2]), kept[which], got, t)
        got = dp_swap(sent, second, dp)
        yield
        mine = step(add, mine, got, t)
        near = dp_swap(mine, second, dp)
        yield
        return [mine, near, dp_swap(step(join, mine, near, t), first, dp)]

    if dp == 4:
        ids = [piece_rows(bits, me) for bits in turns]
    else:
        ids = [[0 * core + i for i in range(4)]] * 2

    class Sum:
        def __init__(self):
            self.runs, self.sent, self.kept, self.pieces = [], [], [], []

        def add(self, sent):
            self.sent.append(sent)
            if dp == 4:
                self.runs.append(halving(sent, self.kept, len(self.runs)))
                next(self.runs[-1])

        def step(self, chosen=slice(None)):
            for run in self.runs[chosen]:
                try:
                    next(run)
                except StopIteration as stop:
                    self.pieces.append(stop.value)

        def finish(self):
            if self.pieces:
                token[0] = after(*(piece[2] for piece in self.pieces))

        def result(self):
            if dp != 4:
                for kept, sent in lax.psum(tuple(zip(self.kept, self.sent)), "dp"):
                    size = kept.shape[0] // 2
                    self.pieces.append((kept[:size], kept[size:], sent))
            return (*self.pieces, *ids, core)

    def small_sum(x):
        for axis, size in (("row", ROWS), ("dp", dp)):
            for mask in (1, 2):
                if size == 4:
                    got = lax.ppermute(x, axis, [(i, i ^ mask) for i in range(size)])
                    yield
                    x = x + now(got)
                    token[0] = x
                else:
                    yield
            if size != 4:
                x = lax.psum(x, axis)
        return x

    def spread(parts):
        got_three = row_swap(parts[3], 1)
        yield
        got_three = now(got_three)
        sent = (parts[2] + got_three.astype(F32)).astype(BF16)
        token[0] = sent
        got_two = row_swap(sent, 2)
        got_one = row_swap(after(parts[1], got_three), 1)
        yield
        return parts[0] + now(got_one).astype(F32) + now(got_two).astype(F32)

    def scatter(term, between=lambda: None):
        part_three = term(3, BF16)
        got_three = row_swap(part_three, 1)
        part_one = term(1, BF16)
        part_two = term(2, F32)
        got_three = now(got_three)
        sent = (part_two + got_three.astype(F32)).astype(BF16)
        token[0] = sent
        got_two = row_swap(sent, 2)
        got_one = row_swap(after(part_one, got_three), 1)
        own = term(0, F32)
        between()
        got_one, got_two = now(got_one), now(got_two)
        return own + got_one.astype(F32) + got_two.astype(F32)

    resid = hidden.astype(F32)
    unit_one, factor_one = norm_stats(resid)
    sent_one = (unit_one * norm_before).astype(BF16)

    def for_other(weight, axis):
        half = weight.shape[axis] // 2
        return lax.dynamic_slice_in_dim(after(weight, sent_one), (1 - core) * half, half, axis)

    heads = (query_weight, key_matrix, value_matrix)
    qkv_x = swap(cat([for_other(w, 1) for w in heads], 1))
    gate_x, up_x = swap(for_other(gate_weight, 1)), swap(for_other(up_weight, 1))
    down_x = swap(for_other(down_weight, 0))
    cosine, sine = rope_tables()

    def settle(x):
        token[0] = after(x, token[0])

    cot = [cotangent]

    def start_cotangent():
        start = hold(cotangent, token[0], t)
        cot.append(row_swap(start, 1))
        cot.append(row_swap(start, 2))

    n1, raws = gather(
        sent_one, lambda s, own, other: step(head_rows, own, other, heads, qkv_x, t),
        lambda: settle(gate_x), start_cotangent,
    )
    settle(up_x)
    settle(down_x)
    att, lse, query, key, value = step(
        lambda *a: attend(*a, groups), t, raws, cosine, sine, query_gain, key_gain
    )
    att_oth = swap(att)
    middle = resid + scatter(
        lambda s, kind: step(
            lambda *a: out_rows(*a[:3], s, kind, *a[3:]),
            att, att_oth, output_weight, t, (cot[1], cot[2]) if s == 3 else (),
        )
    )

    cot.append(row_swap(hold(cot[2], middle, t), 1))
    cot_x = [swap(c) for c in cot]
    unit_two, factor_two = norm_stats(middle)
    sent_two = (unit_two * norm_after).astype(BF16)

    def hidden_units(s, own, other):
        g_mixed = step(g_mixed_rows, cot[s], cot_x[s], down_weight, down_x, t)
        packed = step(mlp, own, other, gate_weight, up_weight, gate_x, up_x, g_mixed, t)
        return packed, swap(packed)

    n2, packs = gather(sent_two, hidden_units)
    width = down_weight.shape[1]
    ff_sum, last_sum = Sum(), Sum()
    for stays in (False, True):
        for which in range(2):
            grad = step(
                lambda *a: ff_grads(which, stays, *a), [p[which] for p in packs], n2, cot, t
            )
            if stays:
                ff_sum.kept.append(grad)
            else:
                ff_sum.add(grad)
    dsecond = scatter(
        lambda s, kind: step(
            lambda *a: mlp_back(*a[:4], kind, a[4]), *packs[s], gate_weight, up_weight, t
        )
    )
    token[0] = dsecond
    ff_sum.step(slice(0, 1))
    dmid_norm, after_part = norm_backward(dsecond, unit_two, factor_two, norm_after)
    dmiddle = cotangent.astype(F32) + dmid_norm

    swapped = []

    def g_attended(s, own, other):
        if swapped:
            token[0] = after(swapped[-1], token[0])
        mine, sent = step(g_heads, own, output_weight, t)
        swapped.append(swap(sent))
        return mine, swapped[-1]

    last = []

    def second_half():
        ff_sum.step(slice(1, 2))

    def feed_forward_rows():
        last.extend(step(down_rows, packs, down_weight, t))

    dmid, datt = gather(dmiddle.astype(BF16), g_attended, second_half, ff_sum.step, True, feed_forward_rows)

    dqkv, gain_parts = step(
        lambda *a: attend_back(*a, groups),
        t, raws, [d for d, _ in datt], [d for _, d in datt],
        cosine, sine, query_gain, key_gain, (query, key, value, lse),
    )
    dqkv_oth = swap(dqkv)
    ff_sum.step()
    parts = step(last_grads, att, att_oth, dqkv, dqkv_oth, dmid, n1, t)
    last_sum.kept += parts[::2]
    last_sum.add(parts[1])
    last_sum.add(parts[3])
    dfirst = scatter(
        lambda s, kind: step(
            lambda *a: head_back(*a[:2], a[2:5], s, kind, a[5]), dqkv, dqkv_oth, *heads, t
        )
    )
    token[0] = dfirst
    last_run = spread(last)
    next(last_run)
    dres_norm, before_part = norm_backward(now(dfirst), unit_one, factor_one, norm_before)
    hidden_grad = dmiddle + dres_norm
    small_run = small_sum(cat([after_part, before_part, gain_parts.reshape(-1)], 0))
    next(small_run)
    ff_sum.finish()
    gate_grad, up_grad, down_grad = step(
        lambda *a: assemble_ff(*a, width, gate_x.shape[1]), *ff_sum.result()
    )
    next(small_run)
    last_sum.step()
    next(small_run)
    next(last_run)
    last_sum.step()
    next(small_run)
    last_sum.step()
    small = finish(small_run)
    after_grad, before_grad = small[:width], small[width : 2 * width]
    gains = small[2 * width :] + swap(small[2 * width :])
    layer_out = (middle + finish(last_run)).astype(BF16)
    query_grad, key_grad, value_grad, output_grad = assemble(
        *last_sum.result(), tuple(w.shape[1] // 2 for w in heads), width // 4, width
    )
    return (
        layer_out,
        hidden_grad,
        before_grad,
        query_grad,
        key_grad,
        value_grad,
        gains[:HEAD_SIZE],
        gains[HEAD_SIZE:],
        output_grad,
        after_grad,
        gate_grad,
        up_grad,
        down_grad,
    )


def solution(mesh):
    placed = (
        P(("dp", "row"), "col"),
        P("col"),
        P("col", "row"),
        P("col", "row"),
        P("col", "row"),
        P(),
        P(),
        P("row", "col"),
        P("col"),
        P("col", "row"),
        P("col", "row"),
        P("row", "col"),
        P(("dp", "row"), "col"),
    )
    return jax.shard_map(
        on_device,
        mesh=mesh,
        in_specs=placed,
        out_specs=(
            P(("dp", "row"), "col"),
            P(("dp", "row"), "col"),
            P("col"),
            P("col", "row"),
            P("col", "row"),
            P("col", "row"),
            P(),
            P(),
            P("row", "col"),
            P("col"),
            P("col", "row"),
            P("col", "row"),
            P("row", "col"),
        ),
        check_vma=False,
    )
```

```python
import functools
import math

import jax
import jax.numpy as jnp
from jax import lax
from jax.experimental import pallas as pl
from jax.experimental.pallas import tpu as pltpu
from jax.sharding import PartitionSpec as P

MODEL_WIDTH = 2048
HEAD_SIZE = 128
SEQUENCE_LENGTH = 1024
EPS = 1e-06
THETA = 1000000.0
ROWS = 4
BLOCK = SEQUENCE_LENGTH // ROWS
SCALE = 1.0 / math.sqrt(HEAD_SIZE)
LOG2 = SCALE * math.log2(math.e)

F32 = jnp.float32
BF16 = jnp.bfloat16
SMEM = pl.BlockSpec(memory_space=pltpu.SMEM)
VMEM = pl.BlockSpec(memory_space=pltpu.VMEM)
NO_COST = pl.CostEstimate(flops=1, transcendentals=0, bytes_accessed=1)


def swap(x):
    return lax.ppermute(x, "col", [(0, 1), (1, 0)])


def row_swap(x, mask):
    return lax.ppermute(x, "row", [(i, i ^ mask) for i in range(ROWS)])


def after(x, *others):
    return lax.optimization_barrier((x, *others))[0]


def dp_swap(x, mask, dp):
    return lax.ppermute(x, "dp", [(i, i ^ mask) for i in range(dp)])


def finish(run):
    try:
        while True:
            next(run)
    except StopIteration as stop:
        return stop.value


def piece_rows(bits, me):
    first, second = bits
    rows = []
    for mask in (0, second, first, first + second):
        who = me ^ mask
        rows.append(((who // first) % 2) * 2 + (who // second) % 2)
    return rows


def assemble_kernel(tall, spans, table_ref, *refs):
    pieces, outs = refs[:6], refs[6:]
    rows, columns = pieces[0].shape
    half, slot = pl.program_id(0), pl.program_id(1)
    for h in range(2):
        for s in range(4):

            @pl.when((half == h) & (slot == s))
            def _(piece=pieces[h * 3 + min(s, 2)], base=rows if s == 3 else 0):
                for (lo, hi), out in zip(spans, outs):
                    out[...] = piece[base : base + tall, lo:hi].astype(F32)
                short = outs[-1].shape[0]
                for c in range(outs[-1].shape[1] // columns):
                    start = base + tall + c * short
                    outs[-1][:, c * columns : (c + 1) * columns] = piece[
                        start : start + short, :
                    ].astype(F32)


def assemble(pieces_a, pieces_b, ids_a, ids_b, core, widths, tall, wide):
    rows, columns = pieces_a[0].shape
    spans, at = [], 0
    for width in widths:
        spans.append((at, at + width))
        at += width
    short = (rows - tall) * columns // wide
    table = jnp.stack([*ids_a, *ids_b, core, 1 - core]).astype(jnp.int32)
    return pl.pallas_call(
        functools.partial(assemble_kernel, tall, spans),
        out_shape=[jax.ShapeDtypeStruct((tall * 4, width * 2), F32) for width in widths]
        + [jax.ShapeDtypeStruct((short * 8, wide), F32)],
        grid_spec=pltpu.PrefetchScalarGridSpec(
            num_scalar_prefetch=1,
            grid=(2, 4),
            in_specs=[pl.BlockSpec(p.shape, lambda h, s, t: (0, 0)) for p in (*pieces_a, *pieces_b)],
            out_specs=[
                pl.BlockSpec((tall, width), lambda h, s, t: (t[h * 4 + s], t[8 + h]))
                for width in widths
            ]
            + [pl.BlockSpec((short, wide), lambda h, s, t: (t[8 + h] * 4 + t[h * 4 + s], 0))],
        ),
        compiler_params=pltpu.CompilerParams(vmem_limit_bytes=16 << 20),
        cost_estimate=NO_COST,
    )(table, *pieces_a, *pieces_b)


def assemble_ff_kernel(table_ref, *refs):
    pieces, (gate, up, down) = refs[:6], refs[6:]
    rows, columns = pieces[0].shape
    tall, ff = gate.shape
    half, slot = pl.program_id(0), pl.program_id(1)
    for h in range(2):
        for s in range(4):

            @pl.when((half == h) & (slot == s))
            def _(piece=pieces[h * 3 + min(s, 2)], base=rows if s == 3 else 0):
                for chunk in range(2 * ff // 256):
                    out, at = (gate, chunk * 256) if chunk * 256 < ff else (up, chunk * 256 - ff)
                    block, col = divmod(chunk * 256, columns)
                    start = base + block * tall
                    out[:, at : at + 256] = piece[start : start + tall, col : col + 256].astype(F32)
                start, short = base + 2 * ff // columns * tall, ff * down.shape[1] // columns
                for c in range(2):
                    down[c * short : (c + 1) * short, :] = piece[
                        start : start + short, c * down.shape[1] : (c + 1) * down.shape[1]
                    ].astype(F32)


def assemble_ff(pieces_a, pieces_b, ids_a, ids_b, core, width, ff):
    table = jnp.stack([*ids_a, *ids_b, core, 1 - core]).astype(jnp.int32)
    quarter = width // 4
    return pl.pallas_call(
        assemble_ff_kernel,
        out_shape=[jax.ShapeDtypeStruct((width, 2 * ff), F32)] * 2
        + [jax.ShapeDtypeStruct((2 * ff, width), F32)],
        grid_spec=pltpu.PrefetchScalarGridSpec(
            num_scalar_prefetch=1,
            grid=(2, 4),
            in_specs=[pl.BlockSpec(p.shape, lambda h, s, t: (0, 0)) for p in (*pieces_a, *pieces_b)],
            out_specs=[pl.BlockSpec((quarter, ff), lambda h, s, t: (t[h * 4 + s], t[8 + h]))] * 2
            + [pl.BlockSpec((ff, quarter), lambda h, s, t: (t[8 + h], t[h * 4 + s]))],
        ),
        compiler_params=pltpu.CompilerParams(vmem_limit_bytes=32 << 20),
        cost_estimate=NO_COST,
    )(table, *pieces_a, *pieces_b)


def cat(items, axis):
    return jnp.concatenate(items, axis)


def rope_tables():
    half = HEAD_SIZE // 2
    freq = THETA ** (-(jnp.arange(half, dtype=F32) * 2.0) / HEAD_SIZE)
    angle = jnp.arange(SEQUENCE_LENGTH, dtype=F32)[:, None] * freq[None, :]
    cosine = jnp.cos(angle)
    sine = jnp.sin(angle)
    return (jnp.concatenate([cosine, cosine], 1), jnp.concatenate([-sine, sine], 1))


def dot(a, b, dims):
    return lax.dot_general(a, b, (dims, ((), ())), preferred_element_type=F32)


NN = ((1,), (0,))
NT = ((1,), (1,))
TN = ((0,), (0,))


def unit_rows(x):
    factor = lax.rsqrt(jnp.mean(x * x, axis=1, keepdims=True) + EPS)
    return x * factor, factor


def raw_scores(query, key, block):
    scores = dot(query, key, NT)
    row = lax.broadcasted_iota(jnp.int32, scores.shape, 0) + block * BLOCK
    column = lax.broadcasted_iota(jnp.int32, scores.shape, 1)
    return jnp.where(row >= column, scores, -1e30)


def attend_kernel(groups, table, *refs):
    raws = refs[:ROWS]
    cosine, sine, q_gain, k_gain = refs[ROWS : ROWS + 4]
    att, lse, query, key, value = refs[ROWS + 4 :]
    width = HEAD_SIZE
    for s in range(ROWS):
        rows = pl.ds(pl.multiple_of(table[s] * BLOCK, BLOCK), BLOCK)
        cos, sin = cosine[rows, :], sine[rows, :]
        for h in range(groups + 1):
            unit, _ = unit_rows(raws[s][:, h * width : (h + 1) * width])
            gained = unit * (q_gain[...] if h < groups else k_gain[...])
            turned = gained * cos + pltpu.roll(gained, width // 2, 1) * sin
            if h < groups:
                query[rows, h * width : (h + 1) * width] = turned.astype(BF16)
            else:
                key[rows, :] = turned.astype(BF16)
        value[rows, :] = raws[s][:, (groups + 1) * width :].astype(BF16)
    for i in range(ROWS):
        span = (i + 1) * BLOCK
        slot = table[ROWS + i]
        rows = pl.ds(pl.multiple_of(slot * BLOCK, BLOCK), BLOCK)
        for h in range(groups):
            cols = slice(h * width, (h + 1) * width)
            scores = raw_scores(query[i * BLOCK : span, cols], key[:span, :], i)
            top = jnp.max(scores, axis=1, keepdims=True)
            expo = jnp.exp2((scores - top) * LOG2)
            total = jnp.sum(expo, axis=1, keepdims=True)
            prob = (expo * (1.0 / total)).astype(BF16)
            att[rows, cols] = dot(prob, value[:span, :], NN).astype(BF16)
            log = top * LOG2 + jnp.log2(total)
            lse[i * BLOCK : span, cols] = jnp.broadcast_to(log, (BLOCK, width))


def attend_back_kernel(groups, table, *refs):
    raws = refs[:ROWS]
    grads, others = refs[ROWS : 2 * ROWS], refs[2 * ROWS : 3 * ROWS]
    cosine, sine, q_gain, k_gain, query, key, value, lse = refs[3 * ROWS : 3 * ROWS + 8]
    out, gains, d_query, d_key, d_value, grad = refs[3 * ROWS + 8 :]
    width = HEAD_SIZE
    for s in range(ROWS):
        rows = pl.ds(pl.multiple_of(table[s] * BLOCK, BLOCK), BLOCK)
        grad[rows, :] = (grads[s][...] + others[s][...].astype(F32)).astype(BF16)
    d_key[...] = jnp.zeros_like(d_key)
    d_value[...] = jnp.zeros_like(d_value)
    for i in range(ROWS):
        span = (i + 1) * BLOCK
        for h in range(groups):
            cols = slice(h * width, (h + 1) * width)
            q = query[i * BLOCK : span, cols]
            g = grad[i * BLOCK : span, cols]
            scores = raw_scores(q, key[:span, :], i)
            log = lse[i * BLOCK : span, h * width : h * width + 1]
            prob = jnp.exp2(scores * LOG2 - log)
            dprob = dot(g, value[:span, :], NT)
            delta = jnp.sum(prob * dprob, axis=1, keepdims=True)
            dscore = (SCALE * prob * (dprob - delta)).astype(BF16)
            d_query[i * BLOCK : span, cols] = dot(dscore, key[:span, :], NN)
            d_key[:span, :] += dot(dscore, q, TN)
            d_value[:span, :] += dot(prob.astype(BF16), g, TN)
    gain_sums = [jnp.zeros((1, width), F32), jnp.zeros((1, width), F32)]
    for s in range(ROWS):
        rows = pl.ds(pl.multiple_of(table[s] * BLOCK, BLOCK), BLOCK)
        cos, sin = cosine[rows, :], sine[rows, :]
        for h in range(groups + 1):
            cols = slice(h * width, (h + 1) * width)
            unit, factor = unit_rows(raws[s][:, cols])
            turned = d_query[rows, cols] if h < groups else d_key[rows, :]
            back = turned * cos + pltpu.roll(turned * sin, width // 2, 1)
            scaled = back * (q_gain[...] if h < groups else k_gain[...])
            inner = jnp.mean(scaled * unit, axis=1, keepdims=True)
            which = 0 if h < groups else 1
            gain_sums[which] += jnp.sum(back * unit, axis=0, keepdims=True)
            out[s * BLOCK : (s + 1) * BLOCK, cols] = (factor * (scaled - unit * inner)).astype(BF16)
        out[s * BLOCK : (s + 1) * BLOCK, (groups + 1) * width :] = d_value[rows, :].astype(BF16)
    gains[0:1, :] = gain_sums[0]
    gains[1:2, :] = gain_sums[1]


def attend(table, raws, cosine, sine, q_gain, k_gain, groups):
    wide = (SEQUENCE_LENGTH, groups * HEAD_SIZE)
    one = (SEQUENCE_LENGTH, HEAD_SIZE)
    return pl.pallas_call(
        functools.partial(attend_kernel, groups),
        out_shape=[
            jax.ShapeDtypeStruct(wide, BF16),
            jax.ShapeDtypeStruct(wide, F32),
            jax.ShapeDtypeStruct(wide, BF16),
            jax.ShapeDtypeStruct(one, BF16),
            jax.ShapeDtypeStruct(one, BF16),
        ],
        in_specs=[SMEM] + [VMEM] * (ROWS + 4),
        out_specs=[VMEM] * 5,
        compiler_params=pltpu.CompilerParams(vmem_limit_bytes=16 << 20),
        cost_estimate=NO_COST,
    )(table, *raws, cosine, sine, q_gain[None], k_gain[None])


def attend_back(table, raws, grads, others, cosine, sine, q_gain, k_gain, saved, groups):
    query, key, value, lse = saved
    return pl.pallas_call(
        functools.partial(attend_back_kernel, groups),
        out_shape=[
            jax.ShapeDtypeStruct((SEQUENCE_LENGTH, (groups + 2) * HEAD_SIZE), BF16),
            jax.ShapeDtypeStruct((2, HEAD_SIZE), F32),
        ],
        in_specs=[SMEM] + [VMEM] * (3 * ROWS + 8),
        out_specs=[VMEM] * 2,
        scratch_shapes=[
            pltpu.VMEM((SEQUENCE_LENGTH, groups * HEAD_SIZE), F32),
            pltpu.VMEM((SEQUENCE_LENGTH, HEAD_SIZE), F32),
            pltpu.VMEM((SEQUENCE_LENGTH, HEAD_SIZE), F32),
            pltpu.VMEM((SEQUENCE_LENGTH, groups * HEAD_SIZE), BF16),
        ],
        compiler_params=pltpu.CompilerParams(vmem_limit_bytes=20 << 20),
        cost_estimate=NO_COST,
    )(table, *raws, *grads, *others, cosine, sine, q_gain[None], k_gain[None], query, key, value, lse)


def product(kernel, t, ins, outs, wait=()):
    return pl.pallas_call(
        kernel,
        out_shape=[jax.ShapeDtypeStruct(shape, kind) for shape, kind in outs],
        in_specs=[SMEM] + [VMEM] * len(ins) + [pl.BlockSpec(memory_space=pl.ANY)] * len(wait),
        out_specs=[VMEM] * len(outs),
        compiler_params=pltpu.CompilerParams(vmem_limit_bytes=16 << 20),
        cost_estimate=NO_COST,
    )(t, *ins, *wait)


def hold_kernel(t, x, *refs):
    refs[-1][...] = x[...]


def hold(x, other, t):
    return product(hold_kernel, t, (x,), [(x.shape, x.dtype)], (other,))[0]


def part(t, other, size, start=0, width=None):
    return pl.ds(pl.multiple_of(t[2 * ROWS + other] * size + start, 128), width or size)


def block_rows(t, s):
    return pl.ds(pl.multiple_of(t[s] * BLOCK, BLOCK), BLOCK)


def head_rows_kernel(t, own, other, q, k, v, x, out):
    at = 0
    for weight in (q, k, v):
        width = weight.shape[1] // 2
        cols = slice(at, at + width)
        out[:, cols] = dot(own[...], weight[:, part(t, 0, width)], NN) + dot(
            other[...], x[:, cols], NN
        )
        at += width


def head_rows(own, other, weights, x, t):
    return product(
        head_rows_kernel, t, (own, other, *weights, x), [((own.shape[0], x.shape[1]), F32)]
    )[0]


def out_rows_kernel(s, t, own, other, weight, *refs):
    out = refs[-1]
    rows = slice(s * BLOCK, (s + 1) * BLOCK)
    half = weight.shape[0] // 2
    total = dot(own[rows, :], weight[part(t, 0, half), :], NN)
    total += dot(other[rows, :], weight[part(t, 1, half), :], NN)
    out[...] = total.astype(out.dtype)


def out_rows(own, other, weight, s, kind, t, wait=()):
    return product(
        functools.partial(out_rows_kernel, s), t, (own, other, weight),
        [((BLOCK, weight.shape[1]), kind)], wait,
    )[0]


def g_mixed_kernel(t, own, other, weight, x, out):
    half = x.shape[0]
    out[...] = dot(own[...], weight[part(t, 0, half), :], NT) + dot(other[...], x[...], NT)


def g_mixed_rows(own, other, weight, x, t):
    return product(
        g_mixed_kernel, t, (own, other, weight, x), [((own.shape[0], x.shape[0]), F32)]
    )[0]


FF_BLOCK = 256


def mlp_kernel(t, own, other, gate_weight, up_weight, gate_x, up_x, g_mixed, out):
    ff = gate_x.shape[1]
    for start in range(0, ff, FF_BLOCK):
        cols = slice(start, start + FF_BLOCK)
        mine = part(t, 0, ff, start, FF_BLOCK)
        gate = dot(own[...], gate_weight[:, mine], NN) + dot(other[...], gate_x[:, cols], NN)
        upper = dot(own[...], up_weight[:, mine], NN) + dot(other[...], up_x[:, cols], NN)
        sigma = 1.0 / (1.0 + jnp.exp(-gate))
        activ = gate * sigma
        grad = g_mixed[:, cols]
        out[0, :, cols] = (activ * upper).astype(BF16)
        out[1, :, cols] = (grad * upper * sigma * (1.0 + gate * (1.0 - sigma))).astype(BF16)
        out[2, :, cols] = (grad * activ).astype(BF16)


def mlp(own, other, gate_weight, up_weight, gate_x, up_x, g_mixed, t):
    return product(
        mlp_kernel, t,
        (own, other, gate_weight, up_weight, gate_x, up_x, g_mixed),
        [((3, own.shape[0], gate_x.shape[1]), BF16)],
    )[0]


def mlp_back_kernel(t, own, other, gate_weight, up_weight, out):
    ff = own.shape[2]
    mine, theirs = part(t, 0, ff), part(t, 1, ff)
    for start in range(0, out.shape[1], 256):
        rows = slice(start, start + 256)
        total = dot(own[1], gate_weight[rows, mine], NT) + dot(own[2], up_weight[rows, mine], NT)
        total += dot(other[1], gate_weight[rows, theirs], NT)
        total += dot(other[2], up_weight[rows, theirs], NT)
        out[:, rows] = total.astype(out.dtype)


def mlp_back(own, other, gate_weight, up_weight, kind, t):
    return product(
        mlp_back_kernel, t, (own, other, gate_weight, up_weight),
        [((own.shape[1], gate_weight.shape[0]), kind)],
    )[0]


def down_rows_kernel(t, weight, *refs):
    half = weight.shape[0] // 2
    for s in range(ROWS):
        out = refs[2 * ROWS + s]
        total = dot(refs[2 * s][0], weight[part(t, 0, half), :], NN)
        total += dot(refs[2 * s + 1][0], weight[part(t, 1, half), :], NN)
        out[...] = total.astype(out.dtype)


def down_rows(packs, weight, t):
    shape = (BLOCK, weight.shape[1])
    return product(
        down_rows_kernel, t, (weight, *[p for pair in packs for p in pair]),
        [(shape, kind) for kind in (F32, BF16, F32, BF16)],
    )


def g_heads_kernel(t, x, weight, own, sent):
    half = weight.shape[0] // 2
    own[...] = dot(x[...], weight[part(t, 0, half), :], NT)
    sent[...] = dot(x[...], weight[part(t, 1, half), :], NT).astype(BF16)


def g_heads(x, weight, t):
    shape = (x.shape[0], weight.shape[0] // 2)
    return product(g_heads_kernel, t, (x, weight), [(shape, F32), (shape, BF16)])


def head_back_kernel(s, t, own, other, q, k, v, out):
    rows = slice(s * BLOCK, (s + 1) * BLOCK)
    total = 0.0
    for which, grad in enumerate((own, other)):
        at = 0
        for weight in (q, k, v):
            width = weight.shape[1] // 2
            total += dot(grad[rows, at : at + width], weight[:, part(t, which, width)], NT)
            at += width
    out[...] = total.astype(out.dtype)


def head_back(own, other, weights, s, kind, t):
    return product(
        functools.partial(head_back_kernel, s), t, (own, other, *weights),
        [((BLOCK, weights[0].shape[0]), kind)],
    )[0]


GRAD_COLUMNS = 512


def ff_grads_kernel(which, stays, t, *refs):
    packs, n2, cot, out = refs[:ROWS], refs[ROWS : 2 * ROWS], refs[2 * ROWS : -1], refs[-1]
    ff = packs[0].shape[2]
    tall = cot[0].shape[1] // 4
    short = ff * tall // GRAD_COLUMNS
    kept = t[2 * ROWS + 2 + which]
    half = kept if stays else 1 - kept
    for j in range(2):
        base = j * out.shape[0] // 2
        cols = pl.ds(pl.multiple_of((half * 2 + j) * tall, 128), tall)
        for part_of in range(2):
            total = 0.0
            for s in range(ROWS):
                total += dot(n2[s][:, cols], packs[s][part_of + 1], TN)
            total = total.astype(BF16)
            for at in range(0, ff, 256):
                block, col = divmod(part_of * ff + at, GRAD_COLUMNS)
                start = base + block * tall
                out[start : start + tall, col : col + 256] = total[:, at : at + 256]
        total = 0.0
        for s in range(ROWS):
            total += dot(packs[s][0], cot[s][:, cols], TN)
        total = total.astype(BF16)
        start = base + 2 * ff // GRAD_COLUMNS * tall
        for c in range(2):
            out[start : start + short, c * tall : (c + 1) * tall] = total[
                c * short : (c + 1) * short, :
            ]


def ff_grads(which, stays, packs, n2, cot, t):
    rows = 3 * packs[0].shape[2] * cot[0].shape[1] // GRAD_COLUMNS // 2
    return product(
        functools.partial(ff_grads_kernel, which, stays), t, (*packs, *n2, *cot),
        [((rows, GRAD_COLUMNS), BF16)],
    )[0]


def last_grads_kernel(t, att, att_other, grad, grad_other, *refs):
    dmid, n1, outs = refs[:ROWS], refs[ROWS : 2 * ROWS], refs[2 * ROWS :]
    columns = grad.shape[1]
    tall, short = n1[0].shape[1] // 4, att.shape[1] // 4
    for which, (x, y) in enumerate(((grad, att), (grad_other, att_other))):
        kept = t[2 * ROWS + 2 + which]
        for out, half in zip(outs[2 * which : 2 * which + 2], (kept, 1 - kept)):
            heads = pl.ds(pl.multiple_of(half * 2 * short, 128), 2 * short)
            total = 0.0
            for s in range(ROWS):
                total += dot(y[s * BLOCK : (s + 1) * BLOCK, heads], dmid[s][...], TN)
            total = total.astype(BF16)
            at = 0
            for j in range(2):
                cols = pl.ds(pl.multiple_of(half * 2 * tall + j * tall, 128), tall)
                upper = 0.0
                for s in range(ROWS):
                    upper += dot(n1[s][:, cols], x[s * BLOCK : (s + 1) * BLOCK, :], TN)
                out[at : at + tall, :] = upper.astype(BF16)
                at += tall
                for c in range(total.shape[1] // columns):
                    out[at : at + short, :] = total[
                        j * short : (j + 1) * short, c * columns : (c + 1) * columns
                    ]
                    at += short


def last_grads(att, att_other, grad, grad_other, dmid, n1, t):
    columns = grad.shape[1]
    rows = n1[0].shape[1] // 2 + att.shape[1] // 2 * dmid[0].shape[1] // columns
    return product(
        last_grads_kernel, t, (att, att_other, grad, grad_other, *dmid, *n1),
        [((rows, columns), BF16)] * 4,
    )


def add_halves_kernel(which, t, kept, got, away, mine):
    size = away.shape[0]
    half = t[2 * ROWS + 3 - which]
    for out, v in ((away, 1 - half), (mine, half)):
        rows = pl.ds(pl.multiple_of(v * size, 128), size)
        out[...] = (kept[rows, :].astype(F32) + got[rows, :].astype(F32)).astype(BF16)


def add_halves(kept, got, which, t):
    shape = (kept.shape[0] // 2, kept.shape[1])
    return product(
        functools.partial(add_halves_kernel, which), t, (kept, got), [(shape, BF16)] * 2
    )


def add_kernel(t, x, y, out):
    out[...] = (x[...].astype(F32) + y[...].astype(F32)).astype(BF16)


def add(x, y, t):
    return product(add_kernel, t, (x, y), [(x.shape, BF16)])[0]


def join_kernel(t, x, y, out):
    rows = x.shape[0]
    out[:rows, :] = x[...]
    out[rows:, :] = y[...]


def join(x, y, t):
    return product(join_kernel, t, (x, y), [((2 * x.shape[0], x.shape[1]), BF16)])[0]


def norm_stats(x):
    part = jnp.sum(x * x, axis=1)
    factor = lax.rsqrt((part + swap(part)) / MODEL_WIDTH + EPS)
    return x * factor[:, None], factor


def norm_backward(grad, unit, factor, gain):
    scaled = grad * gain
    part = jnp.sum(scaled * unit, axis=1)
    inner = (part + swap(part)) / MODEL_WIDTH
    return (factor[:, None] * (scaled - unit * inner[:, None]), jnp.sum(grad * unit, axis=0))


def on_device(
    hidden,
    norm_before,
    query_weight,
    key_matrix,
    value_matrix,
    query_gain,
    key_gain,
    output_weight,
    norm_after,
    gate_weight,
    up_weight,
    down_weight,
    cotangent,
):
    dp = lax.axis_size("dp")
    k, core, me = lax.axis_index("row"), lax.axis_index("col"), lax.axis_index("dp")
    keeps = [me % 2, (me // 2) % 2] if dp == 4 else [0 * me, 0 * me]
    t = jnp.stack([k ^ i for i in range(ROWS)] * 2 + [core, 1 - core] + keeps).astype(jnp.int32)
    groups = query_weight.shape[1] // (2 * HEAD_SIZE)
    token = [hidden]

    def step(function, *args):
        flat, tree = jax.tree.flatten(args)
        flat = lax.optimization_barrier((*flat, token[0]))[:-1]
        out = function(*jax.tree.unflatten(tree, flat))
        token[0] = jax.tree.leaves(out)[0]
        return out

    def now(x):
        return after(x, token[0])

    def gather(x, work, between=lambda: None, later=lambda: None, late=False, then=lambda: None):
        two = row_swap(x, 2)
        first = swap(x)
        token[0] = x
        done = [work(0, x, first)]
        between()
        one = row_swap(now(x) if late else x, 1)
        then()
        two = now(two)
        three = row_swap(two, 1)
        second = swap(two)
        token[0] = two
        one = now(one)
        done.append(work(1, one, swap(one)))
        done.append(work(2, two, second))
        later()
        three = now(three)
        done.append(work(3, three, swap(three)))
        return [x, one, two, three], done

    turns = ((1, 2), (2, 1))

    def halving(sent, kept, which):
        first, second = turns[which]
        got = dp_swap(sent, first, dp)
        yield
        sent, mine = step(lambda *a: add_halves(*a[:2], which, a[2]), kept[which], got, t)
        got = dp_swap(sent, second, dp)
        yield
        mine = step(add, mine, got, t)
        near = dp_swap(mine, second, dp)
        yield
        return [mine, near, dp_swap(step(join, mine, near, t), first, dp)]

    if dp == 4:
        ids = [piece_rows(bits, me) for bits in turns]
    else:
        ids = [[0 * core + i for i in range(4)]] * 2

    class Sum:
        def __init__(self):
            self.runs, self.sent, self.kept, self.pieces = [], [], [], []

        def add(self, sent):
            self.sent.append(sent)
            if dp == 4:
                self.runs.append(halving(sent, self.kept, len(self.runs)))
                next(self.runs[-1])

        def step(self, chosen=slice(None)):
            for run in self.runs[chosen]:
                try:
                    next(run)
                except StopIteration as stop:
                    self.pieces.append(stop.value)

        def finish(self):
            if self.pieces:
                token[0] = after(*(piece[2] for piece in self.pieces))

        def result(self):
            if dp != 4:
                for kept, sent in lax.psum(tuple(zip(self.kept, self.sent)), "dp"):
                    size = kept.shape[0] // 2
                    self.pieces.append((kept[:size], kept[size:], sent))
            return (*self.pieces, *ids, core)

    def small_sum(x):
        for axis, size in (("row", ROWS), ("dp", dp)):
            for mask in (1, 2):
                if size == 4:
                    got = lax.ppermute(x, axis, [(i, i ^ mask) for i in range(size)])
                    yield
                    x = x + now(got)
                    token[0] = x
                else:
                    yield
            if size != 4:
                x = lax.psum(x, axis)
        return x

    def spread(parts):
        got_three = row_swap(parts[3], 1)
        yield
        got_three = now(got_three)
        sent = (parts[2] + got_three.astype(F32)).astype(BF16)
        token[0] = sent
        got_two = row_swap(sent, 2)
        got_one = row_swap(after(parts[1], got_three), 1)
        yield
        return parts[0] + now(got_one).astype(F32) + now(got_two).astype(F32)

    def scatter(term, between=lambda: None):
        part_three = term(3, BF16)
        got_three = row_swap(part_three, 1)
        part_one = term(1, BF16)
        part_two = term(2, F32)
        got_three = now(got_three)
        sent = (part_two + got_three.astype(F32)).astype(BF16)
        token[0] = sent
        got_two = row_swap(sent, 2)
        got_one = row_swap(after(part_one, got_three), 1)
        own = term(0, F32)
        between()
        got_one, got_two = now(got_one), now(got_two)
        return own + got_one.astype(F32) + got_two.astype(F32)

    resid = hidden.astype(F32)
    unit_one, factor_one = norm_stats(resid)
    sent_one = (unit_one * norm_before).astype(BF16)

    def for_other(weight, axis):
        half = weight.shape[axis] // 2
        return lax.dynamic_slice_in_dim(after(weight, sent_one), (1 - core) * half, half, axis)

    heads = (query_weight, key_matrix, value_matrix)
    qkv_x = swap(cat([for_other(w, 1) for w in heads], 1))
    gate_x, up_x = swap(for_other(gate_weight, 1)), swap(for_other(up_weight, 1))
    down_x = swap(for_other(down_weight, 0))
    cosine, sine = rope_tables()

    def settle(x):
        token[0] = after(x, token[0])

    cot = [cotangent]

    def start_cotangent():
        start = hold(cotangent, token[0], t)
        cot.append(row_swap(start, 1))
        cot.append(row_swap(start, 2))

    n1, raws = gather(
        sent_one, lambda s, own, other: step(head_rows, own, other, heads, qkv_x, t),
        lambda: settle(gate_x), start_cotangent,
    )
    settle(up_x)
    settle(down_x)
    att, lse, query, key, value = step(
        lambda *a: attend(*a, groups), t, raws, cosine, sine, query_gain, key_gain
    )
    att_oth = swap(att)
    middle = resid + scatter(
        lambda s, kind: step(
            lambda *a: out_rows(*a[:3], s, kind, *a[3:]),
            att, att_oth, output_weight, t, (cot[1], cot[2]) if s == 3 else (),
        )
    )

    cot.append(row_swap(hold(cot[2], middle, t), 1))
    cot_x = [swap(c) for c in cot]
    unit_two, factor_two = norm_stats(middle)
    sent_two = (unit_two * norm_after).astype(BF16)

    def hidden_units(s, own, other):
        g_mixed = step(g_mixed_rows, cot[s], cot_x[s], down_weight, down_x, t)
        packed = step(mlp, own, other, gate_weight, up_weight, gate_x, up_x, g_mixed, t)
        return packed, swap(packed)

    n2, packs = gather(sent_two, hidden_units)
    width = down_weight.shape[1]
    ff_sum, last_sum = Sum(), Sum()
    def ff_part(which, stays):
        return step(
            lambda *a: ff_grads(which, stays, *a), [p[which] for p in packs], n2, cot, t
        )

    for which in range(2):
        ff_sum.add(ff_part(which, False))

    def keep():
        ff_sum.kept += [ff_part(which, True) for which in range(2)]

    dsecond = scatter(
        lambda s, kind: step(
            lambda *a: mlp_back(*a[:4], kind, a[4]), *packs[s], gate_weight, up_weight, t
        ),
        keep,
    )
    token[0] = dsecond
    ff_sum.step(slice(0, 1))
    dmid_norm, after_part = norm_backward(dsecond, unit_two, factor_two, norm_after)
    dmiddle = cotangent.astype(F32) + dmid_norm

    swapped = []

    def g_attended(s, own, other):
        if swapped:
            token[0] = after(swapped[-1], token[0])
        mine, sent = step(g_heads, own, output_weight, t)
        swapped.append(swap(sent))
        return mine, swapped[-1]

    last = []

    def second_half():
        ff_sum.step(slice(1, 2))

    def feed_forward_rows():
        last.extend(step(down_rows, packs, down_weight, t))

    dmid, datt = gather(dmiddle.astype(BF16), g_attended, second_half, ff_sum.step, True, feed_forward_rows)

    dqkv, gain_parts = step(
        lambda *a: attend_back(*a, groups),
        t, raws, [d for d, _ in datt], [d for _, d in datt],
        cosine, sine, query_gain, key_gain, (query, key, value, lse),
    )
    dqkv_oth = swap(dqkv)
    ff_sum.step()
    parts = step(last_grads, att, att_oth, dqkv, dqkv_oth, dmid, n1, t)
    last_sum.kept += parts[::2]
    last_sum.add(parts[1])
    last_sum.add(parts[3])
    dfirst = scatter(
        lambda s, kind: step(
            lambda *a: head_back(*a[:2], a[2:5], s, kind, a[5]), dqkv, dqkv_oth, *heads, t
        )
    )
    token[0] = dfirst
    last_run = spread(last)
    next(last_run)
    dres_norm, before_part = norm_backward(now(dfirst), unit_one, factor_one, norm_before)
    hidden_grad = dmiddle + dres_norm
    small_run = small_sum(cat([after_part, before_part, gain_parts.reshape(-1)], 0))
    next(small_run)
    ff_sum.finish()
    gate_grad, up_grad, down_grad = step(
        lambda *a: assemble_ff(*a, width, gate_x.shape[1]), *ff_sum.result()
    )
    next(small_run)
    last_sum.step()
    next(small_run)
    next(last_run)
    last_sum.step()
    next(small_run)
    last_sum.step()
    small = finish(small_run)
    after_grad, before_grad = small[:width], small[width : 2 * width]
    gains = small[2 * width :] + swap(small[2 * width :])
    layer_out = (middle + finish(last_run)).astype(BF16)
    query_grad, key_grad, value_grad, output_grad = assemble(
        *last_sum.result(), tuple(w.shape[1] // 2 for w in heads), width // 4, width
    )
    return (
        layer_out,
        hidden_grad,
        before_grad,
        query_grad,
        key_grad,
        value_grad,
        gains[:HEAD_SIZE],
        gains[HEAD_SIZE:],
        output_grad,
        after_grad,
        gate_grad,
        up_grad,
        down_grad,
    )


def solution(mesh):
    placed = (
        P(("dp", "row"), "col"),
        P("col"),
        P("col", "row"),
        P("col", "row"),
        P("col", "row"),
        P(),
        P(),
        P("row", "col"),
        P("col"),
        P("col", "row"),
        P("col", "row"),
        P("row", "col"),
        P(("dp", "row"), "col"),
    )
    return jax.shard_map(
        on_device,
        mesh=mesh,
        in_specs=placed,
        out_specs=(
            P(("dp", "row"), "col"),
            P(("dp", "row"), "col"),
            P("col"),
            P("col", "row"),
            P("col", "row"),
            P("col", "row"),
            P(),
            P(),
            P("row", "col"),
            P("col"),
            P("col", "row"),
            P("col", "row"),
            P("row", "col"),
        ),
        check_vma=False,
    )
```
